512 devices in a mesh: seq: 128 (over z, y, core), mp: 4 (over x).
Axes of the slice: x: 4, y: 4, z: 16, core: 2. Of those that a mesh axis runs over, the one named last changes fastest.
Arguments:
- queries: bfloat16 [8192, 2048], P('seq', 'mp'), may hold values from -14 to 14
- keys: bfloat16 [8192, 2048], P('seq', 'mp'), may hold values from -14 to 14
- values: bfloat16 [8192, 2048], P('seq', 'mp'), may hold values from -6 to 6
- stream: bfloat16 [8192, 2048], P('seq', 'mp'), may hold values from -6 to 6
- seg_lengths: int32 [64], replicated, may hold values from 1 to 256, 8192 in all
- gain: float32 [2048], replicated, may hold values from 0.5 to 1.5
- w_out: bfloat16 [2048, 2048], P('mp', 'seq'), may hold values from -0.125 to 0.125
- w_gate: bfloat16 [2048, 3072], P('seq', 'mp'), may hold values from -0.125 to 0.125
- w_up: bfloat16 [2048, 3072], P('seq', 'mp'), may hold values from -0.125 to 0.125
- w_down: bfloat16 [3072, 2048], P('mp', 'seq'), may hold values from -0.109375 to 0.109375
Outputs:
- mixed: bfloat16 [8192, 2048], P('seq', 'mp')
The draws below stay inside these ranges and needn't reach their ends.
Inputs may be any that keep to these rules, and one draw needn't show every extreme that they name: `seg_lengths`: the segments of landmarks 0 to 63 follow one another and cover the document's 8192 tokens.
All inputs are finite; a program needn't handle non-finite values.
Results may differ from the reference program's by a relative error of at most 0.014.
Values may be sent and summed in bfloat16 or wider, within the bound.
No kernel may reach another device: no remote copies, remote signals or barrier semaphores. Data moves between devices by JAX's collectives and lax.ppermute only.
A program may use at most 64 MiB of HBM per device.

```python
import math
import jax
import jax.numpy as jnp
import numpy as np
from jax import lax

D = 2048
HEADS = 16
FF = 3072
LANDMARKS = 64
PINV_ITERS = 6
HEAD = 128
TOKENS = 8192
N_MP = 4


def shared_signal(key):
    freqs = jax.random.randint(jax.random.fold_in(key, 11), (D,), 1, 33).astype(jnp.float32)
    phases = jax.random.uniform(jax.random.fold_in(key, 12), (D,), jnp.float32, -math.pi, math.pi)
    place = jnp.arange(TOKENS, dtype=jnp.float32) / TOKENS
    return 1.5 * jnp.sin(2.0 * math.pi * place[:, None] * freqs[None, :] + phases[None, :])


def draw_queries(key, part):
    noise = jnp.clip(jax.random.normal(jax.random.fold_in(key, 1), (TOKENS, D), jnp.float32), -4.0, 4.0)
    result = noise + shared_signal(key)
    return result.astype(jnp.bfloat16)


def draw_keys(key, part):
    noise = jnp.clip(jax.random.normal(jax.random.fold_in(key, 2), (TOKENS, D), jnp.float32), -4.0, 4.0)
    result = noise + shared_signal(key)
    return result.astype(jnp.bfloat16)


def steps_of(own_key, dims, cuts, least, largest):
    def one(position, shards_of):
        draws = jax.random.uniform(jax.random.fold_in(jax.random.fold_in(own_key, 6), position), (shards_of,), jnp.float32, least / len(cuts), largest / len(cuts))
        return jnp.repeat(jnp.exp(draws), dims[position] // shards_of).reshape((-1,) + (1,) * (len(dims) - position - 1))

    level = one(*cuts[0])
    for cut in cuts[1:]:
        level = level * one(*cut)
    return level


def profile(count, total, limit, slope):
    portions = [(1 << 20) // math.isqrt(grade ** slope) + 1 for grade in range(2, count + 1)]
    surplus, holding = total - limit - (count - 1), [1] * (count - 1)
    while surplus > 0:
        free = [i for i in range(count - 1) if holding[i] < limit]
        whole, left = sum([portions[i] for i in free]), surplus
        for i in free:
            more = min(limit - holding[i], max(1, left * portions[i] // whole), surplus)
            holding[i] = holding[i] + more
            surplus = surplus - more
    return np.array([limit] + holding)


def ragged(key, count, total, limit, skew):
    if count == 2:
        one = jax.random.randint(key, (), max(1, total - limit), min(limit, total - 1) + 1)
        return jnp.stack([one, total - one])
    tallies = jnp.asarray(profile(count, total, limit, skew), jnp.int32)
    twos = (count - 1) // 2
    donor, taker = tallies[1:1 + 2 * twos:2], tallies[2:2 + 2 * twos:2]
    slack = jnp.minimum(donor - 1, limit - taker)
    shifted = jax.random.randint(jax.random.fold_in(key, 1), (twos,), 0, 1 << 20) % (slack + 1)
    tallies = tallies.at[1:1 + 2 * twos:2].set(donor - shifted).at[2:2 + 2 * twos:2].set(taker + shifted)
    return tallies[jax.random.permutation(jax.random.fold_in(key, 2), count)]


def bell_draw(rng, shape, width, bound, shards=(), held_as=jnp.bfloat16):
    entries = jax.random.normal(rng, shape, jnp.float32) * width
    if len(shards) > 0:
        entries = steps_of(rng, shape, shards, -0.22, 0.18) * entries
    return jnp.clip(entries, min=-bound, max=bound).astype(held_as)


def setup_inputs(seed: int = 0) -> dict:
    splits = jax.random.split(jax.random.key(seed), 11)
    return {
        "queries": draw_queries(jax.random.fold_in(splits[10], 71), 0),
        "keys": draw_keys(jax.random.fold_in(splits[10], 71), 0),
        "values": bell_draw(splits[2], (TOKENS, D), 1.0, 6.0, ((0, 128), (1, 4))),
        "stream": bell_draw(splits[3], (TOKENS, D), 1.0, 6.0, ((0, 128), (1, 4))),
        "seg_lengths": ragged(splits[4], LANDMARKS, TOKENS, 2 * TOKENS // LANDMARKS, 1).astype(jnp.int32),
        "gain": jnp.clip(1.0 + 0.1 * jax.random.normal(splits[5], (D,), jnp.float32), 0.5, 1.5),
        "w_out": bell_draw(splits[6], (D, D), D ** -0.5, 0.125, ((0, 4), (1, 128))),
        "w_gate": bell_draw(splits[7], (D, FF), D ** -0.5, 0.125, ((0, 128), (1, 4))),
        "w_up": bell_draw(splits[8], (D, FF), D ** -0.5, 0.125, ((0, 128), (1, 4))),
        "w_down": bell_draw(splits[9], (FF, D), FF ** -0.5, 0.109375, ((0, 4), (1, 128))),
    }


HIGH_ACCURACY = lax.Precision.HIGHEST
EPS = 1e-05

def inverse_rounds(anchor_block):
    eye = jnp.eye(anchor_block.shape[0], dtype=jnp.float32)
    col_most = jnp.max(lax.optimization_barrier(jnp.sum(anchor_block, axis=0)))
    row_most = jnp.max(lax.optimization_barrier(jnp.sum(anchor_block, axis=1)))
    approx = anchor_block.T / (col_most * row_most)
    for step in range(PINV_ITERS):
        prod = jnp.dot(anchor_block, approx, precision=HIGH_ACCURACY)
        inner = 7.0 * eye - prod
        inner = 15.0 * eye - jnp.dot(prod, inner, precision=HIGH_ACCURACY)
        inner = 13.0 * eye - jnp.dot(prod, inner, precision=HIGH_ACCURACY)
        approx = 0.25 * jnp.dot(approx, inner, precision=HIGH_ACCURACY)
    return approx

def reference(queries, keys, values, stream, seg_lengths, gain, w_out, w_gate, w_up, w_down):
    ends = jnp.cumsum(seg_lengths).astype(jnp.int32)
    starts = ends - seg_lengths
    place = jnp.arange(TOKENS, dtype=jnp.int32)
    member = ((place[:, None] >= starts[None, :]) & (place[:, None] < ends[None, :])).astype(jnp.bfloat16)
    counts = seg_lengths.astype(jnp.float32)
    query_anchors = jnp.dot(member.T, queries, preferred_element_type=jnp.float32) / counts[:, None]
    key_anchors = jnp.dot(member.T, keys, preferred_element_type=jnp.float32) / counts[:, None]
    score_scale = 1.0 / math.sqrt(HEAD)

    def one_head(head):
        low = (head * HEAD).astype(jnp.int32)
        qhead = lax.dynamic_slice_in_dim(queries, low, HEAD, 1).astype(jnp.float32)
        khead = lax.dynamic_slice_in_dim(keys, low, HEAD, 1).astype(jnp.float32)
        vhead = lax.dynamic_slice_in_dim(values, low, HEAD, 1).astype(jnp.float32)
        qmark = lax.dynamic_slice_in_dim(query_anchors, low, HEAD, 1)
        kmark = lax.dynamic_slice_in_dim(key_anchors, low, HEAD, 1)
        nearby_scores = jax.nn.softmax(jnp.dot(qhead, kmark.T, precision=HIGH_ACCURACY) * score_scale, axis=-1)
        anchor_block = jax.nn.softmax(jnp.dot(qmark, kmark.T, precision=HIGH_ACCURACY) * score_scale, axis=-1)
        distant_scores = jnp.dot(qmark, khead.T, precision=HIGH_ACCURACY) * score_scale
        peak = lax.optimization_barrier(jnp.max(distant_scores, axis=-1, keepdims=True))
        layer_weights = jnp.exp(distant_scores - peak)
        mass = lax.optimization_barrier(jnp.sum(layer_weights, axis=-1, keepdims=True))
        collected_rows = jnp.dot(layer_weights, vhead, precision=HIGH_ACCURACY) / mass
        token_mixer = jnp.dot(inverse_rounds(anchor_block), collected_rows, precision=HIGH_ACCURACY)
        return jnp.dot(nearby_scores, token_mixer, precision=HIGH_ACCURACY)
    heads_out = lax.map(one_head, jnp.arange(HEADS, dtype=jnp.int32))
    attn = jnp.transpose(heads_out, (1, 0, 2)).reshape(TOKENS, D).astype(jnp.bfloat16)
    group = D // N_MP
    proj = jnp.zeros((TOKENS, D), jnp.float32)
    for index in range(N_MP):
        part = jnp.dot(attn[:, index * group:(index + 1) * group], w_out[index * group:(index + 1) * group], preferred_element_type=jnp.float32)
        proj = proj + lax.optimization_barrier(part.astype(jnp.bfloat16)).astype(jnp.float32)
    resid = (stream.astype(jnp.float32) + proj).astype(jnp.bfloat16)
    resid32 = resid.astype(jnp.float32)
    meansq = lax.optimization_barrier(jnp.mean(resid32 * resid32, axis=-1, keepdims=True))
    normed = (resid32 * lax.rsqrt(meansq + EPS) * gain[None, :]).astype(jnp.bfloat16)
    share = FF // N_MP
    ffn = jnp.zeros((TOKENS, D), jnp.float32)
    for index in range(N_MP):
        gate = jnp.dot(normed, w_gate[:, index * share:(index + 1) * share], preferred_element_type=jnp.float32)
        upper = jnp.dot(normed, w_up[:, index * share:(index + 1) * share], preferred_element_type=jnp.float32)
        hidden = (jax.nn.silu(gate) * upper).astype(jnp.bfloat16)
        part = jnp.dot(hidden, w_down[index * share:(index + 1) * share], preferred_element_type=jnp.float32)
        ffn = ffn + lax.optimization_barrier(part.astype(jnp.bfloat16)).astype(jnp.float32)
    return (resid32 + ffn).astype(jnp.bfloat16)
```

```python
import math

import jax
import jax.numpy as jnp
from jax import lax
from jax.sharding import Mesh
from jax.sharding import PartitionSpec as P

PINV_ITERS = 6
HEAD = 128
EPS = 1e-05
HI = lax.Precision.HIGHEST
F32 = jnp.float32
BF16 = jnp.bfloat16


def mm(spec, a, b):
    return jnp.einsum(spec, a, b, precision=HI, preferred_element_type=F32)


def inverse_rounds(land):
    eye = jnp.eye(land.shape[-1], dtype=F32)
    col_most = jnp.max(jnp.sum(land, axis=0))
    row_most = jnp.max(jnp.sum(land, axis=1))
    approx = land.T / (col_most * row_most)
    for _ in range(PINV_ITERS):
        prod = mm("ij,jk->ik", land, approx)
        inner = 7.0 * eye - prod
        inner = 15.0 * eye - mm("ij,jk->ik", prod, inner)
        inner = 13.0 * eye - mm("ij,jk->ik", prod, inner)
        approx = 0.25 * mm("ij,jk->ik", approx, inner)
    return approx


def tiles(a):
    return a[:, :512].reshape(a.shape[0], 4, 128).transpose(1, 0, 2)


def halves(a):
    return a[:, 512:].reshape(a.shape[0], 4, 64).transpose(1, 0, 2)


def on_device(queries, keys, values, stream, seg_lengths, gain, w_out, w_gate, w_up, w_down):
    scale = 1.0 / math.sqrt(HEAD)
    z, c = lax.axis_index("z"), lax.axis_index("c")
    down_t, out_t = w_down.T, w_out.T
    mixed_half = jnp.concatenate([halves(w_gate), halves(w_up)], axis=-1)
    down_half = jnp.pad(halves(down_t), ((0, 0), (0, 0), (0, 64)))
    pack = jnp.concatenate(
        [
            tiles(queries),
            tiles(keys),
            tiles(values),
            tiles(w_gate),
            tiles(w_up),
            mixed_half,
            tiles(down_t),
            down_half,
            tiles(out_t),
        ],
        axis=1,
    )
    got = lax.all_to_all(pack, "y", 0, 0)
    q = got[:, 0:64].reshape(256, HEAD)
    k = got[:, 64:128].reshape(256, HEAD)
    v = got[:, 128:192].reshape(256, HEAD)
    weights = lax.all_gather(got[:, 192:], ("z", "c"), axis=0)
    weights = (
        weights.reshape(16, 2, 4, 6, 16, 128).transpose(3, 0, 2, 1, 4, 5).reshape(6, 2048, 128)
    )

    ends = jnp.cumsum(seg_lengths)
    starts = ends - seg_lengths
    block = jnp.arange(4, dtype=jnp.int32)[:, None] * 2 + z * 8 + c
    place = (block * 64 + jnp.arange(64, dtype=jnp.int32)[None, :]).reshape(256)
    member = ((place[:, None] >= starts[None, :]) & (place[:, None] < ends[None, :])).astype(BF16)
    sums = jnp.stack(
        [
            jnp.dot(member.T, q, preferred_element_type=F32),
            jnp.dot(member.T, k, preferred_element_type=F32),
        ]
    )
    mine = jnp.sum(lax.all_to_all(sums, "c", 0, 0), axis=0)
    mine = jnp.sum(lax.all_gather(mine, "z", axis=0), axis=0)
    marks = lax.all_gather(mine / seg_lengths.astype(F32)[:, None], "c", axis=0)
    qm, km = marks[0], marks[1]

    q32, k32, v32 = q.astype(F32), k.astype(F32), v.astype(F32)
    far = mm("jd,td->jt", qm, k32) * scale
    peak = jnp.max(far, axis=-1, keepdims=True)
    far = jnp.exp(far - peak)
    mass = jnp.sum(far, axis=-1, keepdims=True)
    part = mm("jt,td->jd", far, v32)
    stats = jnp.concatenate([peak.reshape(32, 1, 2), mass.reshape(32, 1, 2)], axis=-1)
    send = jnp.concatenate(
        [part.reshape(32, 2, HEAD), jnp.pad(stats, ((0, 0), (0, 0), (0, 124)))], axis=1
    )
    parts = lax.all_to_all(send, ("z", "c"), 0, 0)
    peaks, masses = parts[:, 2, 0:2], parts[:, 2, 2:4]
    factor = jnp.exp(peaks - jnp.max(peaks, axis=0, keepdims=True))
    total = jnp.sum(factor * masses, axis=0)
    gathered = jnp.sum(factor[:, :, None] * parts[:, 0:2], axis=0) / total[:, None]
    gathered = lax.all_to_all(
        jnp.broadcast_to(gathered[None], (32, 2, HEAD)), ("z", "c"), 0, 0
    ).reshape(64, HEAD)

    near = jax.nn.softmax(mm("td,jd->tj", q32, km) * scale, axis=-1)
    land = jax.nn.softmax(mm("id,jd->ij", qm, km) * scale, axis=-1)
    mixer = mm("ij,jd->id", inverse_rounds(land), gathered)
    attn = mm("tj,jd->td", near, mixer).astype(BF16)

    def scatter(terms):
        terms = terms.astype(BF16).reshape(4, 64, 4, 512).transpose(0, 2, 1, 3).reshape(16, 64, 512)
        return jnp.sum(lax.all_to_all(terms, ("y", "x"), 0, 0).astype(F32), axis=0)

    proj = scatter(jnp.einsum("td,ed->te", attn, weights[5], preferred_element_type=F32))
    resid = (stream.astype(F32) + proj).astype(BF16)
    whole = lax.all_to_all(jnp.broadcast_to(resid[None], (16, 64, 512)), ("y", "x"), 0, 0)
    whole = whole.reshape(4, 4, 64, 512).transpose(0, 2, 1, 3).reshape(256, 2048).astype(F32)
    meansq = jnp.mean(whole * whole, axis=-1, keepdims=True)
    normed = (whole * lax.rsqrt(meansq + EPS) * gain[None, :]).astype(BF16)
    first = jnp.einsum("tk,jkl->jtl", normed, weights[0:3], preferred_element_type=F32)
    gate = jnp.concatenate([first[0], first[2][:, :64]], axis=-1)
    up = jnp.concatenate([first[1], first[2][:, 64:]], axis=-1)
    hidden = (jax.nn.silu(gate) * up).astype(BF16)
    down = jnp.concatenate([weights[3], weights[4][:, :64]], axis=-1)
    ffn = scatter(jnp.einsum("th,eh->te", hidden, down, preferred_element_type=F32))
    return (resid.astype(F32) + ffn).astype(BF16)


def solution(mesh):
    fine = Mesh(mesh.devices.reshape(16, 4, 2, 4), ("z", "y", "c", "x"))
    seq = ("z", "y", "c")
    return jax.shard_map(
        on_device,
        mesh=fine,
        in_specs=(
            P(seq, "x"),
            P(seq, "x"),
            P(seq, "x"),
            P(seq, "x"),
            P(),
            P(),
            P("x", seq),
            P(seq, "x"),
            P(seq, "x"),
            P("x", seq),
        ),
        out_specs=P(seq, "x"),
        check_vma=False,
    )
```

```python
import math

import jax
import jax.numpy as jnp
from jax import lax
from jax.experimental import pallas as pl
from jax.experimental.pallas import tpu as pltpu
from jax.sharding import Mesh
from jax.sharding import PartitionSpec as P

PINV_ITERS = 6
HEAD = 128
EPS = 1e-05
SCALE = 1.0 / math.sqrt(HEAD)
HI = lax.Precision.HIGHEST
F32 = jnp.float32
BF16 = jnp.bfloat16


def mm(spec, a, b):
    return jnp.einsum(spec, a, b, precision=HI, preferred_element_type=F32)


def dot(a, b, dims, precision=None):
    return lax.dot_general(
        a, b, (dims, ((), ())), precision=precision, preferred_element_type=F32
    )


def kernel_call(body, out_shape, n_in, scratch=(), cost=None):
    whole = pl.BlockSpec(memory_space=pltpu.VMEM)
    many = isinstance(out_shape, (list, tuple))
    return pl.pallas_call(
        body,
        out_shape=out_shape,
        in_specs=[whole] * n_in,
        out_specs=[whole] * len(out_shape) if many else whole,
        scratch_shapes=list(scratch),
        cost_estimate=cost,
    )


def shape(dims, dtype):
    return jax.ShapeDtypeStruct(dims, dtype)


def pack_body(q, k, v, wg, wu, wd, wo, out):
    for y in range(4):
        tile = slice(y * 128, y * 128 + 128)
        out[y, 0:64] = q[:, tile]
        out[y, 64:128] = k[:, tile]
        out[y, 128:192] = v[:, tile]
        out[y, 192:208] = wg[:, tile]
        out[y, 208:224] = wu[:, tile]
        last = slice(512 + (y // 2) * 128, 640 + (y // 2) * 128)
        lane = lax.broadcasted_iota(jnp.int32, (16, 128), 1)
        g, u, d = (w[:, last].astype(F32) for w in (wg, wu, wd))
        if y % 2 == 0:
            mixed = jnp.where(lane < 64, g, pltpu.roll(u, 64, 1))
        else:
            mixed = jnp.where(lane < 64, pltpu.roll(g, 64, 1), u)
            d = pltpu.roll(d, 64, 1)
        out[y, 224:240] = mixed.astype(BF16)
        out[y, 240:256] = wd[:, tile]
        out[y, 256:272] = jnp.where(lane < 64, d, 0.0).astype(BF16)
        out[y, 272:288] = wo[:, tile]


def marks_body(got, starts, ends, sums, weights):
    weights[...] = got[:, 192:288]
    at = lax.broadcasted_iota(jnp.int32, (64, 256), 1)
    at = at + (at // 64) * 64
    member = ((at >= starts[...]) & (at < ends[...])).astype(BF16)
    for i in range(2):
        part = got[:, 64 * i : 64 * i + 64].reshape(256, HEAD)
        sums[i] = dot(member, part, ((1,), (0,)))


def far_body(got, marks, out):
    k = got[:, 64:128].reshape(256, HEAD).astype(F32)
    v = got[:, 128:192].reshape(256, HEAD).astype(F32)
    far = dot(marks[0], k, ((1,), (1,)), HI) * SCALE
    peak = jnp.max(far, axis=-1, keepdims=True)
    far = jnp.exp(far - peak)
    mass = jnp.sum(far, axis=-1, keepdims=True)
    part = dot(far, v, ((1,), (0,)), HI)
    lane = lax.broadcasted_iota(jnp.int32, (64, HEAD), 1)
    stats = jnp.where(lane < 64, peak, mass)
    for i in range(2):
        out[:, i, :] = part[32 * i : 32 * i + 32]
        out[:, 2 + i, :] = stats[32 * i : 32 * i + 32]


def merge_body(parts, out):
    rows = []
    for i in range(2):
        stats = parts[:, 2 + i, :]
        low = lax.broadcasted_iota(jnp.int32, (32, HEAD), 1) < 64
        other = pltpu.roll(stats, 64, 1)
        peak = jnp.where(low, stats, other)
        mass = jnp.where(low, other, stats)
        factor = jnp.exp(peak - jnp.max(peak, axis=0, keepdims=True))
        total = jnp.sum(factor * mass, axis=0, keepdims=True)
        rows.append(jnp.sum(factor * parts[:, i, :], axis=0, keepdims=True) / total)
    for i in range(2):
        out[:, i, :] = jnp.broadcast_to(rows[i], (32, HEAD))


def spread(terms, out, y):
    for x in range(4):
        out[y * 4 + x] = terms[:, x * 512 : x * 512 + 512].astype(BF16)


def unmix(weights, tile, dest, lanes):
    for z in range(16):
        for c in range(2):
            for y in range(4):
                low = (z * 8 + y * 2 + c) * 16
                dest[low : low + 16, lanes] = weights[
                    z * 2 + c, y, tile * 16 : tile * 16 + 16, :
                ]


def proj_body(near, inverse, gathered, weights, out, wo):
    unmix(weights, 5, wo, slice(0, 128))
    gath = jnp.concatenate([gathered[:, 0, :], gathered[:, 1, :]], axis=0)
    mixer = dot(inverse[...], gath, ((1,), (0,)), HI)
    attn = dot(near[...], mixer, ((1,), (0,)), HI).astype(BF16)
    for y in range(4):
        spread(dot(attn[y * 64 : y * 64 + 64], wo[...], ((1,), (1,))), out, y)


def resid_body(parts, stream, out):
    total = parts[0].astype(F32)
    for i in range(1, 16):
        total = total + parts[i].astype(F32)
    resid = (stream[...].astype(F32) + total).astype(BF16)
    for i in range(16):
        out[i] = resid


def last_body(parts, resid, out):
    total = parts[0].astype(F32)
    for i in range(1, 16):
        total = total + parts[i].astype(F32)
    out[...] = (resid[0].astype(F32) + total).astype(BF16)


def ffn_body(whole, gain, weights, out, normed, w1, w2):
    for t in range(3):
        unmix(weights, t, w1, slice(t * 128, t * 128 + 128))
    for t in range(2):
        unmix(weights, 3 + t, w2, slice(t * 128, t * 128 + 128))
    for y in range(4):
        blocks = [whole[y * 4 + x].astype(F32) for x in range(4)]
        square = sum(jnp.sum(b * b, axis=-1, keepdims=True) for b in blocks)
        factor = lax.rsqrt(square * (1.0 / 2048.0) + EPS)
        for x in range(4):
            lanes = slice(x * 512, x * 512 + 512)
            normed[y * 64 : y * 64 + 64, lanes] = (
                blocks[x] * factor * gain[:, lanes]
            ).astype(BF16)
    first = dot(normed[...], w1[...], ((1,), (0,)))
    lane = lax.broadcasted_iota(jnp.int32, (256, 128), 1)
    gate, up, mixed = (first[:, t * 128 : t * 128 + 128] for t in range(3))
    hid0 = gate / (1.0 + jnp.exp(-gate)) * up
    hid1 = mixed / (1.0 + jnp.exp(-mixed)) * pltpu.roll(mixed, 64, 1)
    hid1 = jnp.where(lane < 64, hid1, 0.0)
    hidden = jnp.concatenate([hid0, hid1], axis=-1).astype(BF16)
    for y in range(4):
        spread(dot(hidden[y * 64 : y * 64 + 64], w2[...], ((1,), (1,))), out, y)


def inverse_rounds(land):
    eye = jnp.eye(land.shape[-1], dtype=F32)
    col_most = jnp.max(jnp.sum(land, axis=0))
    row_most = jnp.max(jnp.sum(land, axis=1))
    approx = land.T / (col_most * row_most)
    for _ in range(PINV_ITERS):
        prod = mm("ij,jk->ik", land, approx)
        inner = 7.0 * eye - prod
        inner = 15.0 * eye - mm("ij,jk->ik", prod, inner)
        inner = 13.0 * eye - mm("ij,jk->ik", prod, inner)
        approx = 0.25 * mm("ij,jk->ik", approx, inner)
    return approx


def on_device(queries, keys, values, stream, seg_lengths, gain, w_out, w_gate, w_up, w_down):
    z, c = lax.axis_index("z"), lax.axis_index("c")
    pack = kernel_call(pack_body, shape((4, 288, 128), BF16), 7)(
        queries, keys, values, w_gate, w_up, w_down.T, w_out.T
    )
    got = lax.all_to_all(pack, "y", 0, 0)
    ends = jnp.cumsum(seg_lengths) - (z * 512 + c * 64)
    sums, mine_w = kernel_call(
        marks_body, [shape((2, 64, HEAD), F32), shape((4, 96, 128), BF16)], 3
    )(got, (ends - seg_lengths)[:, None], ends[:, None])
    weights = lax.all_gather(mine_w, ("z", "c"), axis=0)

    mine = jnp.sum(lax.all_to_all(sums, "c", 0, 0), axis=0)
    mine = jnp.sum(lax.all_gather(mine, "z", axis=0), axis=0)
    marks = lax.all_gather(mine / seg_lengths.astype(F32)[:, None], "c", axis=0)
    qm, km = marks[0], marks[1]

    send = kernel_call(far_body, shape((32, 4, HEAD), F32), 2)(got, marks)
    parts = lax.all_to_all(send, ("z", "c"), 0, 0)
    gathered = kernel_call(merge_body, shape((32, 2, HEAD), F32), 1)(parts)
    gathered = lax.all_to_all(gathered, ("z", "c"), 0, 0)

    q32 = got[:, 0:64].reshape(256, HEAD).astype(F32)
    near = jax.nn.softmax(mm("td,jd->tj", q32, km) * SCALE, axis=-1)
    land = jax.nn.softmax(mm("id,jd->ij", qm, km) * SCALE, axis=-1)
    inverse = inverse_rounds(land)

    terms = kernel_call(
        proj_body, shape((16, 64, 512), BF16), 4, [pltpu.VMEM((2048, 128), BF16)]
    )(near, inverse, gathered, weights)
    resid = kernel_call(resid_body, shape((16, 64, 512), BF16), 2)(
        lax.all_to_all(terms, ("y", "x"), 0, 0), stream
    )
    whole = lax.all_to_all(resid, ("y", "x"), 0, 0)
    terms = kernel_call(
        ffn_body,
        shape((16, 64, 512), BF16),
        3,
        [
            pltpu.VMEM((256, 2048), BF16),
            pltpu.VMEM((2048, 384), BF16),
            pltpu.VMEM((2048, 256), BF16),
        ],
    )(whole, gain[None, :], weights)
    return kernel_call(last_body, shape((64, 512), BF16), 2)(
        lax.all_to_all(terms, ("y", "x"), 0, 0), resid[0:1]
    )


def solution(mesh):
    fine = Mesh(mesh.devices.reshape(16, 4, 2, 4), ("z", "y", "c", "x"))
    seq = ("z", "y", "c")
    return jax.shard_map(
        on_device,
        mesh=fine,
        in_specs=(
            P(seq, "x"),
            P(seq, "x"),
            P(seq, "x"),
            P(seq, "x"),
            P(),
            P(),
            P("x", seq),
            P(seq, "x"),
            P(seq, "x"),
            P("x", seq),
        ),
        out_specs=P(seq, "x"),
        check_vma=False,
    )
```

```python
import math

import jax
import jax.numpy as jnp
from jax import lax
from jax.experimental import pallas as pl
from jax.experimental.pallas import tpu as pltpu
from jax.sharding import Mesh
from jax.sharding import PartitionSpec as P

PINV_ITERS = 6
HEAD = 128
EPS = 1e-05
SCALE = 1.0 / math.sqrt(HEAD)
HI = lax.Precision.HIGHEST
F32 = jnp.float32
BF16 = jnp.bfloat16


def mm(spec, a, b):
    return jnp.einsum(spec, a, b, precision=HI, preferred_element_type=F32)


def dot(a, b, dims, precision=None):
    return lax.dot_general(
        a, b, (dims, ((), ())), precision=precision, preferred_element_type=F32
    )


def kernel_call(body, out_shape, n_in, scratch=(), cost=None):
    whole = pl.BlockSpec(memory_space=pltpu.VMEM)
    many = isinstance(out_shape, (list, tuple))
    return pl.pallas_call(
        body,
        out_shape=out_shape,
        in_specs=[whole] * n_in,
        out_specs=[whole] * len(out_shape) if many else whole,
        scratch_shapes=list(scratch),
        cost_estimate=cost,
    )


def shape(dims, dtype):
    return jax.ShapeDtypeStruct(dims, dtype)


def pack_body(q, k, v, wg, wu, wd, wo, out):
    for y in range(4):
        tile = slice(y * 128, y * 128 + 128)
        out[y, 0:64] = q[:, tile]
        out[y, 64:128] = k[:, tile]
        out[y, 128:192] = v[:, tile]
        out[y, 192:208] = wg[:, tile]
        out[y, 208:224] = wu[:, tile]
        last = slice(512 + (y // 2) * 128, 640 + (y // 2) * 128)
        lane = lax.broadcasted_iota(jnp.int32, (16, 128), 1)
        g, u, d = (w[:, last].astype(F32) for w in (wg, wu, wd))
        if y % 2 == 0:
            mixed = jnp.where(lane < 64, g, pltpu.roll(u, 64, 1))
        else:
            mixed = jnp.where(lane < 64, pltpu.roll(g, 64, 1), u)
            d = pltpu.roll(d, 64, 1)
        out[y, 224:240] = mixed.astype(BF16)
        out[y, 240:256] = wd[:, tile]
        out[y, 256:272] = jnp.where(lane < 64, d, 0.0).astype(BF16)
        out[y, 272:288] = wo[:, tile]


def marks_body(got, starts, ends, sums, weights):
    weights[...] = got[:, 192:288]
    at = lax.broadcasted_iota(jnp.int32, (64, 256), 1)
    at = at + (at // 64) * 64
    member = ((at >= starts[...]) & (at < ends[...])).astype(BF16)
    for i in range(2):
        part = dot(member, got[:, 64 * i : 64 * i + 64].reshape(256, HEAD), ((1,), (0,)))
        sums[:, 2 * i, :] = part[0:32]
        sums[:, 2 * i + 1, :] = part[32:64]


def total_body(parts, counts, out):
    for i in range(4):
        row = jnp.sum(parts[:, i, :], axis=0, keepdims=True) / counts[i % 2]
        out[:, i, :] = jnp.broadcast_to(row, (32, HEAD))


def both(ref, i):
    return jnp.concatenate([ref[:, i, :], ref[:, i + 1, :]], axis=0)


def far_body(got, marks, out):
    k = got[:, 64:128].reshape(256, HEAD).astype(F32)
    v = got[:, 128:192].reshape(256, HEAD).astype(F32)
    far = dot(both(marks, 0), k, ((1,), (1,)), HI) * SCALE
    peak = jnp.max(far, axis=-1, keepdims=True)
    far = jnp.exp(far - peak)
    mass = jnp.sum(far, axis=-1, keepdims=True)
    part = dot(far, v, ((1,), (0,)), HI)
    lane = lax.broadcasted_iota(jnp.int32, (64, HEAD), 1)
    stats = jnp.where(lane < 64, peak, mass)
    for i in range(2):
        out[:, i, :] = part[32 * i : 32 * i + 32]
        out[:, 2 + i, :] = stats[32 * i : 32 * i + 32]


def merge_body(parts, out):
    rows = []
    for i in range(2):
        stats = parts[:, 2 + i, :]
        low = lax.broadcasted_iota(jnp.int32, (32, HEAD), 1) < 64
        other = pltpu.roll(stats, 64, 1)
        peak = jnp.where(low, stats, other)
        mass = jnp.where(low, other, stats)
        factor = jnp.exp(peak - jnp.max(peak, axis=0, keepdims=True))
        total = jnp.sum(factor * mass, axis=0, keepdims=True)
        rows.append(jnp.sum(factor * parts[:, i, :], axis=0, keepdims=True) / total)
    for i in range(2):
        out[:, i, :] = jnp.broadcast_to(rows[i], (32, HEAD))


def spread(terms, out, y):
    for x in range(4):
        out[y * 4 + x] = terms[:, x * 512 : x * 512 + 512].astype(BF16)


def unmix(weights, tile, dest, lanes):
    for z in range(16):
        for c in range(2):
            for y in range(4):
                low = (z * 8 + y * 2 + c) * 16
                dest[low : low + 16, lanes] = weights[
                    z * 2 + c, y, tile * 16 : tile * 16 + 16, :
                ]


def unmix_body(weights, w1, w2, wo):
    for t in range(3):
        unmix(weights, t, w1, slice(t * 128, t * 128 + 128))
    for t in range(2):
        unmix(weights, 3 + t, w2, slice(t * 128, t * 128 + 128))
    unmix(weights, 5, wo, slice(0, 128))


def proj_body(near, inverse, gathered, wo, out):
    mixer = dot(inverse[...], both(gathered, 0), ((1,), (0,)), HI)
    attn = dot(near[...], mixer, ((1,), (0,)), HI).astype(BF16)
    for y in range(4):
        spread(dot(attn[y * 64 : y * 64 + 64], wo[...], ((1,), (1,))), out, y)


def resid_body(parts, stream, out):
    total = parts[0].astype(F32)
    for i in range(1, 16):
        total = total + parts[i].astype(F32)
    resid = (stream[...].astype(F32) + total).astype(BF16)
    for i in range(16):
        out[i] = resid


def last_body(parts, resid, out):
    total = parts[0].astype(F32)
    for i in range(1, 16):
        total = total + parts[i].astype(F32)
    out[...] = (resid[0].astype(F32) + total).astype(BF16)


def ffn_body(whole, gain, w1, w2, out, normed):
    for y in range(4):
        blocks = [whole[y * 4 + x].astype(F32) for x in range(4)]
        square = sum(jnp.sum(b * b, axis=-1, keepdims=True) for b in blocks)
        factor = lax.rsqrt(square * (1.0 / 2048.0) + EPS)
        for x in range(4):
            lanes = slice(x * 512, x * 512 + 512)
            normed[y * 64 : y * 64 + 64, lanes] = (
                blocks[x] * factor * gain[:, lanes]
            ).astype(BF16)
    first = dot(normed[...], w1[...], ((1,), (0,)))
    lane = lax.broadcasted_iota(jnp.int32, (256, 128), 1)
    gate, up, mixed = (first[:, t * 128 : t * 128 + 128] for t in range(3))
    hid0 = gate / (1.0 + jnp.exp(-gate)) * up
    hid1 = mixed / (1.0 + jnp.exp(-mixed)) * pltpu.roll(mixed, 64, 1)
    hid1 = jnp.where(lane < 64, hid1, 0.0)
    hidden = jnp.concatenate([hid0, hid1], axis=-1).astype(BF16)
    for y in range(4):
        spread(dot(hidden[y * 64 : y * 64 + 64], w2[...], ((1,), (1,))), out, y)


def inverse_rounds(land):
    eye = jnp.eye(land.shape[-1], dtype=F32)
    col_most = jnp.max(jnp.sum(land, axis=0))
    row_most = jnp.max(jnp.sum(land, axis=1))
    approx = land.T / (col_most * row_most)
    for _ in range(PINV_ITERS):
        prod = mm("ij,jk->ik", land, approx)
        inner = 7.0 * eye - prod
        inner = 15.0 * eye - mm("ij,jk->ik", prod, inner)
        inner = 13.0 * eye - mm("ij,jk->ik", prod, inner)
        approx = 0.25 * mm("ij,jk->ik", approx, inner)
    return approx


def on_device(queries, keys, values, stream, seg_lengths, gain, w_out, w_gate, w_up, w_down):
    z, c = lax.axis_index("z"), lax.axis_index("c")
    pack = kernel_call(pack_body, shape((4, 288, 128), BF16), 7)(
        queries, keys, values, w_gate, w_up, w_down.T, w_out.T
    )
    got = lax.all_to_all(pack, "y", 0, 0)
    ends = jnp.cumsum(seg_lengths) - (z * 512 + c * 64)
    sums, mine_w = kernel_call(
        marks_body, [shape((32, 4, HEAD), F32), shape((4, 96, 128), BF16)], 3
    )(got, (ends - seg_lengths)[:, None], ends[:, None])
    weights = lax.all_gather(mine_w, ("z", "c"), axis=0)
    w1, w2, wo = kernel_call(
        unmix_body,
        [shape((2048, 384), BF16), shape((2048, 256), BF16), shape((2048, 128), BF16)],
        1,
    )(weights)

    counts = lax.dynamic_index_in_dim(seg_lengths.reshape(2, 32), z * 2 + c, 1, keepdims=False)
    counts = jnp.broadcast_to(counts.astype(F32)[:, None, None], (2, 1, HEAD))
    marks = lax.all_to_all(sums, ("z", "c"), 0, 0)
    marks = kernel_call(total_body, shape((32, 4, HEAD), F32), 2)(marks, counts)
    marks = lax.all_to_all(marks, ("z", "c"), 0, 0)
    qm = jnp.concatenate([marks[:, 0], marks[:, 1]], axis=0)
    km = jnp.concatenate([marks[:, 2], marks[:, 3]], axis=0)

    send = kernel_call(far_body, shape((32, 4, HEAD), F32), 2)(got, marks)
    parts = lax.all_to_all(send, ("z", "c"), 0, 0)
    gathered = kernel_call(merge_body, shape((32, 2, HEAD), F32), 1)(parts)
    gathered = lax.all_to_all(gathered, ("z", "c"), 0, 0)

    q32 = got[:, 0:64].reshape(256, HEAD).astype(F32)
    near = jax.nn.softmax(mm("td,jd->tj", q32, km) * SCALE, axis=-1)
    land = jax.nn.softmax(mm("id,jd->ij", qm, km) * SCALE, axis=-1)
    inverse = inverse_rounds(land)

    terms = kernel_call(proj_body, shape((16, 64, 512), BF16), 4)(near, inverse, gathered, wo)
    resid = kernel_call(resid_body, shape((16, 64, 512), BF16), 2)(
        lax.all_to_all(terms, ("y", "x"), 0, 0), stream
    )
    whole = lax.all_to_all(resid, ("y", "x"), 0, 0)
    terms = kernel_call(
        ffn_body, shape((16, 64, 512), BF16), 4, [pltpu.VMEM((256, 2048), BF16)]
    )(whole, gain[None, :], w1, w2)
    return kernel_call(last_body, shape((64, 512), BF16), 2)(
        lax.all_to_all(terms, ("y", "x"), 0, 0), resid[0:1]
    )


def solution(mesh):
    fine = Mesh(mesh.devices.reshape(16, 4, 2, 4), ("z", "y", "c", "x"))
    seq = ("z", "y", "c")
    return jax.shard_map(
        on_device,
        mesh=fine,
        in_specs=(
            P(seq, "x"),
            P(seq, "x"),
            P(seq, "x"),
            P(seq, "x"),
            P(),
            P(),
            P("x", seq),
            P(seq, "x"),
            P(seq, "x"),
            P("x", seq),
        ),
        out_specs=P(seq, "x"),
        check_vma=False,
    )
```

```python
import math

import jax
import jax.numpy as jnp
from jax import lax
from jax.experimental import pallas as pl
from jax.experimental.pallas import tpu as pltpu
from jax.sharding import Mesh
from jax.sharding import PartitionSpec as P

PINV_ITERS = 6
HEAD = 128
EPS = 1e-05
SCALE = 1.0 / math.sqrt(HEAD)
HI = lax.Precision.HIGHEST
F32 = jnp.float32
BF16 = jnp.bfloat16


def mm(spec, a, b):
    return jnp.einsum(spec, a, b, precision=HI, preferred_element_type=F32)


def dot(a, b, dims, precision=None):
    return lax.dot_general(
        a, b, (dims, ((), ())), precision=precision, preferred_element_type=F32
    )


def kernel_call(body, out_shape, n_in, scratch=(), cost=None):
    whole = pl.BlockSpec(memory_space=pltpu.VMEM)
    many = isinstance(out_shape, (list, tuple))
    return pl.pallas_call(
        body,
        out_shape=out_shape,
        in_specs=[whole] * n_in,
        out_specs=[whole] * len(out_shape) if many else whole,
        scratch_shapes=list(scratch),
        cost_estimate=cost,
    )


def shape(dims, dtype):
    return jax.ShapeDtypeStruct(dims, dtype)


def pack_body(q, k, v, wg, wu, wd, wo, out):
    for y in range(4):
        tile = slice(y * 128, y * 128 + 128)
        out[y, 0:64] = q[:, tile]
        out[y, 64:128] = k[:, tile]
        out[y, 128:192] = v[:, tile]
        out[y, 192:208] = wo[:, tile]
        for t in range(3):
            low = ((y % 2) * 3 + t) * 128
            for i, w in enumerate((wg, wu, wd)):
                at = 208 + (3 * i + t) * 16
                out[y, at : at + 16] = w[:, low : low + 128]


def marks_body(got, starts, ends, sums, weights):
    weights[...] = got[:, 192:352]
    at = lax.broadcasted_iota(jnp.int32, (64, 256), 1)
    at = at + (at // 64) * 64
    member = ((at >= starts[...]) & (at < ends[...])).astype(BF16)
    for i in range(2):
        part = got[:, 64 * i : 64 * i + 64].reshape(256, HEAD)
        sums[i] = dot(member, part, ((1,), (0,)))


def far_body(got, marks, out):
    k = got[:, 64:128].reshape(256, HEAD).astype(F32)
    v = got[:, 128:192].reshape(256, HEAD).astype(F32)
    far = dot(marks[0], k, ((1,), (1,)), HI) * SCALE
    peak = jnp.max(far, axis=-1, keepdims=True)
    far = jnp.exp(far - peak)
    mass = jnp.sum(far, axis=-1, keepdims=True)
    part = dot(far, v, ((1,), (0,)), HI)
    lane = lax.broadcasted_iota(jnp.int32, (64, HEAD), 1)
    stats = jnp.where(lane < 64, peak, mass)
    for i in range(2):
        out[:, i, :] = part[32 * i : 32 * i + 32]
        out[:, 2 + i, :] = stats[32 * i : 32 * i + 32]


def merge_body(parts, out):
    rows = []
    for i in range(2):
        stats = parts[:, 2 + i, :]
        low = lax.broadcasted_iota(jnp.int32, (32, HEAD), 1) < 64
        other = pltpu.roll(stats, 64, 1)
        peak = jnp.where(low, stats, other)
        mass = jnp.where(low, other, stats)
        factor = jnp.exp(peak - jnp.max(peak, axis=0, keepdims=True))
        total = jnp.sum(factor * mass, axis=0, keepdims=True)
        rows.append(jnp.sum(factor * parts[:, i, :], axis=0, keepdims=True) / total)
    for i in range(2):
        out[:, i, :] = jnp.broadcast_to(rows[i], (32, HEAD))


def spread(terms, out):
    for y in range(terms.shape[0] // 64):
        for x in range(4):
            out[y * 4 + x] = terms[y * 64 : y * 64 + 64, x * 512 : x * 512 + 512].astype(BF16)


def unmix(weights, tile, dest, lanes):
    for z in range(16):
        for c in range(2):
            for y in range(4):
                low = (z * 8 + y * 2 + c) * 16
                dest[low : low + 16, lanes] = weights[
                    z * 2 + c, y, tile * 16 : tile * 16 + 16, :
                ]


def unmix_body(weights, w1, w2):
    for t in range(6):
        unmix(weights, 1 + t, w1, slice(t * 128, t * 128 + 128))
    for t in range(3):
        unmix(weights, 7 + t, w2, slice(t * 128, t * 128 + 128))


def both(ref, i):
    return jnp.concatenate([ref[:, i, :], ref[:, i + 1, :]], axis=0)


def proj_body(near, inverse, gathered, weights, out, wo):
    unmix(weights, 0, wo, slice(0, 128))
    mixer = dot(inverse[...], both(gathered, 0), ((1,), (0,)), HI)
    attn = dot(near[...], mixer, ((1,), (0,)), HI).astype(BF16)
    spread(dot(attn, wo[...], ((1,), (1,))), out)


def ffn_body(whole, gain, w1, w2, out, normed):
    for y in range(2):
        blocks = [whole[y * 4 + x].astype(F32) for x in range(4)]
        square = sum(jnp.sum(b * b, axis=-1, keepdims=True) for b in blocks)
        factor = lax.rsqrt(square * (1.0 / 2048.0) + EPS)
        for x in range(4):
            lanes = slice(x * 512, x * 512 + 512)
            normed[y * 64 : y * 64 + 64, lanes] = (
                blocks[x] * factor * gain[:, lanes]
            ).astype(BF16)
    first = dot(normed[...], w1[...], ((1,), (0,)))
    gate, up = first[:, :384], first[:, 384:]
    hidden = (gate / (1.0 + jnp.exp(-gate)) * up).astype(BF16)
    spread(dot(hidden, w2[...], ((1,), (1,))), out)


def inverse_rounds(land):
    eye = jnp.eye(land.shape[-1], dtype=F32)
    col_most = jnp.max(jnp.sum(land, axis=0))
    row_most = jnp.max(jnp.sum(land, axis=1))
    approx = land.T / (col_most * row_most)
    for _ in range(PINV_ITERS):
        prod = mm("ij,jk->ik", land, approx)
        inner = 7.0 * eye - prod
        inner = 15.0 * eye - mm("ij,jk->ik", prod, inner)
        inner = 13.0 * eye - mm("ij,jk->ik", prod, inner)
        approx = 0.25 * mm("ij,jk->ik", approx, inner)
    return approx


def on_device(queries, keys, values, stream, seg_lengths, gain, w_out, w_gate, w_up, w_down):
    z, c = lax.axis_index("z"), lax.axis_index("c")
    y_axes = ("yh", "yl")
    pack = kernel_call(pack_body, shape((4, 352, 128), BF16), 7)(
        queries, keys, values, w_gate, w_up, w_down.T, w_out.T
    )
    got = lax.all_to_all(pack, y_axes, 0, 0)
    ends = jnp.cumsum(seg_lengths) - (z * 512 + c * 64)
    sums, mine_w = kernel_call(
        marks_body, [shape((2, 64, HEAD), F32), shape((4, 160, 128), BF16)], 3
    )(got, (ends - seg_lengths)[:, None], ends[:, None])
    weights = lax.all_gather(mine_w, ("z", "c"), axis=0)

    mine = jnp.sum(lax.all_to_all(sums, "c", 0, 0), axis=0)
    mine = jnp.sum(lax.all_gather(mine, "z", axis=0), axis=0)
    marks = lax.all_gather(mine / seg_lengths.astype(F32)[:, None], "c", axis=0)
    qm, km = marks[0], marks[1]

    send = kernel_call(far_body, shape((32, 4, HEAD), F32), 2)(got, marks)
    parts = lax.all_to_all(send, ("z", "c"), 0, 0)
    gathered = kernel_call(merge_body, shape((32, 2, HEAD), F32), 1)(parts)
    gathered = lax.all_to_all(gathered, ("z", "c"), 0, 0)

    q32 = got[:, 0:64].reshape(256, HEAD).astype(F32)
    near = jax.nn.softmax(mm("td,jd->tj", q32, km) * SCALE, axis=-1)
    land = jax.nn.softmax(mm("id,jd->ij", qm, km) * SCALE, axis=-1)
    inverse = inverse_rounds(land)

    block = pl.BlockSpec(memory_space=pltpu.VMEM)
    terms = pl.pallas_call(
        proj_body,
        grid=(1,),
        out_shape=shape((16, 64, 512), BF16),
        in_specs=[block] * 3 + [pl.BlockSpec((32, 4, 16, 128), lambda i: (0, 0, 0, 0))],
        out_specs=block,
        scratch_shapes=[pltpu.VMEM((2048, 128), BF16)],
    )(near, inverse, gathered, weights)
    parts = lax.all_to_all(terms, (*y_axes, "x"), 0, 0)
    w1, w2 = kernel_call(unmix_body, [shape((2048, 768), BF16), shape((2048, 384), BF16)], 1)(
        weights
    )
    resid = (stream.astype(F32) + jnp.sum(parts.astype(F32), axis=0)).astype(BF16)
    whole = lax.all_to_all(jnp.broadcast_to(resid[None], (8, 64, 512)), ("yl", "x"), 0, 0)
    terms = kernel_call(
        ffn_body, shape((8, 64, 512), BF16), 4, [pltpu.VMEM((128, 2048), BF16)]
    )(whole, gain[None, :], w1, w2)
    parts = lax.all_to_all(terms, ("yl", "x"), 0, 0)
    return (resid.astype(F32) + jnp.sum(parts.astype(F32), axis=0)).astype(BF16)


def solution(mesh):
    fine = Mesh(mesh.devices.reshape(16, 2, 2, 2, 4), ("z", "yh", "yl", "c", "x"))
    seq = ("z", "yh", "yl", "c")
    return jax.shard_map(
        on_device,
        mesh=fine,
        in_specs=(
            P(seq, "x"),
            P(seq, "x"),
            P(seq, "x"),
            P(seq, "x"),
            P(),
            P(),
            P("x", seq),
            P(seq, "x"),
            P(seq, "x"),
            P("x", seq),
        ),
        out_specs=P(seq, "x"),
        check_vma=False,
    )
```

```python
import math

import jax
import jax.numpy as jnp
from jax import lax
from jax.experimental import pallas as pl
from jax.experimental.pallas import tpu as pltpu
from jax.sharding import Mesh
from jax.sharding import PartitionSpec as P

PINV_ITERS = 6
HEAD = 128
EPS = 1e-05
SCALE = 1.0 / math.sqrt(HEAD)
HI = lax.Precision.HIGHEST
F32 = jnp.float32
BF16 = jnp.bfloat16


def dot(a, b, dims, precision=None):
    return lax.dot_general(
        a, b, (dims, ((), ())), precision=precision, preferred_element_type=F32
    )


def kernel_call(body, out_shape, n_in, scratch=(), cost=None):
    whole = pl.BlockSpec(memory_space=pltpu.VMEM)
    many = isinstance(out_shape, (list, tuple))
    return pl.pallas_call(
        body,
        out_shape=out_shape,
        in_specs=[whole] * n_in,
        out_specs=[whole] * len(out_shape) if many else whole,
        scratch_shapes=list(scratch),
        cost_estimate=cost,
    )


def shape(dims, dtype):
    return jax.ShapeDtypeStruct(dims, dtype)


def pack_body(q, k, v, wg, wu, wd, wo, out):
    for y in range(4):
        tile = slice(y * 128, y * 128 + 128)
        out[y, 0:64] = q[:, tile]
        out[y, 64:128] = k[:, tile]
        out[y, 128:192] = v[:, tile]
        out[y, 192:208] = wo[:, tile]
        for t in range(3):
            low = ((y % 2) * 3 + t) * 128
            for i, w in enumerate((wg, wu, wd)):
                at = 208 + (3 * i + t) * 16
                out[y, at : at + 16] = w[:, low : low + 128]


def marks_body(got, starts, ends, sums, weights, kv):
    weights[...] = got[:, 192:352]
    kv[...] = got[:, 64:192]
    at = lax.broadcasted_iota(jnp.int32, (64, 256), 1)
    at = at + (at // 64) * 64
    member = ((at >= starts[...]) & (at < ends[...])).astype(BF16)
    for i in range(2):
        part = got[:, 64 * i : 64 * i + 64].reshape(256, HEAD)
        sums[i] = dot(member, part, ((1,), (0,)))


def far_body(core, mine, other, marks, out):
    query = marks[0, pl.ds(core[0] * 32, 32), :]
    far = [
        dot(query, kv[:, 0:64].reshape(256, HEAD).astype(F32), ((1,), (1,)), HI) * SCALE
        for kv in (mine, other)
    ]
    peak = jnp.maximum(*(jnp.max(f, axis=-1, keepdims=True) for f in far))
    far = [jnp.exp(f - peak) for f in far]
    mass = sum(jnp.sum(f, axis=-1, keepdims=True) for f in far)
    part = sum(
        dot(f, kv[:, 64:128].reshape(256, HEAD).astype(F32), ((1,), (0,)), HI)
        for f, kv in zip(far, (mine, other))
    )
    row = lax.broadcasted_iota(jnp.int32, (32, HEAD), 0)
    lane = lax.broadcasted_iota(jnp.int32, (32, HEAD), 1)
    stats = jnp.where(lane == row, peak, 0.0) + jnp.where(lane == row + 32, mass, 0.0)
    stats = jnp.broadcast_to(jnp.sum(stats, axis=0, keepdims=True), (8, HEAD))
    for z in range(16):
        out[z, 0:32] = part
        out[z, 32:40] = stats


def merge_body(parts, out):
    row = lax.broadcasted_iota(jnp.int32, (16, 32, HEAD), 1)
    lane = lax.broadcasted_iota(jnp.int32, (16, 32, HEAD), 2)
    stats = jnp.broadcast_to(parts[:, 32:33, :], (16, 32, HEAD))
    peak = jnp.sum(jnp.where(lane == row, stats, 0.0), axis=-1, keepdims=True)
    mass = jnp.sum(jnp.where(lane == row + 32, stats, 0.0), axis=-1, keepdims=True)
    factor = jnp.exp(peak - jnp.max(peak, axis=0, keepdims=True))
    total = jnp.sum(factor * mass, axis=0)
    out[...] = jnp.sum(factor * parts[:, 0:32, :], axis=0) / total


def softmax(scores, axis):
    scores = jnp.exp(scores - jnp.max(scores, axis=axis, keepdims=True))
    return scores / jnp.sum(scores, axis=axis, keepdims=True)


def near_body(got, marks, near, inverse):
    qm, km = marks[0], marks[1]
    query = got[:, 0:64].reshape(256, HEAD).astype(F32)
    near[...] = softmax(dot(query, km, ((1,), (1,)), HI) * SCALE, -1)
    land = softmax(dot(qm, km, ((1,), (1,)), HI) * SCALE, 1)
    across = softmax(dot(km, qm, ((1,), (1,)), HI) * SCALE, 0)
    most = jnp.max(jnp.sum(land, axis=0, keepdims=True), axis=1, keepdims=True) * jnp.max(
        jnp.sum(land, axis=1, keepdims=True), axis=0, keepdims=True
    )
    row = lax.broadcasted_iota(jnp.int32, (64, 64), 0)
    eye = (row == lax.broadcasted_iota(jnp.int32, (64, 64), 1)).astype(F32)
    mul = lambda a, b: dot(a, b, ((1,), (0,)), HI)
    approx = across / most
    for _ in range(PINV_ITERS):
        prod = mul(land, approx)
        inner = 7.0 * eye - prod
        inner = 15.0 * eye - mul(prod, inner)
        inner = 13.0 * eye - mul(prod, inner)
        approx = 0.25 * mul(approx, inner)
    inverse[...] = approx


def spread(terms, out):
    for y in range(terms.shape[0] // 64):
        for x in range(4):
            out[y * 4 + x] = terms[y * 64 : y * 64 + 64, x * 512 : x * 512 + 512].astype(BF16)


def unmix(weights, tile, dest, lanes):
    for z in range(16):
        for c in range(2):
            for y in range(4):
                low = (z * 8 + y * 2 + c) * 16
                dest[low : low + 16, lanes] = weights[
                    z * 2 + c, y, tile * 16 : tile * 16 + 16, :
                ]


def unmix_body(weights, w1, w2):
    for t in range(6):
        unmix(weights, 1 + t, w1, slice(t * 128, t * 128 + 128))
    for t in range(3):
        unmix(weights, 7 + t, w2, slice(t * 128, t * 128 + 128))


def proj_body(near, inverse, gathered, weights, out, wo):
    unmix(weights, 0, wo, slice(0, 128))
    mixer = dot(inverse[...], gathered[...], ((1,), (0,)), HI)
    attn = dot(near[...], mixer, ((1,), (0,)), HI).astype(BF16)
    spread(dot(attn, wo[...], ((1,), (1,))), out)


def ffn_body(whole, gain, w1, w2, out, normed):
    for y in range(2):
        blocks = [whole[y * 4 + x].astype(F32) for x in range(4)]
        square = sum(jnp.sum(b * b, axis=-1, keepdims=True) for b in blocks)
        factor = lax.rsqrt(square * (1.0 / 2048.0) + EPS)
        for x in range(4):
            lanes = slice(x * 512, x * 512 + 512)
            normed[y * 64 : y * 64 + 64, lanes] = (
                blocks[x] * factor * gain[:, lanes]
            ).astype(BF16)
    first = dot(normed[...], w1[...], ((1,), (0,)))
    gate, up = first[:, :384], first[:, 384:]
    hidden = (gate / (1.0 + jnp.exp(-gate)) * up).astype(BF16)
    spread(dot(hidden, w2[...], ((1,), (1,))), out)


def on_device(queries, keys, values, stream, seg_lengths, gain, w_out, w_gate, w_up, w_down):
    z, c = lax.axis_index("z"), lax.axis_index("c")
    y_axes = ("yh", "yl")
    pack = kernel_call(pack_body, shape((4, 352, 128), BF16), 7)(
        queries, keys, values, w_gate, w_up, w_down.T, w_out.T
    )
    got = lax.all_to_all(pack, y_axes, 0, 0)
    ends = jnp.cumsum(seg_lengths) - (z * 512 + c * 64)
    sums, mine_w, kv = kernel_call(
        marks_body,
        [shape((2, 64, HEAD), F32), shape((4, 160, 128), BF16), shape((4, 128, 128), BF16)],
        3,
    )(got, (ends - seg_lengths)[:, None], ends[:, None])
    weights = lax.all_gather(mine_w, ("z", "c"), axis=0)

    other = lax.ppermute(kv, "c", [(0, 1), (1, 0)])
    mine = lax.all_to_all(sums, "c", 0, 0)
    mine, other = lax.optimization_barrier((mine, other))
    mine = jnp.sum(mine, axis=0)
    mine = jnp.sum(lax.all_gather(mine, "z", axis=0), axis=0)
    marks = lax.all_gather(mine / seg_lengths.astype(F32)[:, None], "c", axis=0)
    block = pl.BlockSpec(memory_space=pltpu.VMEM)
    send = pl.pallas_call(
        far_body,
        out_shape=shape((16, 40, HEAD), F32),
        in_specs=[pl.BlockSpec(memory_space=pltpu.SMEM)] + [block] * 3,
        out_specs=block,
    )(c[None], kv, other, marks)
    parts = lax.all_to_all(send, "z", 0, 0)
    near, inverse = kernel_call(
        near_body,
        [shape((256, 64), F32), shape((64, 64), F32)],
        2,
        cost=pl.CostEstimate(flops=10**9, bytes_accessed=2 * 10**7, transcendentals=0),
    )(got, marks)
    gathered = kernel_call(merge_body, shape((32, HEAD), F32), 1)(parts)
    gathered = lax.all_gather(gathered, "c", axis=0, tiled=True)

    terms = pl.pallas_call(
        proj_body,
        grid=(1,),
        out_shape=shape((16, 64, 512), BF16),
        in_specs=[block] * 3 + [pl.BlockSpec((32, 4, 16, 128), lambda i: (0, 0, 0, 0))],
        out_specs=block,
        scratch_shapes=[pltpu.VMEM((2048, 128), BF16)],
    )(near, inverse, gathered, weights)
    parts = lax.all_to_all(terms, (*y_axes, "x"), 0, 0)
    w1, w2 = kernel_call(unmix_body, [shape((2048, 768), BF16), shape((2048, 384), BF16)], 1)(
        weights
    )
    resid = (stream.astype(F32) + jnp.sum(parts.astype(F32), axis=0)).astype(BF16)
    whole = lax.all_to_all(jnp.broadcast_to(resid[None], (8, 64, 512)), ("yl", "x"), 0, 0)
    terms = kernel_call(
        ffn_body, shape((8, 64, 512), BF16), 4, [pltpu.VMEM((128, 2048), BF16)]
    )(whole, gain[None, :], w1, w2)
    parts = lax.all_to_all(terms, ("yl", "x"), 0, 0)
    return (resid.astype(F32) + jnp.sum(parts.astype(F32), axis=0)).astype(BF16)


def solution(mesh):
    fine = Mesh(mesh.devices.reshape(16, 2, 2, 2, 4), ("z", "yh", "yl", "c", "x"))
    seq = ("z", "yh", "yl", "c")
    return jax.shard_map(
        on_device,
        mesh=fine,
        in_specs=(
            P(seq, "x"),
            P(seq, "x"),
            P(seq, "x"),
            P(seq, "x"),
            P(),
            P(),
            P("x", seq),
            P(seq, "x"),
            P(seq, "x"),
            P("x", seq),
        ),
        out_specs=P(seq, "x"),
        check_vma=False,
    )
```

```python
import math

import jax
import jax.numpy as jnp
from jax import lax
from jax.experimental import pallas as pl
from jax.experimental.pallas import tpu as pltpu
from jax.sharding import Mesh
from jax.sharding import PartitionSpec as P

PINV_ITERS = 6
HEAD = 128
EPS = 1e-05
SCALE = 1.0 / math.sqrt(HEAD)
HI = lax.Precision.HIGHEST
F32 = jnp.float32
BF16 = jnp.bfloat16
SMALL = 24 << 20
LARGE = 60 << 20


def dot(a, b, dims, precision=None):
    return lax.dot_general(
        a, b, (dims, ((), ())), precision=precision, preferred_element_type=F32
    )


def kernel_call(body, out_shape, n_in, scratch=(), cost=None, core=None, grant=SMALL, n_far=0):
    whole = pl.BlockSpec(memory_space=pltpu.VMEM)
    many = isinstance(out_shape, (list, tuple))
    call = pl.pallas_call(
        body,
        out_shape=out_shape,
        in_specs=([] if core is None else [pl.BlockSpec(memory_space=pltpu.SMEM)])
        + [whole] * n_in
        + [pl.BlockSpec(memory_space=pltpu.HBM)] * n_far,
        out_specs=[whole] * len(out_shape) if many else whole,
        scratch_shapes=list(scratch),
        cost_estimate=cost,
        compiler_params=pltpu.CompilerParams(vmem_limit_bytes=grant),
    )
    return call if core is None else lambda *args: call(core, *args)


def shape(dims, dtype):
    return jax.ShapeDtypeStruct(dims, dtype)


def pack_body(q, k, v, wg, wu, wd, wo, out):
    for y in range(4):
        tile = slice(y * 128, y * 128 + 128)
        out[y, 0:64] = q[:, tile]
        out[y, 64:128] = k[:, tile]
        out[y, 128:192] = v[:, tile]
        out[y, 192:208] = wo[:, tile]
        for t in range(3):
            low = ((y % 2) * 3 + t) * 128
            for i, w in enumerate((wg, wu, wd)):
                at = 208 + (3 * i + t) * 16
                out[y, at : at + 16] = w[:, low : low + 128]


def marks_body(core, mine, other, starts, ends, out):
    c = core[0]
    low = pl.multiple_of(c * 64, 64)
    total = None
    for got, place in ((mine, c), (other, 1 - c)):
        at = lax.broadcasted_iota(jnp.int32, (64, 256), 1)
        at = at + (at // 64) * 64 + place * 64
        member = ((at >= starts[...]) & (at < ends[...])).astype(BF16)
        part = dot(member, got[:, pl.ds(low, 64), :].reshape(256, HEAD), ((1,), (0,)))
        total = part if total is None else total + part
    out[...] = total


def far_body(core, mine, other, marks, out):
    query = marks[0, pl.ds(core[0] * 32, 32), :]
    far = [
        dot(query, got[:, 64:128].reshape(256, HEAD).astype(F32), ((1,), (1,)), HI) * SCALE
        for got in (mine, other)
    ]
    peak = jnp.maximum(*(jnp.max(f, axis=-1, keepdims=True) for f in far))
    far = [jnp.exp(f - peak) for f in far]
    mass = sum(jnp.sum(f, axis=-1, keepdims=True) for f in far)
    part = sum(
        dot(f, got[:, 128:192].reshape(256, HEAD).astype(F32), ((1,), (0,)), HI)
        for f, got in zip(far, (mine, other))
    )
    row = lax.broadcasted_iota(jnp.int32, (32, HEAD), 0)
    lane = lax.broadcasted_iota(jnp.int32, (32, HEAD), 1)
    stats = jnp.where(lane == row, peak, 0.0) + jnp.where(lane == row + 32, mass, 0.0)
    stats = jnp.broadcast_to(jnp.sum(stats, axis=0, keepdims=True), (8, HEAD))
    for z in range(16):
        out[z, 0:32] = part
        out[z, 32:40] = stats


def merge_body(parts, out):
    row = lax.broadcasted_iota(jnp.int32, (16, 32, HEAD), 1)
    lane = lax.broadcasted_iota(jnp.int32, (16, 32, HEAD), 2)
    stats = jnp.broadcast_to(parts[:, 32:33, :], (16, 32, HEAD))
    peak = jnp.sum(jnp.where(lane == row, stats, 0.0), axis=-1, keepdims=True)
    mass = jnp.sum(jnp.where(lane == row + 32, stats, 0.0), axis=-1, keepdims=True)
    factor = jnp.exp(peak - jnp.max(peak, axis=0, keepdims=True))
    total = jnp.sum(factor * mass, axis=0)
    out[...] = jnp.sum(factor * parts[:, 0:32, :], axis=0) / total


def softmax(scores, axis):
    scores = jnp.exp(scores - jnp.max(scores, axis=axis, keepdims=True))
    return scores / jnp.sum(scores, axis=axis, keepdims=True)


def near_body(got, marks, near, inverse):
    qm, km = marks[0], marks[1]
    query = got[:, 0:64].reshape(256, HEAD).astype(F32)
    near[...] = softmax(dot(query, km, ((1,), (1,)), HI) * SCALE, -1)
    land = softmax(dot(qm, km, ((1,), (1,)), HI) * SCALE, 1)
    across = softmax(dot(km, qm, ((1,), (1,)), HI) * SCALE, 0)
    most = jnp.max(jnp.sum(land, axis=0, keepdims=True), axis=1, keepdims=True) * jnp.max(
        jnp.sum(land, axis=1, keepdims=True), axis=0, keepdims=True
    )
    row = lax.broadcasted_iota(jnp.int32, (64, 64), 0)
    eye = (row == lax.broadcasted_iota(jnp.int32, (64, 64), 1)).astype(F32)
    mul = lambda a, b: dot(a, b, ((1,), (0,)), HI)
    approx = across / most
    for _ in range(PINV_ITERS):
        prod = mul(land, approx)
        inner = 7.0 * eye - prod
        inner = 15.0 * eye - mul(prod, inner)
        inner = 13.0 * eye - mul(prod, inner)
        approx = 0.25 * mul(approx, inner)
    inverse[...] = approx


def spread(terms, out):
    for y in range(terms.shape[0] // 64):
        for x in range(4):
            out[y * 4 + x] = terms[y * 64 : y * 64 + 64, x * 512 : x * 512 + 512].astype(BF16)


def unmix(weights, tile, dest, lanes):
    for z in range(16):
        for c in range(2):
            for y in range(4):
                low = (z * 8 + y * 2 + c) * 16
                dest[low : low + 16, lanes] = weights[
                    z * 2 + c, y, tile * 16 : tile * 16 + 16, :
                ]


def unmix_body(weights, w1, w2, raw, sem):
    copy = pltpu.make_async_copy(weights.at[:, :, 16:160], raw, sem)
    copy.start()
    copy.wait()
    for t in range(6):
        unmix(raw, t, w1, slice(t * 128, t * 128 + 128))
    for t in range(3):
        unmix(raw, 6 + t, w2, slice(t * 128, t * 128 + 128))


def proj_body(near, inverse, gathered, weights, out, raw, wo, sem):
    copy = pltpu.make_async_copy(weights.at[:, :, 0:16], raw, sem)
    copy.start()
    mixer = dot(inverse[...], gathered[...], ((1,), (0,)), HI)
    attn = dot(near[...], mixer, ((1,), (0,)), HI).astype(BF16)
    copy.wait()
    unmix(raw, 0, wo, slice(0, 128))
    spread(dot(attn, wo[...], ((1,), (1,))), out)


def ffn_body(whole, gain, far1, far2, out, normed, w1, w2, sems):
    first_copy = pltpu.make_async_copy(far1, w1, sems.at[0])
    second_copy = pltpu.make_async_copy(far2, w2, sems.at[1])
    first_copy.start()
    second_copy.start()
    for y in range(2):
        blocks = [whole[y * 4 + x].astype(F32) for x in range(4)]
        square = sum(jnp.sum(b * b, axis=-1, keepdims=True) for b in blocks)
        factor = lax.rsqrt(square * (1.0 / 2048.0) + EPS)
        for x in range(4):
            lanes = slice(x * 512, x * 512 + 512)
            normed[y * 64 : y * 64 + 64, lanes] = (
                blocks[x] * factor * gain[:, lanes]
            ).astype(BF16)
    first_copy.wait()
    first = dot(normed[...], w1[...], ((1,), (0,)))
    gate, up = first[:, :384], first[:, 384:]
    hidden = (gate / (1.0 + jnp.exp(-gate)) * up).astype(BF16)
    second_copy.wait()
    spread(dot(hidden, w2[...], ((1,), (1,))), out)


def on_device(queries, keys, values, stream, seg_lengths, gain, w_out, w_gate, w_up, w_down):
    z, c = lax.axis_index("z"), lax.axis_index("c")
    y_axes = ("yh", "yl")
    pack = kernel_call(pack_body, shape((4, 352, 128), BF16), 7, grant=None)(
        queries, keys, values, w_gate, w_up, w_down.T, w_out.T
    )
    got = lax.all_to_all(pack, y_axes, 0, 0)
    weights = lax.all_gather(got[:, 192:352], ("z", "c"), axis=0)
    other = lax.ppermute(got, "c", [(0, 1), (1, 0)])
    ends = jnp.cumsum(seg_lengths) - z * 512
    mine = kernel_call(marks_body, shape((64, HEAD), F32), 4, core=c[None])(
        got, other, (ends - seg_lengths)[:, None], ends[:, None]
    )
    mine = jnp.sum(lax.all_gather(mine, "z", axis=0), axis=0)
    marks = lax.all_gather(mine / seg_lengths.astype(F32)[:, None], "c", axis=0)
    send = kernel_call(far_body, shape((16, 40, HEAD), F32), 3, core=c[None])(got, other, marks)
    parts = lax.all_to_all(send, "z", 0, 0)
    near, inverse = kernel_call(
        near_body,
        [shape((256, 64), F32), shape((64, 64), F32)],
        2,
        cost=pl.CostEstimate(flops=10**9, bytes_accessed=2 * 10**7, transcendentals=0),
    )(got, marks)
    gathered = kernel_call(merge_body, shape((32, HEAD), F32), 1)(parts)
    gathered = lax.all_gather(gathered, "c", axis=0, tiled=True)

    terms = kernel_call(
        proj_body,
        shape((16, 64, 512), BF16),
        3,
        [
            pltpu.VMEM((32, 4, 16, 128), BF16),
            pltpu.VMEM((2048, 128), BF16),
            pltpu.SemaphoreType.DMA(()),
        ],
        n_far=1,
        grant=LARGE,
    )(near, inverse, gathered, weights)
    parts = lax.all_to_all(terms, (*y_axes, "x"), 0, 0)
    w1, w2 = kernel_call(
        unmix_body,
        [shape((2048, 768), BF16), shape((2048, 384), BF16)],
        0,
        [pltpu.VMEM((32, 4, 144, 128), BF16), pltpu.SemaphoreType.DMA(())],
        n_far=1,
        grant=LARGE,
    )(weights)
    resid = (stream.astype(F32) + jnp.sum(parts.astype(F32), axis=0)).astype(BF16)
    whole = lax.all_to_all(jnp.broadcast_to(resid[None], (8, 64, 512)), ("yl", "x"), 0, 0)
    terms = kernel_call(
        ffn_body,
        shape((8, 64, 512), BF16),
        2,
        [
            pltpu.VMEM((128, 2048), BF16),
            pltpu.VMEM((2048, 768), BF16),
            pltpu.VMEM((2048, 384), BF16),
            pltpu.SemaphoreType.DMA((2,)),
        ],
        n_far=2,
        grant=LARGE,
    )(whole, gain[None, :], w1, w2)
    parts = lax.all_to_all(terms, ("yl", "x"), 0, 0)
    return (resid.astype(F32) + jnp.sum(parts.astype(F32), axis=0)).astype(BF16)


def solution(mesh):
    fine = Mesh(mesh.devices.reshape(16, 2, 2, 2, 4), ("z", "yh", "yl", "c", "x"))
    seq = ("z", "yh", "yl", "c")
    return jax.shard_map(
        on_device,
        mesh=fine,
        in_specs=(
            P(seq, "x"),
            P(seq, "x"),
            P(seq, "x"),
            P(seq, "x"),
            P(),
            P(),
            P("x", seq),
            P(seq, "x"),
            P(seq, "x"),
            P("x", seq),
        ),
        out_specs=P(seq, "x"),
        check_vma=False,
    )
```

```python
import math

import jax
import jax.numpy as jnp
from jax import lax
from jax.experimental import pallas as pl
from jax.experimental.pallas import tpu as pltpu
from jax.sharding import Mesh
from jax.sharding import PartitionSpec as P

PINV_ITERS = 6
HEAD = 128
EPS = 1e-05
SCALE = 1.0 / math.sqrt(HEAD)
HI = lax.Precision.HIGHEST
F32 = jnp.float32
BF16 = jnp.bfloat16
SMALL = 24 << 20
LARGE = 60 << 20


def dot(a, b, dims, precision=None):
    return lax.dot_general(
        a, b, (dims, ((), ())), precision=precision, preferred_element_type=F32
    )


def kernel_call(body, out_shape, n_in, scratch=(), cost=None, core=None, grant=SMALL, n_far=0):
    whole = pl.BlockSpec(memory_space=pltpu.VMEM)
    many = isinstance(out_shape, (list, tuple))
    call = pl.pallas_call(
        body,
        out_shape=out_shape,
        in_specs=([] if core is None else [pl.BlockSpec(memory_space=pltpu.SMEM)])
        + [whole] * n_in
        + [pl.BlockSpec(memory_space=pltpu.HBM)] * n_far,
        out_specs=[whole] * len(out_shape) if many else whole,
        scratch_shapes=list(scratch),
        cost_estimate=cost,
        compiler_params=pltpu.CompilerParams(vmem_limit_bytes=grant),
    )
    return call if core is None else lambda *args: call(core, *args)


def shape(dims, dtype):
    return jax.ShapeDtypeStruct(dims, dtype)


def pack_body(q, k, v, wg, wu, wd, wo, out):
    for y in range(4):
        tile = slice(y * 128, y * 128 + 128)
        out[y, 0:64] = q[:, tile]
        out[y, 64:128] = k[:, tile]
        out[y, 128:192] = v[:, tile]
        for t in range(4):
            out[y, 192 + t * 16 : 208 + t * 16] = wo[:, t * 128 : t * 128 + 128]
        for t in range(3):
            low = ((y % 2) * 3 + t) * 128
            for i, w in enumerate((wg, wu, wd)):
                at = 256 + (3 * i + t) * 16
                out[y, at : at + 16] = w[:, low : low + 128]


def marks_body(core, mine, other, starts, ends, out):
    c = core[0]
    low = pl.multiple_of(c * 64, 64)
    total = None
    for got, place in ((mine, c), (other, 1 - c)):
        at = lax.broadcasted_iota(jnp.int32, (64, 256), 1)
        at = at + (at // 64) * 64 + place * 64
        member = ((at >= starts[...]) & (at < ends[...])).astype(BF16)
        part = dot(member, got[:, pl.ds(low, 64), :].reshape(256, HEAD), ((1,), (0,)))
        total = part if total is None else total + part
    out[...] = total


def far_body(core, mine, other, marks, out):
    query = marks[0, pl.ds(core[0] * 32, 32), :]
    far = [
        dot(query, got[:, 64:128].reshape(256, HEAD).astype(F32), ((1,), (1,)), HI) * SCALE
        for got in (mine, other)
    ]
    peak = jnp.maximum(*(jnp.max(f, axis=-1, keepdims=True) for f in far))
    far = [jnp.exp(f - peak) for f in far]
    mass = sum(jnp.sum(f, axis=-1, keepdims=True) for f in far)
    part = sum(
        dot(f, got[:, 128:192].reshape(256, HEAD).astype(F32), ((1,), (0,)), HI)
        for f, got in zip(far, (mine, other))
    )
    row = lax.broadcasted_iota(jnp.int32, (32, HEAD), 0)
    lane = lax.broadcasted_iota(jnp.int32, (32, HEAD), 1)
    stats = jnp.where(lane == row, peak, 0.0) + jnp.where(lane == row + 32, mass, 0.0)
    stats = jnp.broadcast_to(jnp.sum(stats, axis=0, keepdims=True), (8, HEAD))
    for z in range(16):
        out[z, 0:32] = part
        out[z, 32:40] = stats


def merge_body(parts, out):
    row = lax.broadcasted_iota(jnp.int32, (16, 32, HEAD), 1)
    lane = lax.broadcasted_iota(jnp.int32, (16, 32, HEAD), 2)
    stats = jnp.broadcast_to(parts[:, 32:33, :], (16, 32, HEAD))
    peak = jnp.sum(jnp.where(lane == row, stats, 0.0), axis=-1, keepdims=True)
    mass = jnp.sum(jnp.where(lane == row + 32, stats, 0.0), axis=-1, keepdims=True)
    factor = jnp.exp(peak - jnp.max(peak, axis=0, keepdims=True))
    total = jnp.sum(factor * mass, axis=0)
    out[...] = jnp.sum(factor * parts[:, 0:32, :], axis=0) / total


def softmax(scores, axis):
    scores = jnp.exp(scores - jnp.max(scores, axis=axis, keepdims=True))
    return scores / jnp.sum(scores, axis=axis, keepdims=True)


def inverse_body(marks, out):
    qm, km = marks[0], marks[1]
    out[0] = km
    land = softmax(dot(qm, km, ((1,), (1,)), HI) * SCALE, 1)
    across = softmax(dot(km, qm, ((1,), (1,)), HI) * SCALE, 0)
    most = jnp.max(jnp.sum(land, axis=0, keepdims=True), axis=1, keepdims=True) * jnp.max(
        jnp.sum(land, axis=1, keepdims=True), axis=0, keepdims=True
    )
    row = lax.broadcasted_iota(jnp.int32, (64, 64), 0)
    eye = (row == lax.broadcasted_iota(jnp.int32, (64, 64), 1)).astype(F32)
    mul = lambda a, b: dot(a, b, ((1,), (0,)), HI)
    approx = across / most
    for _ in range(PINV_ITERS):
        prod = mul(land, approx)
        inner = 7.0 * eye - prod
        inner = 15.0 * eye - mul(prod, inner)
        inner = 13.0 * eye - mul(prod, inner)
        approx = 0.25 * mul(approx, inner)
    out[1] = jnp.concatenate([approx, jnp.zeros_like(approx)], axis=-1)


def near_body(queries, heads, out):
    for h in range(4):
        query = queries[:, h * HEAD : h * HEAD + HEAD].astype(F32)
        near = softmax(dot(query, heads[h, 0], ((1,), (1,)), HI) * SCALE, -1)
        out[h] = jnp.concatenate([near, jnp.zeros_like(near)], axis=-1)


def spread(terms, out):
    for y in range(terms.shape[0] // 64):
        for x in range(4):
            out[y * 4 + x] = terms[y * 64 : y * 64 + 64, x * 512 : x * 512 + 512].astype(BF16)


def unmix(blocks, tile, dest, lanes, c):
    for z in range(16):
        for y in range(4):
            low = pl.multiple_of((z * 8 + y * 2 + c) * 16, 16)
            dest[pl.ds(low, 16), lanes] = blocks[z, y, tile * 16 : tile * 16 + 16, :]


def unmix_body(core, mine, other, w1, w2, raw, sems):
    copies = [
        pltpu.make_async_copy(far.at[:, :, 64:208], raw.at[i], sems.at[i])
        for i, far in enumerate((mine, other))
    ]
    for copy in copies:
        copy.start()
    for i, c in enumerate((core[0], 1 - core[0])):
        copies[i].wait()
        for t in range(6):
            unmix(raw.at[i], t, w1, slice(t * 128, t * 128 + 128), c)
        for t in range(3):
            unmix(raw.at[i], 6 + t, w2, slice(t * 128, t * 128 + 128), c)


def proj_body(core, near, heads, gathered, mine, other, out, raw, wo, sems):
    copies = [
        pltpu.make_async_copy(far.at[:, :, 0:64], raw.at[i], sems.at[i])
        for i, far in enumerate((mine, other))
    ]
    for copy in copies:
        copy.start()
    attn = []
    for h in range(4):
        mixer = dot(heads[h, 1][:, :64], gathered[h], ((1,), (0,)), HI)
        attn.append(dot(near[h][:, :64], mixer, ((1,), (0,)), HI).astype(BF16))
    attn = jnp.concatenate(attn, axis=-1)
    for i, c in enumerate((core[0], 1 - core[0])):
        copies[i].wait()
        for t in range(4):
            unmix(raw.at[i], t, wo, slice(t * 128, t * 128 + 128), c)
    spread(dot(attn, wo[...], ((1,), (1,))), out)


def ffn_body(whole, gain, far1, far2, out, normed, w1, w2, sems):
    first_copy = pltpu.make_async_copy(far1, w1, sems.at[0])
    second_copy = pltpu.make_async_copy(far2, w2, sems.at[1])
    first_copy.start()
    second_copy.start()
    for y in range(2):
        blocks = [whole[y * 4 + x].astype(F32) for x in range(4)]
        square = sum(jnp.sum(b * b, axis=-1, keepdims=True) for b in blocks)
        factor = lax.rsqrt(square * (1.0 / 2048.0) + EPS)
        for x in range(4):
            lanes = slice(x * 512, x * 512 + 512)
            normed[y * 64 : y * 64 + 64, lanes] = (
                blocks[x] * factor * gain[:, lanes]
            ).astype(BF16)
    first_copy.wait()
    first = dot(normed[...], w1[...], ((1,), (0,)))
    gate, up = first[:, :384], first[:, 384:]
    hidden = (gate / (1.0 + jnp.exp(-gate)) * up).astype(BF16)
    second_copy.wait()
    spread(dot(hidden, w2[...], ((1,), (1,))), out)


def on_device(queries, keys, values, stream, seg_lengths, gain, w_out, w_gate, w_up, w_down):
    z, c = lax.axis_index("z"), lax.axis_index("c")
    y_axes = ("yh", "yl")
    pack = kernel_call(pack_body, shape((4, 400, 128), BF16), 7, grant=None)(
        queries, keys, values, w_gate, w_up, w_down.T, w_out.T
    )
    got = lax.all_to_all(pack, y_axes, 0, 0)
    weights = lax.all_gather(got[:, 192:400], "z", axis=0)
    other = lax.ppermute(got, "c", [(0, 1), (1, 0)])
    ends = jnp.cumsum(seg_lengths) - z * 512
    mine = kernel_call(marks_body, shape((64, HEAD), F32), 4, core=c[None])(
        got, other, (ends - seg_lengths)[:, None], ends[:, None]
    )
    mine = jnp.sum(lax.all_gather(mine, "z", axis=0), axis=0)
    marks = lax.all_gather(mine / seg_lengths.astype(F32)[:, None], "c", axis=0)
    send = kernel_call(far_body, shape((16, 40, HEAD), F32), 3, core=c[None])(got, other, marks)
    parts = lax.all_to_all(send, "z", 0, 0)
    heads = kernel_call(
        inverse_body,
        shape((2, 64, HEAD), F32),
        1,
        cost=pl.CostEstimate(flops=10**9, bytes_accessed=2 * 10**7, transcendentals=0),
    )(marks)
    heads = lax.all_gather(heads, y_axes, axis=0)
    near = kernel_call(near_body, shape((4, 64, HEAD), F32), 2)(queries, heads)
    parts, near, heads = lax.optimization_barrier((parts, near, heads))
    gathered = kernel_call(merge_body, shape((32, HEAD), F32), 1)(parts)
    gathered = lax.all_gather(gathered, "c", axis=0, tiled=True)
    gathered, weights = lax.optimization_barrier((gathered, weights))
    swapped = lax.ppermute(weights, "c", [(0, 1), (1, 0)])
    gathered = lax.all_gather(gathered, y_axes, axis=0)
    terms = kernel_call(
        proj_body,
        shape((4, 64, 512), BF16),
        3,
        [
            pltpu.VMEM((2, 16, 4, 64, 128), BF16),
            pltpu.VMEM((2048, 512), BF16),
            pltpu.SemaphoreType.DMA((2,)),
        ],
        core=c[None],
        n_far=2,
        grant=LARGE,
    )(near, heads, gathered, weights, swapped)
    parts = lax.all_to_all(terms, "x", 0, 0)
    w1, w2 = kernel_call(
        unmix_body,
        [shape((2048, 768), BF16), shape((2048, 384), BF16)],
        0,
        [pltpu.VMEM((2, 16, 4, 144, 128), BF16), pltpu.SemaphoreType.DMA((2,))],
        core=c[None],
        n_far=2,
        grant=LARGE,
    )(weights, swapped)
    resid = (stream.astype(F32) + jnp.sum(parts.astype(F32), axis=0)).astype(BF16)
    whole = lax.all_to_all(jnp.broadcast_to(resid[None], (8, 64, 512)), ("yl", "x"), 0, 0)
    terms = kernel_call(
        ffn_body,
        shape((8, 64, 512), BF16),
        2,
        [
            pltpu.VMEM((128, 2048), BF16),
            pltpu.VMEM((2048, 768), BF16),
            pltpu.VMEM((2048, 384), BF16),
            pltpu.SemaphoreType.DMA((2,)),
        ],
        n_far=2,
        grant=LARGE,
    )(whole, gain[None, :], w1, w2)
    parts = lax.all_to_all(terms, ("yl", "x"), 0, 0)
    return (resid.astype(F32) + jnp.sum(parts.astype(F32), axis=0)).astype(BF16)


def solution(mesh):
    fine = Mesh(mesh.devices.reshape(16, 2, 2, 2, 4), ("z", "yh", "yl", "c", "x"))
    seq = ("z", "yh", "yl", "c")
    return jax.shard_map(
        on_device,
        mesh=fine,
        in_specs=(
            P(seq, "x"),
            P(seq, "x"),
            P(seq, "x"),
            P(seq, "x"),
            P(),
            P(),
            P("x", seq),
            P(seq, "x"),
            P(seq, "x"),
            P("x", seq),
        ),
        out_specs=P(seq, "x"),
        check_vma=False,
    )
```

```python
import math

import jax
import jax.numpy as jnp
from jax import lax
from jax.experimental import pallas as pl
from jax.experimental.pallas import tpu as pltpu
from jax.sharding import Mesh
from jax.sharding import PartitionSpec as P

PINV_ITERS = 6
HEAD = 128
EPS = 1e-05
SCALE = 1.0 / math.sqrt(HEAD)
HI = lax.Precision.HIGHEST
F32 = jnp.float32
BF16 = jnp.bfloat16
SMALL = 24 << 20
LARGE = 60 << 20


def dot(a, b, dims, precision=None):
    return lax.dot_general(
        a, b, (dims, ((), ())), precision=precision, preferred_element_type=F32
    )


def kernel_call(body, out_shape, n_in, scratch=(), cost=None, core=None, grant=SMALL, n_far=0):
    whole = pl.BlockSpec(memory_space=pltpu.VMEM)
    many = isinstance(out_shape, (list, tuple))
    call = pl.pallas_call(
        body,
        out_shape=out_shape,
        in_specs=([] if core is None else [pl.BlockSpec(memory_space=pltpu.SMEM)])
        + [whole] * n_in
        + [pl.BlockSpec(memory_space=pltpu.HBM)] * n_far,
        out_specs=[whole] * len(out_shape) if many else whole,
        scratch_shapes=list(scratch),
        cost_estimate=cost,
        compiler_params=pltpu.CompilerParams(vmem_limit_bytes=grant),
    )
    return call if core is None else lambda *args: call(core, *args)


def shape(dims, dtype):
    return jax.ShapeDtypeStruct(dims, dtype)


def pack_body(q, k, v, wg, wu, wd, wo, out):
    for y in range(4):
        tile = slice(y * 128, y * 128 + 128)
        out[y, 0:64] = q[:, tile]
        out[y, 64:128] = k[:, tile]
        out[y, 128:192] = v[:, tile]
        for t in range(4):
            out[y, 192 + t * 16 : 208 + t * 16] = wo[:, t * 128 : t * 128 + 128]
        for t in range(3):
            low = ((y % 2) * 3 + t) * 128
            for i, w in enumerate((wg, wu, wd)):
                at = 256 + (3 * i + t) * 16
                out[y, at : at + 16] = w[:, low : low + 128]


def marks_body(core, mine, other, starts, ends, out):
    c = core[0]
    low = pl.multiple_of(c * 64, 64)
    total = None
    for got, place in ((mine, c), (other, 1 - c)):
        at = lax.broadcasted_iota(jnp.int32, (64, 256), 1)
        at = at + (at // 64) * 64 + place * 64
        member = ((at >= starts[...]) & (at < ends[...])).astype(BF16)
        part = dot(member, got[:, pl.ds(low, 64), :].reshape(256, HEAD), ((1,), (0,)))
        total = part if total is None else total + part
    out[...] = total


def far_body(core, mine, other, marks, out):
    query = marks[0, pl.ds(core[0] * 32, 32), :]
    far = [
        dot(query, got[:, 64:128].reshape(256, HEAD).astype(F32), ((1,), (1,)), HI) * SCALE
        for got in (mine, other)
    ]
    peak = jnp.maximum(*(jnp.max(f, axis=-1, keepdims=True) for f in far))
    far = [jnp.exp(f - peak) for f in far]
    mass = sum(jnp.sum(f, axis=-1, keepdims=True) for f in far)
    part = sum(
        dot(f, got[:, 128:192].reshape(256, HEAD).astype(F32), ((1,), (0,)), HI)
        for f, got in zip(far, (mine, other))
    )
    row = lax.broadcasted_iota(jnp.int32, (32, HEAD), 0)
    lane = lax.broadcasted_iota(jnp.int32, (32, HEAD), 1)
    stats = jnp.where(lane == row, peak, 0.0) + jnp.where(lane == row + 32, mass, 0.0)
    stats = jnp.broadcast_to(jnp.sum(stats, axis=0, keepdims=True), (8, HEAD))
    for z in range(16):
        out[z, 0:32] = part
        out[z, 32:40] = stats


def merge_body(parts, out):
    row = lax.broadcasted_iota(jnp.int32, (16, 32, HEAD), 1)
    lane = lax.broadcasted_iota(jnp.int32, (16, 32, HEAD), 2)
    stats = jnp.broadcast_to(parts[:, 32:33, :], (16, 32, HEAD))
    peak = jnp.sum(jnp.where(lane == row, stats, 0.0), axis=-1, keepdims=True)
    mass = jnp.sum(jnp.where(lane == row + 32, stats, 0.0), axis=-1, keepdims=True)
    factor = jnp.exp(peak - jnp.max(peak, axis=0, keepdims=True))
    total = jnp.sum(factor * mass, axis=0)
    rows = jnp.sum(factor * parts[:, 0:32, :], axis=0) / total
    for i in range(8):
        out[i] = rows


def softmax(scores, axis):
    scores = jnp.exp(scores - jnp.max(scores, axis=axis, keepdims=True))
    return scores / jnp.sum(scores, axis=axis, keepdims=True)


def inverse_body(marks, out):
    qm, km = marks[0], marks[1]
    out[0] = km
    land = softmax(dot(qm, km, ((1,), (1,)), HI) * SCALE, 1)
    across = softmax(dot(km, qm, ((1,), (1,)), HI) * SCALE, 0)
    most = jnp.max(jnp.sum(land, axis=0, keepdims=True), axis=1, keepdims=True) * jnp.max(
        jnp.sum(land, axis=1, keepdims=True), axis=0, keepdims=True
    )
    row = lax.broadcasted_iota(jnp.int32, (64, 64), 0)
    eye = (row == lax.broadcasted_iota(jnp.int32, (64, 64), 1)).astype(F32)
    mul = lambda a, b: dot(a, b, ((1,), (0,)), HI)
    approx = across / most
    for _ in range(PINV_ITERS):
        prod = mul(land, approx)
        inner = 7.0 * eye - prod
        inner = 15.0 * eye - mul(prod, inner)
        inner = 13.0 * eye - mul(prod, inner)
        approx = 0.25 * mul(approx, inner)
    out[1] = jnp.concatenate([approx, jnp.zeros_like(approx)], axis=-1)


def near_body(queries, heads, out):
    for h in range(4):
        query = queries[:, h * HEAD : h * HEAD + HEAD].astype(F32)
        near = softmax(dot(query, heads[h, 0], ((1,), (1,)), HI) * SCALE, -1)
        out[h] = jnp.concatenate([near, jnp.zeros_like(near)], axis=-1)


def spread(terms, out):
    for y in range(terms.shape[0] // 64):
        for x in range(4):
            out[y * 4 + x] = terms[y * 64 : y * 64 + 64, x * 512 : x * 512 + 512].astype(BF16)


def unmix(blocks, tile, dest, lanes, c):
    for z in range(16):
        for y in range(4):
            low = pl.multiple_of((z * 8 + y * 2 + c) * 16, 16)
            dest[pl.ds(low, 16), lanes] = blocks[z, y, tile * 16 : tile * 16 + 16, :]


def unmix_body(core, mine, other, w1, w2, raw, sems):
    copies = [
        pltpu.make_async_copy(far.at[:, :, 64:208], raw.at[i], sems.at[i])
        for i, far in enumerate((mine, other))
    ]
    for copy in copies:
        copy.start()
    for i, c in enumerate((core[0], 1 - core[0])):
        copies[i].wait()
        for t in range(6):
            unmix(raw.at[i], t, w1, slice(t * 128, t * 128 + 128), c)
        for t in range(3):
            unmix(raw.at[i], 6 + t, w2, slice(t * 128, t * 128 + 128), c)


def proj_body(core, near, heads, gathered, mine, other, out, wo):
    for t in range(4):
        lanes = slice(t * 128, t * 128 + 128)
        unmix(mine, t, wo, lanes, core[0])
        unmix(other, t, wo, lanes, 1 - core[0])
    attn = []
    for h in range(4):
        rows = jnp.concatenate([gathered[2 * h], gathered[2 * h + 1]], axis=0)
        mixer = dot(heads[h, 1][:, :64], rows, ((1,), (0,)), HI)
        attn.append(dot(near[h][:, :64], mixer, ((1,), (0,)), HI).astype(BF16))
    attn = jnp.concatenate(attn, axis=-1)
    spread(dot(attn, wo[...], ((1,), (1,))), out)


def ffn_body(whole, gain, far1, far2, out, normed, w1, w2, sems):
    first_copy = pltpu.make_async_copy(far1, w1, sems.at[0])
    second_copy = pltpu.make_async_copy(far2, w2, sems.at[1])
    first_copy.start()
    second_copy.start()
    for y in range(2):
        blocks = [whole[y * 4 + x].astype(F32) for x in range(4)]
        square = sum(jnp.sum(b * b, axis=-1, keepdims=True) for b in blocks)
        factor = lax.rsqrt(square * (1.0 / 2048.0) + EPS)
        for x in range(4):
            lanes = slice(x * 512, x * 512 + 512)
            normed[y * 64 : y * 64 + 64, lanes] = (
                blocks[x] * factor * gain[:, lanes]
            ).astype(BF16)
    first_copy.wait()
    first = dot(normed[...], w1[...], ((1,), (0,)))
    gate, up = first[:, :384], first[:, 384:]
    hidden = (gate / (1.0 + jnp.exp(-gate)) * up).astype(BF16)
    second_copy.wait()
    spread(dot(hidden, w2[...], ((1,), (1,))), out)


def on_device(queries, keys, values, stream, seg_lengths, gain, w_out, w_gate, w_up, w_down):
    z, c = lax.axis_index("z"), lax.axis_index("c")
    y_axes = ("yh", "yl")
    pack = kernel_call(pack_body, shape((4, 400, 128), BF16), 7, grant=None)(
        queries, keys, values, w_gate, w_up, w_down.T, w_out.T
    )
    got = lax.all_to_all(pack, y_axes, 0, 0)
    weights = lax.all_gather(got[:, 192:400], "z", axis=0)
    other = lax.ppermute(got, "c", [(0, 1), (1, 0)])
    ends = jnp.cumsum(seg_lengths) - z * 512
    mine = kernel_call(marks_body, shape((64, HEAD), F32), 4, core=c[None])(
        got, other, (ends - seg_lengths)[:, None], ends[:, None]
    )
    mine = jnp.sum(lax.all_gather(mine, "z", axis=0), axis=0)
    marks = lax.all_gather(mine / seg_lengths.astype(F32)[:, None], "c", axis=0)
    send = kernel_call(far_body, shape((16, 40, HEAD), F32), 3, core=c[None])(got, other, marks)
    parts = lax.all_to_all(send, "z", 0, 0)
    heads = kernel_call(
        inverse_body,
        shape((2, 64, HEAD), F32),
        1,
        cost=pl.CostEstimate(flops=10**9, bytes_accessed=2 * 10**7, transcendentals=0),
    )(marks)
    heads = lax.all_gather(heads, y_axes, axis=0)
    near = kernel_call(near_body, shape((4, 64, HEAD), F32), 2)(queries, heads)
    parts, near, heads = lax.optimization_barrier((parts, near, heads))
    gathered = kernel_call(merge_body, shape((8, 32, HEAD), F32), 1)(parts)
    gathered = lax.all_to_all(gathered, (*y_axes, "c"), 0, 0)
    weights, gathered = lax.optimization_barrier((weights, gathered))
    w_out = weights[:, :, 0:64]
    swapped = lax.ppermute(w_out, "c", [(0, 1), (1, 0)])
    terms = kernel_call(
        proj_body,
        shape((4, 64, 512), BF16),
        5,
        [pltpu.VMEM((2048, 512), BF16)],
        core=c[None],
    )(near, heads, gathered, w_out, swapped)
    terms, weights = lax.optimization_barrier((terms, weights))
    swapped = lax.ppermute(weights, "c", [(0, 1), (1, 0)])
    parts = lax.all_to_all(terms, "x", 0, 0)
    w1, w2 = kernel_call(
        unmix_body,
        [shape((2048, 768), BF16), shape((2048, 384), BF16)],
        0,
        [pltpu.VMEM((2, 16, 4, 144, 128), BF16), pltpu.SemaphoreType.DMA((2,))],
        core=c[None],
        n_far=2,
        grant=LARGE,
    )(weights, swapped)
    resid = (stream.astype(F32) + jnp.sum(parts.astype(F32), axis=0)).astype(BF16)
    whole = lax.all_to_all(jnp.broadcast_to(resid[None], (8, 64, 512)), ("yl", "x"), 0, 0)
    terms = kernel_call(
        ffn_body,
        shape((8, 64, 512), BF16),
        2,
        [
            pltpu.VMEM((128, 2048), BF16),
            pltpu.VMEM((2048, 768), BF16),
            pltpu.VMEM((2048, 384), BF16),
            pltpu.SemaphoreType.DMA((2,)),
        ],
        n_far=2,
        grant=LARGE,
    )(whole, gain[None, :], w1, w2)
    parts = lax.all_to_all(terms, ("yl", "x"), 0, 0)
    return (resid.astype(F32) + jnp.sum(parts.astype(F32), axis=0)).astype(BF16)


def solution(mesh):
    fine = Mesh(mesh.devices.reshape(16, 2, 2, 2, 4), ("z", "yh", "yl", "c", "x"))
    seq = ("z", "yh", "yl", "c")
    return jax.shard_map(
        on_device,
        mesh=fine,
        in_specs=(
            P(seq, "x"),
            P(seq, "x"),
            P(seq, "x"),
            P(seq, "x"),
            P(),
            P(),
            P("x", seq),
            P(seq, "x"),
            P(seq, "x"),
            P("x", seq),
        ),
        out_specs=P(seq, "x"),
        check_vma=False,
    )
```

```python
import math

import jax
import jax.numpy as jnp
from jax import lax
from jax.experimental import pallas as pl
from jax.experimental.pallas import tpu as pltpu
from jax.sharding import Mesh
from jax.sharding import PartitionSpec as P

PINV_ITERS = 6
HEAD = 128
EPS = 1e-05
SCALE = 1.0 / math.sqrt(HEAD)
HI = lax.Precision.HIGHEST
F32 = jnp.float32
BF16 = jnp.bfloat16
SMALL = 24 << 20
LARGE = 60 << 20


def dot(a, b, dims, precision=None):
    return lax.dot_general(
        a, b, (dims, ((), ())), precision=precision, preferred_element_type=F32
    )


def kernel_call(body, out_shape, n_in, scratch=(), cost=None, core=None, grant=SMALL, n_far=0):
    whole = pl.BlockSpec(memory_space=pltpu.VMEM)
    many = isinstance(out_shape, (list, tuple))
    call = pl.pallas_call(
        body,
        out_shape=out_shape,
        in_specs=([] if core is None else [pl.BlockSpec(memory_space=pltpu.SMEM)])
        + [whole] * n_in
        + [pl.BlockSpec(memory_space=pltpu.HBM)] * n_far,
        out_specs=[whole] * len(out_shape) if many else whole,
        scratch_shapes=list(scratch),
        cost_estimate=cost,
        compiler_params=pltpu.CompilerParams(vmem_limit_bytes=grant),
    )
    return call if core is None else lambda *args: call(core, *args)


def shape(dims, dtype):
    return jax.ShapeDtypeStruct(dims, dtype)


def pack_body(q, k, v, wg, wu, wd, wo, out):
    for y in range(4):
        tile = slice(y * 128, y * 128 + 128)
        out[y, 0:64] = q[:, tile]
        out[y, 64:128] = k[:, tile]
        out[y, 128:192] = v[:, tile]
        for t in range(4):
            out[y, 192 + t * 16 : 208 + t * 16] = wo[:, t * 128 : t * 128 + 128]
        for t in range(3):
            low = ((y % 2) * 3 + t) * 128
            for i, w in enumerate((wg, wu, wd)):
                at = 256 + (3 * i + t) * 16
                out[y, at : at + 16] = w[:, low : low + 128]


def marks_body(place, mine, other, lengths, out):
    c = place[0]
    row = lax.broadcasted_iota(jnp.int32, (64, 64), 0)
    lane = lax.broadcasted_iota(jnp.int32, (64, 64), 1)
    sizes = jnp.broadcast_to(lengths[...], (64, 64)).astype(F32)
    starts = jnp.sum(jnp.where(lane < row, sizes, 0.0), axis=1, keepdims=True)
    ends = jnp.sum(jnp.where(lane <= row, sizes, 0.0), axis=1, keepdims=True)
    starts, ends = (e.astype(jnp.int32) - place[1] * 512 for e in (starts, ends))
    low = pl.multiple_of(c * 64, 64)
    total = None
    for got, at_core in ((mine, c), (other, 1 - c)):
        at = lax.broadcasted_iota(jnp.int32, (64, 256), 1)
        at = at + (at // 64) * 64 + at_core * 64
        member = ((at >= starts) & (at < ends)).astype(BF16)
        part = dot(member, got[:, pl.ds(low, 64), :].reshape(256, HEAD), ((1,), (0,)))
        total = part if total is None else total + part
    out[...] = total


def far_body(core, mine, other, marks, out):
    query = marks[0, pl.ds(core[0] * 32, 32), :]
    far = [
        dot(query, got[:, 64:128].reshape(256, HEAD).astype(F32), ((1,), (1,)), HI) * SCALE
        for got in (mine, other)
    ]
    peak = jnp.maximum(*(jnp.max(f, axis=-1, keepdims=True) for f in far))
    far = [jnp.exp(f - peak) for f in far]
    mass = sum(jnp.sum(f, axis=-1, keepdims=True) for f in far)
    part = sum(
        dot(f, got[:, 128:192].reshape(256, HEAD).astype(F32), ((1,), (0,)), HI)
        for f, got in zip(far, (mine, other))
    )
    row = lax.broadcasted_iota(jnp.int32, (32, HEAD), 0)
    lane = lax.broadcasted_iota(jnp.int32, (32, HEAD), 1)
    stats = jnp.where(lane == row, peak, 0.0) + jnp.where(lane == row + 32, mass, 0.0)
    stats = jnp.broadcast_to(jnp.sum(stats, axis=0, keepdims=True), (8, HEAD))
    for z in range(16):
        out[z, 0:32] = part
        out[z, 32:40] = stats


def merge_body(parts, out):
    row = lax.broadcasted_iota(jnp.int32, (16, 32, HEAD), 1)
    lane = lax.broadcasted_iota(jnp.int32, (16, 32, HEAD), 2)
    stats = jnp.broadcast_to(parts[:, 32:33, :], (16, 32, HEAD))
    peak = jnp.sum(jnp.where(lane == row, stats, 0.0), axis=-1, keepdims=True)
    mass = jnp.sum(jnp.where(lane == row + 32, stats, 0.0), axis=-1, keepdims=True)
    factor = jnp.exp(peak - jnp.max(peak, axis=0, keepdims=True))
    total = jnp.sum(factor * mass, axis=0)
    rows = jnp.sum(factor * parts[:, 0:32, :], axis=0) / total
    for i in range(8):
        out[i] = rows


def softmax(scores, axis):
    scores = jnp.exp(scores - jnp.max(scores, axis=axis, keepdims=True))
    return scores / jnp.sum(scores, axis=axis, keepdims=True)


def inverse_body(marks, out):
    qm, km = marks[0], marks[1]
    out[0] = km
    land = softmax(dot(qm, km, ((1,), (1,)), HI) * SCALE, 1)
    across = softmax(dot(km, qm, ((1,), (1,)), HI) * SCALE, 0)
    most = jnp.max(jnp.sum(land, axis=0, keepdims=True), axis=1, keepdims=True) * jnp.max(
        jnp.sum(land, axis=1, keepdims=True), axis=0, keepdims=True
    )
    row = lax.broadcasted_iota(jnp.int32, (64, 64), 0)
    eye = (row == lax.broadcasted_iota(jnp.int32, (64, 64), 1)).astype(F32)
    mul = lambda a, b: dot(a, b, ((1,), (0,)), HI)
    approx = across / most
    for _ in range(PINV_ITERS):
        prod = mul(land, approx)
        inner = 7.0 * eye - prod
        inner = 15.0 * eye - mul(prod, inner)
        inner = 13.0 * eye - mul(prod, inner)
        approx = 0.25 * mul(approx, inner)
    out[1] = jnp.concatenate([approx, jnp.zeros_like(approx)], axis=-1)


def near_body(queries, heads, out):
    for h in range(4):
        query = queries[:, h * HEAD : h * HEAD + HEAD].astype(F32)
        near = softmax(dot(query, heads[h, 0], ((1,), (1,)), HI) * SCALE, -1)
        out[h] = jnp.concatenate([near, jnp.zeros_like(near)], axis=-1)


def spread(terms, out):
    for y in range(terms.shape[0] // 64):
        for x in range(4):
            out[y * 4 + x] = terms[y * 64 : y * 64 + 64, x * 512 : x * 512 + 512].astype(BF16)


def unmix(blocks, tile, dest, lanes, c):
    for z in range(16):
        for y in range(4):
            low = pl.multiple_of((z * 8 + y * 2 + c) * 16, 16)
            dest[pl.ds(low, 16), lanes] = blocks[z, y, tile * 16 : tile * 16 + 16, :]


def unmix_body(core, mine, other, w1, w2, raw, sems):
    copies = [
        pltpu.make_async_copy(far.at[:, :, 64:208], raw.at[i], sems.at[i])
        for i, far in enumerate((mine, other))
    ]
    for copy in copies:
        copy.start()
    for i, c in enumerate((core[0], 1 - core[0])):
        copies[i].wait()
        for t in range(6):
            unmix(raw.at[i], t, w1, slice(t * 128, t * 128 + 128), c)
        for t in range(3):
            unmix(raw.at[i], 6 + t, w2, slice(t * 128, t * 128 + 128), c)


def proj_body(core, near, heads, gathered, mine, other, out, wo):
    for t in range(4):
        lanes = slice(t * 128, t * 128 + 128)
        unmix(mine, t, wo, lanes, core[0])
        unmix(other, t, wo, lanes, 1 - core[0])
    attn = []
    for h in range(4):
        rows = jnp.concatenate([gathered[2 * h], gathered[2 * h + 1]], axis=0)
        mixer = dot(heads[h, 1][:, :64], rows, ((1,), (0,)), HI)
        attn.append(dot(near[h][:, :64], mixer, ((1,), (0,)), HI).astype(BF16))
    attn = jnp.concatenate(attn, axis=-1)
    spread(dot(attn, wo[...], ((1,), (1,))), out)


def ffn_body(whole, gain, far1, far2, out, normed, w1, w2, sems):
    first_copy = pltpu.make_async_copy(far1, w1, sems.at[0])
    second_copy = pltpu.make_async_copy(far2, w2, sems.at[1])
    first_copy.start()
    second_copy.start()
    for y in range(2):
        blocks = [whole[y * 4 + x].astype(F32) for x in range(4)]
        square = sum(jnp.sum(b * b, axis=-1, keepdims=True) for b in blocks)
        factor = lax.rsqrt(square * (1.0 / 2048.0) + EPS)
        for x in range(4):
            lanes = slice(x * 512, x * 512 + 512)
            normed[y * 64 : y * 64 + 64, lanes] = (
                blocks[x] * factor * gain[:, lanes]
            ).astype(BF16)
    first_copy.wait()
    first = dot(normed[...], w1[...], ((1,), (0,)))
    gate, up = first[:, :384], first[:, 384:]
    hidden = (gate / (1.0 + jnp.exp(-gate)) * up).astype(BF16)
    second_copy.wait()
    spread(dot(hidden, w2[...], ((1,), (1,))), out)


def on_device(queries, keys, values, stream, seg_lengths, gain, w_out, w_gate, w_up, w_down):
    z, c = lax.axis_index("z"), lax.axis_index("c")
    y_axes = ("yh", "yl")
    pack = kernel_call(pack_body, shape((4, 400, 128), BF16), 7, grant=None)(
        queries, keys, values, w_gate, w_up, w_down.T, w_out.T
    )
    got = lax.all_to_all(pack, y_axes, 0, 0)
    weights = lax.all_gather(got[:, 192:400], "z", axis=0)
    other = lax.ppermute(got, "c", [(0, 1), (1, 0)])
    place = jnp.stack([c, z]).astype(jnp.int32)
    mine = kernel_call(marks_body, shape((64, HEAD), F32), 3, core=place)(
        got, other, seg_lengths[None, :]
    )
    mine = jnp.sum(lax.all_gather(mine, "z", axis=0), axis=0)
    marks = lax.all_gather(mine / seg_lengths.astype(F32)[:, None], "c", axis=0)
    send = kernel_call(far_body, shape((16, 40, HEAD), F32), 3, core=c[None])(got, other, marks)
    parts = lax.all_to_all(send, "z", 0, 0)
    heads = kernel_call(
        inverse_body,
        shape((2, 64, HEAD), F32),
        1,
        cost=pl.CostEstimate(flops=10**9, bytes_accessed=2 * 10**7, transcendentals=0),
    )(marks)
    heads = lax.all_gather(heads, y_axes, axis=0)
    near = kernel_call(near_body, shape((4, 64, HEAD), F32), 2)(queries, heads)
    parts, near, heads = lax.optimization_barrier((parts, near, heads))
    gathered = kernel_call(merge_body, shape((8, 32, HEAD), F32), 1)(parts)
    gathered = lax.all_to_all(gathered, (*y_axes, "c"), 0, 0)
    weights, gathered = lax.optimization_barrier((weights, gathered))
    w_out = weights[:, :, 0:64]
    swapped = lax.ppermute(w_out, "c", [(0, 1), (1, 0)])
    terms = kernel_call(
        proj_body,
        shape((4, 64, 512), BF16),
        5,
        [pltpu.VMEM((2048, 512), BF16)],
        core=c[None],
    )(near, heads, gathered, w_out, swapped)
    terms, weights = lax.optimization_barrier((terms, weights))
    swapped = lax.ppermute(weights, "c", [(0, 1), (1, 0)])
    parts = lax.all_to_all(terms, "x", 0, 0)
    w1, w2 = kernel_call(
        unmix_body,
        [shape((2048, 768), BF16), shape((2048, 384), BF16)],
        0,
        [pltpu.VMEM((2, 16, 4, 144, 128), BF16), pltpu.SemaphoreType.DMA((2,))],
        core=c[None],
        n_far=2,
        grant=LARGE,
    )(weights, swapped)
    resid = (stream.astype(F32) + jnp.sum(parts.astype(F32), axis=0)).astype(BF16)
    whole = lax.all_to_all(jnp.broadcast_to(resid[None], (8, 64, 512)), ("yl", "x"), 0, 0)
    terms = kernel_call(
        ffn_body,
        shape((8, 64, 512), BF16),
        2,
        [
            pltpu.VMEM((128, 2048), BF16),
            pltpu.VMEM((2048, 768), BF16),
            pltpu.VMEM((2048, 384), BF16),
            pltpu.SemaphoreType.DMA((2,)),
        ],
        n_far=2,
        grant=LARGE,
    )(whole, gain[None, :], w1, w2)
    parts = lax.all_to_all(terms, ("yl", "x"), 0, 0)
    return (resid.astype(F32) + jnp.sum(parts.astype(F32), axis=0)).astype(BF16)


def solution(mesh):
    fine = Mesh(mesh.devices.reshape(16, 2, 2, 2, 4), ("z", "yh", "yl", "c", "x"))
    seq = ("z", "yh", "yl", "c")
    return jax.shard_map(
        on_device,
        mesh=fine,
        in_specs=(
            P(seq, "x"),
            P(seq, "x"),
            P(seq, "x"),
            P(seq, "x"),
            P(),
            P(),
            P("x", seq),
            P(seq, "x"),
            P(seq, "x"),
            P("x", seq),
        ),
        out_specs=P(seq, "x"),
        check_vma=False,
    )
```

```python
import math

import jax
import jax.numpy as jnp
from jax import lax
from jax.experimental import pallas as pl
from jax.experimental.pallas import tpu as pltpu
from jax.sharding import Mesh
from jax.sharding import PartitionSpec as P

PINV_ITERS = 6
HEAD = 128
EPS = 1e-05
SCALE = 1.0 / math.sqrt(HEAD)
HI = lax.Precision.HIGHEST
F32 = jnp.float32
BF16 = jnp.bfloat16
SMALL = 24 << 20
LARGE = 60 << 20
SLICE = (0, 1, 1, 0)
SWAP = ((0, 1), (1, 0))
PAIR = ((0, 3), (3, 0), (1, 2), (2, 1))


def dot(a, b, dims, precision=None):
    return lax.dot_general(
        a, b, (dims, ((), ())), precision=precision, preferred_element_type=F32
    )


def kernel_call(body, out_shape, n_in, scratch=(), cost=None, core=None, grant=SMALL, n_far=0):
    whole = pl.BlockSpec(memory_space=pltpu.VMEM)
    many = isinstance(out_shape, (list, tuple))
    call = pl.pallas_call(
        body,
        out_shape=out_shape,
        in_specs=([] if core is None else [pl.BlockSpec(memory_space=pltpu.SMEM)])
        + [whole] * n_in
        + [pl.BlockSpec(memory_space=pltpu.HBM)] * n_far,
        out_specs=[whole] * len(out_shape) if many else whole,
        scratch_shapes=list(scratch),
        cost_estimate=cost,
        compiler_params=pltpu.CompilerParams(vmem_limit_bytes=grant),
    )
    return call if core is None else lambda *args: call(core, *args)


def shape(dims, dtype):
    return jax.ShapeDtypeStruct(dims, dtype)


def pack_body(q, k, v, wg, wu, wd, wo, out):
    for y in range(4):
        tile = slice(y * 128, y * 128 + 128)
        out[y, 0:64] = q[:, tile]
        out[y, 64:128] = k[:, tile]
        out[y, 128:192] = v[:, tile]
        out[y, 192:208] = wo[:, tile]
        for t in range(3):
            low = (SLICE[y] * 3 + t) * 128
            for i, w in enumerate((wg, wu, wd)):
                at = 208 + (3 * i + t) * 16
                out[y, at : at + 16] = w[:, low : low + 128]


def marks_body(place, mine, other, lengths, out):
    c = place[0]
    row = lax.broadcasted_iota(jnp.int32, (64, 64), 0)
    lane = lax.broadcasted_iota(jnp.int32, (64, 64), 1)
    sizes = jnp.broadcast_to(lengths[...], (64, 64)).astype(F32)
    starts = jnp.sum(jnp.where(lane < row, sizes, 0.0), axis=1, keepdims=True)
    ends = jnp.sum(jnp.where(lane <= row, sizes, 0.0), axis=1, keepdims=True)
    starts, ends = (e.astype(jnp.int32) - place[1] * 512 for e in (starts, ends))
    low = pl.multiple_of(c * 64, 64)
    total = None
    for got, at_core in ((mine, c), (other, 1 - c)):
        at = lax.broadcasted_iota(jnp.int32, (64, 256), 1)
        at = at + (at // 64) * 64 + at_core * 64
        member = ((at >= starts) & (at < ends)).astype(BF16)
        part = dot(member, got[:, pl.ds(low, 64), :].reshape(256, HEAD), ((1,), (0,)))
        total = part if total is None else total + part
    out[...] = total


def shard_body(half, got, out):
    for y in range(4):
        out[y * 16 : y * 16 + 16] = got[y, 192:208]
    for i in range(2):
        out[64 + i * 144 : 208 + i * 144] = got[half[0] * 2 + i, 208:352]


def far_body(core, mine, other, marks, out):
    query = marks[0, pl.ds(core[0] * 32, 32), :]
    far = [
        dot(query, got[:, 64:128].reshape(256, HEAD).astype(F32), ((1,), (1,)), HI) * SCALE
        for got in (mine, other)
    ]
    peak = jnp.maximum(*(jnp.max(f, axis=-1, keepdims=True) for f in far))
    far = [jnp.exp(f - peak) for f in far]
    mass = sum(jnp.sum(f, axis=-1, keepdims=True) for f in far)
    part = sum(
        dot(f, got[:, 128:192].reshape(256, HEAD).astype(F32), ((1,), (0,)), HI)
        for f, got in zip(far, (mine, other))
    )
    row = lax.broadcasted_iota(jnp.int32, (32, HEAD), 0)
    lane = lax.broadcasted_iota(jnp.int32, (32, HEAD), 1)
    stats = jnp.where(lane == row, peak, 0.0) + jnp.where(lane == row + 32, mass, 0.0)
    stats = jnp.broadcast_to(jnp.sum(stats, axis=0, keepdims=True), (8, HEAD))
    for z in range(16):
        out[z, 0:32] = part
        out[z, 32:40] = stats


def merge_body(parts, out):
    row = lax.broadcasted_iota(jnp.int32, (16, 32, HEAD), 1)
    lane = lax.broadcasted_iota(jnp.int32, (16, 32, HEAD), 2)
    stats = jnp.broadcast_to(parts[:, 32:33, :], (16, 32, HEAD))
    peak = jnp.sum(jnp.where(lane == row, stats, 0.0), axis=-1, keepdims=True)
    mass = jnp.sum(jnp.where(lane == row + 32, stats, 0.0), axis=-1, keepdims=True)
    factor = jnp.exp(peak - jnp.max(peak, axis=0, keepdims=True))
    total = jnp.sum(factor * mass, axis=0)
    out[...] = jnp.sum(factor * parts[:, 0:32, :], axis=0) / total


def softmax(scores, axis):
    scores = jnp.exp(scores - jnp.max(scores, axis=axis, keepdims=True))
    return scores / jnp.sum(scores, axis=axis, keepdims=True)


def near_body(got, marks, near, inverse):
    qm, km = marks[0], marks[1]
    query = got[:, 0:64].reshape(256, HEAD).astype(F32)
    near[...] = softmax(dot(query, km, ((1,), (1,)), HI) * SCALE, -1)
    land = softmax(dot(qm, km, ((1,), (1,)), HI) * SCALE, 1)
    across = softmax(dot(km, qm, ((1,), (1,)), HI) * SCALE, 0)
    most = jnp.max(jnp.sum(land, axis=0, keepdims=True), axis=1, keepdims=True) * jnp.max(
        jnp.sum(land, axis=1, keepdims=True), axis=0, keepdims=True
    )
    row = lax.broadcasted_iota(jnp.int32, (64, 64), 0)
    eye = (row == lax.broadcasted_iota(jnp.int32, (64, 64), 1)).astype(F32)
    mul = lambda a, b: dot(a, b, ((1,), (0,)), HI)
    approx = across / most
    for _ in range(PINV_ITERS):
        prod = mul(land, approx)
        inner = 7.0 * eye - prod
        inner = 15.0 * eye - mul(prod, inner)
        inner = 13.0 * eye - mul(prod, inner)
        approx = 0.25 * mul(approx, inner)
    inverse[...] = approx


def spread(terms, out):
    for y in range(terms.shape[0] // 64):
        for x in range(4):
            out[y * 4 + x] = terms[y * 64 : y * 64 + 64, x * 512 : x * 512 + 512].astype(BF16)


def unmix_body(place, mine, mine_core, pair, pair_core, w1, w2, raw, sems):
    c, half = place[0], place[1]
    fars = (mine, mine_core, pair, pair_core)
    copies = [
        pltpu.make_async_copy(far, raw.at[i], sems.at[i]) for i, far in enumerate(fars)
    ]
    for copy in copies:
        copy.start()
    sources = ((half, c), (half, 1 - c), (1 - half, c), (1 - half, 1 - c))
    for i, (h, core) in enumerate(sources):
        copies[i].wait()
        for z in range(16):
            for y in range(2):
                low = pl.multiple_of((z * 8 + h * 4 + y * 2 + core) * 16, 16)
                for t in range(9):
                    at = y * 144 + t * 16
                    rows = raw[i, z, at : at + 16, :]
                    if t < 6:
                        w1[pl.ds(low, 16), t * 128 : t * 128 + 128] = rows
                    else:
                        w2[pl.ds(low, 16), t * 128 - 768 : t * 128 - 640] = rows


def proj_body(place, near, inverse, gathered, mine, other, out, wo):
    for blocks, core in ((mine, place[0]), (other, 1 - place[0])):
        for z in range(16):
            for y in range(4):
                low = pl.multiple_of((z * 8 + y * 2 + core) * 16, 16)
                wo[pl.ds(low, 16), :] = blocks[z, y * 16 : y * 16 + 16, :]
    mixer = dot(inverse[...], gathered[...], ((1,), (0,)), HI)
    attn = dot(near[...], mixer, ((1,), (0,)), HI).astype(BF16)
    spread(dot(attn, wo[...], ((1,), (1,))), out)


def ffn_body(whole, gain, far1, far2, out, normed, w1, w2, sems):
    first_copy = pltpu.make_async_copy(far1, w1, sems.at[0])
    second_copy = pltpu.make_async_copy(far2, w2, sems.at[1])
    first_copy.start()
    second_copy.start()
    for y in range(2):
        blocks = [whole[y * 4 + x].astype(F32) for x in range(4)]
        square = sum(jnp.sum(b * b, axis=-1, keepdims=True) for b in blocks)
        factor = lax.rsqrt(square * (1.0 / 2048.0) + EPS)
        for x in range(4):
            lanes = slice(x * 512, x * 512 + 512)
            normed[y * 64 : y * 64 + 64, lanes] = (
                blocks[x] * factor * gain[:, lanes]
            ).astype(BF16)
    first_copy.wait()
    first = dot(normed[...], w1[...], ((1,), (0,)))
    gate, up = first[:, :384], first[:, 384:]
    hidden = (gate / (1.0 + jnp.exp(-gate)) * up).astype(BF16)
    second_copy.wait()
    spread(dot(hidden, w2[...], ((1,), (1,))), out)


def on_device(queries, keys, values, stream, seg_lengths, gain, w_out, w_gate, w_up, w_down):
    z, c = lax.axis_index("z"), lax.axis_index("c")
    y_axes = ("yh", "yl")
    pack = kernel_call(pack_body, shape((4, 352, 128), BF16), 7, grant=None)(
        queries, keys, values, w_gate, w_up, w_down.T, w_out.T
    )
    got = lax.all_to_all(pack, y_axes, 0, 0)
    yh = lax.axis_index("yh")
    place = jnp.stack([c, z, yh]).astype(jnp.int32)
    shard = kernel_call(shard_body, shape((352, 128), BF16), 1, core=yh[None])(got)
    weights = lax.all_gather(shard, "z", axis=0)
    other = lax.ppermute(got, "c", SWAP)
    mine = kernel_call(marks_body, shape((64, HEAD), F32), 3, core=place)(
        got, other, seg_lengths[None, :]
    )
    mine = jnp.sum(lax.all_gather(mine, "z", axis=0), axis=0)
    marks = lax.all_gather(mine / seg_lengths.astype(F32)[:, None], "c", axis=0)
    send = kernel_call(far_body, shape((16, 40, HEAD), F32), 3, core=c[None])(got, other, marks)
    parts = lax.all_to_all(send, "z", 0, 0)
    near, inverse = kernel_call(
        near_body,
        [shape((256, 64), F32), shape((64, 64), F32)],
        2,
        cost=pl.CostEstimate(flops=10**9, bytes_accessed=2 * 10**7, transcendentals=0),
    )(got, marks)
    w_out, ffn = weights[:, 0:64], weights[:, 64:352]
    w_other = lax.ppermute(w_out, "c", SWAP)
    pair = lax.ppermute(ffn, y_axes, PAIR)
    parts, near, inverse, w_other, ffn = lax.optimization_barrier(
        (parts, near, inverse, w_other, ffn)
    )
    gathered = kernel_call(merge_body, shape((32, HEAD), F32), 1)(parts)
    gathered = lax.all_gather(gathered, "c", axis=0, tiled=True)
    terms = kernel_call(
        proj_body, shape((16, 64, 512), BF16), 5, [pltpu.VMEM((2048, 128), BF16)], core=place
    )(near, inverse, gathered, w_out, w_other)
    parts = lax.all_to_all(terms, (*y_axes, "x"), 0, 0)
    ffn, pair, terms = lax.optimization_barrier((ffn, pair, terms))
    ffn_core = lax.ppermute(ffn, "c", SWAP)
    pair_core = lax.ppermute(pair, "c", SWAP)
    w1, w2 = kernel_call(
        unmix_body,
        [shape((2048, 768), BF16), shape((2048, 384), BF16)],
        0,
        [pltpu.VMEM((4, 16, 288, 128), BF16), pltpu.SemaphoreType.DMA((4,))],
        core=jnp.stack([c, yh]).astype(jnp.int32),
        n_far=4,
        grant=LARGE,
    )(ffn, ffn_core, pair, pair_core)
    resid = (stream.astype(F32) + jnp.sum(parts.astype(F32), axis=0)).astype(BF16)
    whole = lax.all_to_all(jnp.broadcast_to(resid[None], (8, 64, 512)), ("yl", "x"), 0, 0)
    terms = kernel_call(
        ffn_body,
        shape((8, 64, 512), BF16),
        2,
        [
            pltpu.VMEM((128, 2048), BF16),
            pltpu.VMEM((2048, 768), BF16),
            pltpu.VMEM((2048, 384), BF16),
            pltpu.SemaphoreType.DMA((2,)),
        ],
        n_far=2,
        grant=LARGE,
    )(whole, gain[None, :], w1, w2)
    parts = lax.all_to_all(terms, ("yl", "x"), 0, 0)
    return (resid.astype(F32) + jnp.sum(parts.astype(F32), axis=0)).astype(BF16)


def solution(mesh):
    fine = Mesh(mesh.devices.reshape(16, 2, 2, 2, 4), ("z", "yh", "yl", "c", "x"))
    seq = ("z", "yh", "yl", "c")
    return jax.shard_map(
        on_device,
        mesh=fine,
        in_specs=(
            P(seq, "x"),
            P(seq, "x"),
            P(seq, "x"),
            P(seq, "x"),
            P(),
            P(),
            P("x", seq),
            P(seq, "x"),
            P(seq, "x"),
            P("x", seq),
        ),
        out_specs=P(seq, "x"),
        check_vma=False,
    )
```

```python
import math

import jax
import jax.numpy as jnp
from jax import lax
from jax.experimental import pallas as pl
from jax.experimental.pallas import tpu as pltpu
from jax.sharding import Mesh
from jax.sharding import PartitionSpec as P

PINV_ITERS = 6
HEAD = 128
EPS = 1e-05
SCALE = 1.0 / math.sqrt(HEAD)
HI = lax.Precision.HIGHEST
F32 = jnp.float32
BF16 = jnp.bfloat16
SMALL = 24 << 20
LARGE = 60 << 20


def dot(a, b, dims, precision=None):
    return lax.dot_general(
        a, b, (dims, ((), ())), precision=precision, preferred_element_type=F32
    )


def kernel_call(body, out_shape, n_in, scratch=(), cost=None, core=None, grant=SMALL, n_far=0):
    whole = pl.BlockSpec(memory_space=pltpu.VMEM)
    many = isinstance(out_shape, (list, tuple))
    call = pl.pallas_call(
        body,
        out_shape=out_shape,
        in_specs=([] if core is None else [pl.BlockSpec(memory_space=pltpu.SMEM)])
        + [whole] * n_in
        + [pl.BlockSpec(memory_space=pltpu.HBM)] * n_far,
        out_specs=[whole] * len(out_shape) if many else whole,
        scratch_shapes=list(scratch),
        cost_estimate=cost,
        compiler_params=pltpu.CompilerParams(vmem_limit_bytes=grant),
    )
    return call if core is None else lambda *args: call(core, *args)


def shape(dims, dtype):
    return jax.ShapeDtypeStruct(dims, dtype)


def pack_body(q, k, v, wg, wu, wd, wo, out):
    for y in range(4):
        tile = slice(y * 128, y * 128 + 128)
        out[y, 0:64] = q[:, tile]
        out[y, 64:128] = k[:, tile]
        out[y, 128:192] = v[:, tile]
        for t in range(4):
            out[y, 192 + t * 16 : 208 + t * 16] = wo[:, t * 128 : t * 128 + 128]
        for t in range(3):
            low = ((y % 2) * 3 + t) * 128
            for i, w in enumerate((wg, wu, wd)):
                at = 256 + (3 * i + t) * 16
                out[y, at : at + 16] = w[:, low : low + 128]


def marks_body(place, mine, other, lengths, out):
    c = place[0]
    row = lax.broadcasted_iota(jnp.int32, (64, 64), 0)
    lane = lax.broadcasted_iota(jnp.int32, (64, 64), 1)
    sizes = jnp.broadcast_to(lengths[...], (64, 64))
    starts = jnp.sum(jnp.where(lane < row, sizes, 0.0), axis=1, keepdims=True)
    ends = jnp.sum(jnp.where(lane <= row, sizes, 0.0), axis=1, keepdims=True)
    starts, ends = (e.astype(jnp.int32) - place[1] * 512 for e in (starts, ends))
    low = pl.multiple_of(c * 64, 64)
    total = None
    for got, at_core in ((mine, c), (other, 1 - c)):
        at = lax.broadcasted_iota(jnp.int32, (64, 256), 1)
        at = at + (at // 64) * 64 + at_core * 64
        member = ((at >= starts) & (at < ends)).astype(BF16)
        part = dot(member, got[:, pl.ds(low, 64), :].reshape(256, HEAD), ((1,), (0,)))
        total = part if total is None else total + part
    out[...] = total


def far_body(core, mine, other, marks, out):
    query = marks[0, pl.ds(core[0] * 32, 32), :]
    far = [
        dot(query, got[:, 64:128].reshape(256, HEAD).astype(F32), ((1,), (1,)), HI) * SCALE
        for got in (mine, other)
    ]
    peak = jnp.maximum(*(jnp.max(f, axis=-1, keepdims=True) for f in far))
    far = [jnp.exp(f - peak) for f in far]
    mass = sum(jnp.sum(f, axis=-1, keepdims=True) for f in far)
    part = sum(
        dot(f, got[:, 128:192].reshape(256, HEAD).astype(F32), ((1,), (0,)), HI)
        for f, got in zip(far, (mine, other))
    )
    row = lax.broadcasted_iota(jnp.int32, (32, HEAD), 0)
    lane = lax.broadcasted_iota(jnp.int32, (32, HEAD), 1)
    stats = jnp.where(lane == row, peak, 0.0) + jnp.where(lane == row + 32, mass, 0.0)
    stats = jnp.broadcast_to(jnp.sum(stats, axis=0, keepdims=True), (8, HEAD))
    for z in range(16):
        out[z, 0:32] = part
        out[z, 32:40] = stats


def merge_body(parts, out):
    row = lax.broadcasted_iota(jnp.int32, (16, 32, HEAD), 1)
    lane = lax.broadcasted_iota(jnp.int32, (16, 32, HEAD), 2)
    stats = jnp.broadcast_to(parts[:, 32:33, :], (16, 32, HEAD))
    peak = jnp.sum(jnp.where(lane == row, stats, 0.0), axis=-1, keepdims=True)
    mass = jnp.sum(jnp.where(lane == row + 32, stats, 0.0), axis=-1, keepdims=True)
    factor = jnp.exp(peak - jnp.max(peak, axis=0, keepdims=True))
    total = jnp.sum(factor * mass, axis=0)
    rows = jnp.sum(factor * parts[:, 0:32, :], axis=0) / total
    for i in range(8):
        out[i] = rows


def softmax(scores, axis):
    scores = jnp.exp(scores - jnp.max(scores, axis=axis, keepdims=True))
    return scores / jnp.sum(scores, axis=axis, keepdims=True)


def inverse_body(marks, out):
    qm, km = marks[0], marks[1]
    out[0] = km
    land = softmax(dot(qm, km, ((1,), (1,)), HI) * SCALE, 1)
    across = softmax(dot(km, qm, ((1,), (1,)), HI) * SCALE, 0)
    most = jnp.max(jnp.sum(land, axis=0, keepdims=True), axis=1, keepdims=True) * jnp.max(
        jnp.sum(land, axis=1, keepdims=True), axis=0, keepdims=True
    )
    row = lax.broadcasted_iota(jnp.int32, (64, 64), 0)
    eye = (row == lax.broadcasted_iota(jnp.int32, (64, 64), 1)).astype(F32)
    mul = lambda a, b: dot(a, b, ((1,), (0,)), HI)
    approx = across / most
    for _ in range(PINV_ITERS):
        prod = mul(land, approx)
        inner = 7.0 * eye - prod
        inner = 15.0 * eye - mul(prod, inner)
        inner = 13.0 * eye - mul(prod, inner)
        approx = 0.25 * mul(approx, inner)
    out[1] = jnp.concatenate([approx, jnp.zeros_like(approx)], axis=-1)


def near_body(queries, heads, out):
    for h in range(4):
        query = queries[:, h * HEAD : h * HEAD + HEAD].astype(F32)
        near = softmax(dot(query, heads[h, 0], ((1,), (1,)), HI) * SCALE, -1)
        out[h] = jnp.concatenate([near, jnp.zeros_like(near)], axis=-1)


def spread(terms, out):
    for y in range(terms.shape[0] // 64):
        for x in range(4):
            out[y * 4 + x] = terms[y * 64 : y * 64 + 64, x * 512 : x * 512 + 512].astype(BF16)


def unmix(blocks, tile, dest, lanes, c):
    for z in range(16):
        for y in range(4):
            low = pl.multiple_of((z * 8 + y * 2 + c) * 16, 16)
            dest[pl.ds(low, 16), lanes] = blocks[z, y, tile * 16 : tile * 16 + 16, :]


def unmix_body(core, mine, other, w1, w2, raw, sems):
    copies = [
        pltpu.make_async_copy(far.at[:, :, 64:208], raw.at[i], sems.at[i])
        for i, far in enumerate((mine, other))
    ]
    for copy in copies:
        copy.start()
    for i, c in enumerate((core[0], 1 - core[0])):
        copies[i].wait()
        for t in range(6):
            unmix(raw.at[i], t, w1, slice(t * 128, t * 128 + 128), c)
        for t in range(3):
            unmix(raw.at[i], 6 + t, w2, slice(t * 128, t * 128 + 128), c)


def proj_body(core, near, heads, gathered, mine, other, out, wo):
    for t in range(4):
        lanes = slice(t * 128, t * 128 + 128)
        unmix(mine, t, wo, lanes, core[0])
        unmix(other, t, wo, lanes, 1 - core[0])
    attn = []
    for h in range(4):
        rows = jnp.concatenate([gathered[2 * h], gathered[2 * h + 1]], axis=0)
        mixer = dot(heads[h, 1][:, :64], rows, ((1,), (0,)), HI)
        attn.append(dot(near[h][:, :64], mixer, ((1,), (0,)), HI).astype(BF16))
    attn = jnp.concatenate(attn, axis=-1)
    spread(dot(attn, wo[...], ((1,), (1,))), out)


def ffn_body(whole, gain, far1, far2, out, normed, w1, w2, sems):
    first_copy = pltpu.make_async_copy(far1, w1, sems.at[0])
    second_copy = pltpu.make_async_copy(far2, w2, sems.at[1])
    first_copy.start()
    second_copy.start()
    for y in range(2):
        blocks = [whole[y * 4 + x].astype(F32) for x in range(4)]
        square = sum(jnp.sum(b * b, axis=-1, keepdims=True) for b in blocks)
        factor = lax.rsqrt(square * (1.0 / 2048.0) + EPS)
        for x in range(4):
            lanes = slice(x * 512, x * 512 + 512)
            normed[y * 64 : y * 64 + 64, lanes] = (
                blocks[x] * factor * gain[:, lanes]
            ).astype(BF16)
    first_copy.wait()
    first = dot(normed[...], w1[...], ((1,), (0,)))
    gate, up = first[:, :384], first[:, 384:]
    hidden = (gate / (1.0 + jnp.exp(-gate)) * up).astype(BF16)
    second_copy.wait()
    spread(dot(hidden, w2[...], ((1,), (1,))), out)


def on_device(queries, keys, values, stream, seg_lengths, gain, w_out, w_gate, w_up, w_down):
    z, c = lax.axis_index("z"), lax.axis_index("c")
    y_axes = ("yh", "yl")
    pack = kernel_call(pack_body, shape((4, 400, 128), BF16), 7, grant=None)(
        queries, keys, values, w_gate, w_up, w_down.T, w_out.T
    )
    got = lax.all_to_all(pack, y_axes, 0, 0)
    weights = lax.all_gather(got[:, 192:400], "z", axis=0)
    other = lax.ppermute(got, "c", [(0, 1), (1, 0)])
    lengths = seg_lengths.astype(F32)
    place = jnp.stack([c, z]).astype(jnp.int32)
    mine = kernel_call(marks_body, shape((64, HEAD), F32), 3, core=place)(
        got, other, lengths[None, :]
    )
    mine = jnp.sum(lax.all_gather(mine, "z", axis=0), axis=0)
    marks = lax.all_gather(mine / lengths[:, None], "c", axis=0)
    send = kernel_call(far_body, shape((16, 40, HEAD), F32), 3, core=c[None])(got, other, marks)
    parts = lax.all_to_all(send, "z", 0, 0)
    heads = kernel_call(
        inverse_body,
        shape((2, 64, HEAD), F32),
        1,
        cost=pl.CostEstimate(flops=10**9, bytes_accessed=2 * 10**7, transcendentals=0),
    )(marks)
    heads = lax.all_gather(heads, y_axes, axis=0)
    near = kernel_call(near_body, shape((4, 64, HEAD), F32), 2)(queries, heads)
    parts, near, heads = lax.optimization_barrier((parts, near, heads))
    gathered = kernel_call(merge_body, shape((8, 32, HEAD), F32), 1)(parts)
    gathered = lax.all_to_all(gathered, (*y_axes, "c"), 0, 0)
    weights, gathered = lax.optimization_barrier((weights, gathered))
    w_out = weights[:, :, 0:64]
    swapped = lax.ppermute(w_out, "c", [(0, 1), (1, 0)])
    terms = kernel_call(
        proj_body,
        shape((4, 64, 512), BF16),
        5,
        [pltpu.VMEM((2048, 512), BF16)],
        core=c[None],
    )(near, heads, gathered, w_out, swapped)
    terms, weights = lax.optimization_barrier((terms, weights))
    swapped = lax.ppermute(weights, "c", [(0, 1), (1, 0)])
    parts = lax.all_to_all(terms, "x", 0, 0)
    w1, w2 = kernel_call(
        unmix_body,
        [shape((2048, 768), BF16), shape((2048, 384), BF16)],
        0,
        [pltpu.VMEM((2, 16, 4, 144, 128), BF16), pltpu.SemaphoreType.DMA((2,))],
        core=c[None],
        n_far=2,
        grant=LARGE,
    )(weights, swapped)
    resid = (stream.astype(F32) + jnp.sum(parts.astype(F32), axis=0)).astype(BF16)
    whole = lax.all_to_all(jnp.broadcast_to(resid[None], (8, 64, 512)), ("yl", "x"), 0, 0)
    terms = kernel_call(
        ffn_body,
        shape((8, 64, 512), BF16),
        2,
        [
            pltpu.VMEM((128, 2048), BF16),
            pltpu.VMEM((2048, 768), BF16),
            pltpu.VMEM((2048, 384), BF16),
            pltpu.SemaphoreType.DMA((2,)),
        ],
        n_far=2,
        grant=LARGE,
    )(whole, gain[None, :], w1, w2)
    parts = lax.all_to_all(terms, ("yl", "x"), 0, 0)
    return (resid.astype(F32) + jnp.sum(parts.astype(F32), axis=0)).astype(BF16)


def solution(mesh):
    fine = Mesh(mesh.devices.reshape(16, 2, 2, 2, 4), ("z", "yh", "yl", "c", "x"))
    seq = ("z", "yh", "yl", "c")
    return jax.shard_map(
        on_device,
        mesh=fine,
        in_specs=(
            P(seq, "x"),
            P(seq, "x"),
            P(seq, "x"),
            P(seq, "x"),
            P(),
            P(),
            P("x", seq),
            P(seq, "x"),
            P(seq, "x"),
            P("x", seq),
        ),
        out_specs=P(seq, "x"),
        check_vma=False,
    )
```

```python
import math

import jax
import jax.numpy as jnp
import numpy as np
from jax import lax
from jax.experimental import pallas as pl
from jax.experimental.pallas import tpu as pltpu
from jax.sharding import Mesh
from jax.sharding import PartitionSpec as P

PINV_ITERS = 6
HEAD = 128
EPS = 1e-05
SCALE = 1.0 / math.sqrt(HEAD)
HI = lax.Precision.HIGHEST
F32 = jnp.float32
BF16 = jnp.bfloat16
SMALL = 24 << 20
LARGE = 60 << 20


def dot(a, b, dims, precision=None):
    return lax.dot_general(
        a, b, (dims, ((), ())), precision=precision, preferred_element_type=F32
    )


def kernel_call(body, out_shape, n_in, scratch=(), cost=None, core=None, grant=SMALL, n_far=0):
    whole = pl.BlockSpec(memory_space=pltpu.VMEM)
    many = isinstance(out_shape, (list, tuple))
    call = pl.pallas_call(
        body,
        out_shape=out_shape,
        in_specs=([] if core is None else [pl.BlockSpec(memory_space=pltpu.SMEM)])
        + [whole] * n_in
        + [pl.BlockSpec(memory_space=pltpu.HBM)] * n_far,
        out_specs=[whole] * len(out_shape) if many else whole,
        scratch_shapes=list(scratch),
        cost_estimate=cost,
        compiler_params=pltpu.CompilerParams(vmem_limit_bytes=grant),
    )
    return call if core is None else lambda *args: call(core, *args)


def shape(dims, dtype):
    return jax.ShapeDtypeStruct(dims, dtype)


def pack_body(q, k, v, wg, wu, wd, wo, out):
    for y in range(4):
        tile = slice(y * 128, y * 128 + 128)
        out[y, 0:64] = q[:, tile]
        out[y, 64:128] = k[:, tile]
        out[y, 128:192] = v[:, tile]
        for t in range(4):
            out[y, 192 + t * 16 : 208 + t * 16] = wo[:, t * 128 : t * 128 + 128]
        for t in range(3):
            low = ((y % 2) * 3 + t) * 128
            for i, w in enumerate((wg, wu, wd)):
                at = 256 + (3 * i + t) * 16
                out[y, at : at + 16] = w[:, low : low + 128]


def marks_body(place, mine, other, lengths, out):
    c = place[0]
    row = lax.broadcasted_iota(jnp.int32, (64, 64), 0)
    lane = lax.broadcasted_iota(jnp.int32, (64, 64), 1)
    sizes = jnp.broadcast_to(lengths[...], (64, 64))
    starts = jnp.sum(jnp.where(lane < row, sizes, 0.0), axis=1, keepdims=True)
    ends = jnp.sum(jnp.where(lane <= row, sizes, 0.0), axis=1, keepdims=True)
    starts, ends = (e.astype(jnp.int32) - place[1] * 512 for e in (starts, ends))
    low = pl.multiple_of(c * 64, 64)
    total = None
    for got, at_core in ((mine, c), (other, 1 - c)):
        at = lax.broadcasted_iota(jnp.int32, (64, 256), 1)
        at = at + (at // 64) * 64 + at_core * 64
        member = ((at >= starts) & (at < ends)).astype(BF16)
        part = dot(member, got[:, pl.ds(low, 64), :].reshape(256, HEAD), ((1,), (0,)))
        total = part if total is None else total + part
    out[...] = total


def far_body(core, mine, other, marks, out):
    query = marks[0, pl.ds(core[0] * 32, 32), :]
    far = [
        dot(query, got[:, 64:128].reshape(256, HEAD).astype(F32), ((1,), (1,)), HI) * SCALE
        for got in (mine, other)
    ]
    peak = jnp.maximum(*(jnp.max(f, axis=-1, keepdims=True) for f in far))
    far = [jnp.exp(f - peak) for f in far]
    mass = sum(jnp.sum(f, axis=-1, keepdims=True) for f in far)
    part = sum(
        dot(f, got[:, 128:192].reshape(256, HEAD).astype(F32), ((1,), (0,)), HI)
        for f, got in zip(far, (mine, other))
    )
    row = lax.broadcasted_iota(jnp.int32, (32, HEAD), 0)
    lane = lax.broadcasted_iota(jnp.int32, (32, HEAD), 1)
    stats = jnp.where(lane == row, peak, 0.0) + jnp.where(lane == row + 32, mass, 0.0)
    stats = jnp.broadcast_to(jnp.sum(stats, axis=0, keepdims=True), (8, HEAD))
    for z in range(16):
        out[z, 0:32] = part
        out[z, 32:40] = stats


def merge_body(parts, out):
    row = lax.broadcasted_iota(jnp.int32, (16, 32, HEAD), 1)
    lane = lax.broadcasted_iota(jnp.int32, (16, 32, HEAD), 2)
    stats = jnp.broadcast_to(parts[:, 32:33, :], (16, 32, HEAD))
    peak = jnp.sum(jnp.where(lane == row, stats, 0.0), axis=-1, keepdims=True)
    mass = jnp.sum(jnp.where(lane == row + 32, stats, 0.0), axis=-1, keepdims=True)
    factor = jnp.exp(peak - jnp.max(peak, axis=0, keepdims=True))
    total = jnp.sum(factor * mass, axis=0)
    rows = jnp.sum(factor * parts[:, 0:32, :], axis=0) / total
    for i in range(8):
        out[i] = rows


def softmax(scores, axis):
    scores = jnp.exp(scores - jnp.max(scores, axis=axis, keepdims=True))
    return scores / jnp.sum(scores, axis=axis, keepdims=True)


def inverse_body(marks, out):
    qm, km = marks[0], marks[1]
    out[0] = km
    land = softmax(dot(qm, km, ((1,), (1,)), HI) * SCALE, 1)
    across = softmax(dot(km, qm, ((1,), (1,)), HI) * SCALE, 0)
    most = jnp.max(jnp.sum(land, axis=0, keepdims=True), axis=1, keepdims=True) * jnp.max(
        jnp.sum(land, axis=1, keepdims=True), axis=0, keepdims=True
    )
    row = lax.broadcasted_iota(jnp.int32, (64, 64), 0)
    eye = (row == lax.broadcasted_iota(jnp.int32, (64, 64), 1)).astype(F32)
    mul = lambda a, b: dot(a, b, ((1,), (0,)), HI)
    approx = across / most
    for _ in range(PINV_ITERS):
        prod = mul(land, approx)
        inner = 7.0 * eye - prod
        inner = 15.0 * eye - mul(prod, inner)
        inner = 13.0 * eye - mul(prod, inner)
        approx = 0.25 * mul(approx, inner)
    out[1] = jnp.concatenate([approx, jnp.zeros_like(approx)], axis=-1)


def near_body(queries, heads, out):
    for h in range(4):
        query = queries[:, h * HEAD : h * HEAD + HEAD].astype(F32)
        near = softmax(dot(query, heads[h, 0], ((1,), (1,)), HI) * SCALE, -1)
        out[h] = jnp.concatenate([near, jnp.zeros_like(near)], axis=-1)


def spread(terms, out):
    for y in range(terms.shape[0] // 64):
        for x in range(4):
            out[y * 4 + x] = terms[y * 64 : y * 64 + 64, x * 512 : x * 512 + 512].astype(BF16)


def unmix(blocks, tile, dest, lanes, c):
    for z in range(16):
        for y in range(4):
            low = pl.multiple_of((z * 8 + y * 2 + c) * 16, 16)
            dest[pl.ds(low, 16), lanes] = blocks[z, y, tile * 16 : tile * 16 + 16, :]


def unmix_body(core, mine, other, w1, w2, raw, sems):
    copies = [
        pltpu.make_async_copy(far.at[:, :, 64:208], raw.at[i], sems.at[i])
        for i, far in enumerate((mine, other))
    ]
    for copy in copies:
        copy.start()
    for i, c in enumerate((core[0], 1 - core[0])):
        copies[i].wait()
        for t in range(6):
            unmix(raw.at[i], t, w1, slice(t * 128, t * 128 + 128), c)
        for t in range(3):
            unmix(raw.at[i], 6 + t, w2, slice(t * 128, t * 128 + 128), c)


def attn_body(near, heads, gathered, out):
    for h in range(4):
        rows = jnp.concatenate([gathered[2 * h], gathered[2 * h + 1]], axis=0)
        mixer = dot(heads[h, 1][:, :64], rows, ((1,), (0,)), HI)
        attn = dot(near[h][:, :64], mixer, ((1,), (0,)), HI)
        out[:, h * HEAD : h * HEAD + HEAD] = attn.astype(BF16)


def proj_body(core, mine, other, weights, out, raw, wo, sem):
    copy = pltpu.make_async_copy(weights.at[:, :, 0:64], raw, sem)
    copy.start()
    copy.wait()
    for z in range(16):
        for y in range(4):
            low = (z * 4 + y) * 16
            for t in range(4):
                lanes = slice(t * 128, t * 128 + 128)
                wo[low : low + 16, lanes] = raw[z, y, t * 16 : t * 16 + 16, :]
    for attn, c in ((mine, core[0]), (other, 1 - core[0])):
        terms = dot(attn[...], wo[...], ((1,), (1,)))
        for x in range(4):
            out[c * 4 + x] = terms[:, x * 256 : x * 256 + 256].astype(BF16)


def ffn_body(whole, gain, far1, far2, out, normed, w1, w2, sems):
    first_copy = pltpu.make_async_copy(far1, w1, sems.at[0])
    second_copy = pltpu.make_async_copy(far2, w2, sems.at[1])
    first_copy.start()
    second_copy.start()
    for y in range(2):
        blocks = [whole[y * 4 + x].astype(F32) for x in range(4)]
        square = sum(jnp.sum(b * b, axis=-1, keepdims=True) for b in blocks)
        factor = lax.rsqrt(square * (1.0 / 2048.0) + EPS)
        for x in range(4):
            lanes = slice(x * 512, x * 512 + 512)
            normed[y * 64 : y * 64 + 64, lanes] = (
                blocks[x] * factor * gain[:, lanes]
            ).astype(BF16)
    first_copy.wait()
    first = dot(normed[...], w1[...], ((1,), (0,)))
    gate, up = first[:, :384], first[:, 384:]
    hidden = (gate / (1.0 + jnp.exp(-gate)) * up).astype(BF16)
    second_copy.wait()
    spread(dot(hidden, w2[...], ((1,), (1,))), out)


def on_device(queries, keys, values, stream, seg_lengths, gain, w_out, w_gate, w_up, w_down):
    z, c = lax.axis_index("z"), lax.axis_index("c")
    y_axes = ("yh", "yl")
    pack = kernel_call(pack_body, shape((4, 400, 128), BF16), 7, grant=None)(
        queries, keys, values, w_gate, w_up, w_down.T, w_out.T
    )
    got = lax.all_to_all(pack, y_axes, 0, 0)
    weights = lax.all_gather(got[:, 192:400], "z", axis=0)
    other = lax.ppermute(got, "c", [(0, 1), (1, 0)])
    lengths = seg_lengths.astype(F32)
    place = jnp.stack([c, z]).astype(jnp.int32)
    mine = kernel_call(marks_body, shape((64, HEAD), F32), 3, core=place)(
        got, other, lengths[None, :]
    )
    mine = jnp.sum(lax.all_gather(mine, "z", axis=0), axis=0)
    marks = lax.all_gather(mine / lengths[:, None], "c", axis=0)
    send = kernel_call(far_body, shape((16, 40, HEAD), F32), 3, core=c[None])(got, other, marks)
    parts = lax.all_to_all(send, "z", 0, 0)
    heads = kernel_call(
        inverse_body,
        shape((2, 64, HEAD), F32),
        1,
        cost=pl.CostEstimate(flops=10**9, bytes_accessed=2 * 10**7, transcendentals=0),
    )(marks)
    heads = lax.all_gather(heads, y_axes, axis=0)
    near = kernel_call(near_body, shape((4, 64, HEAD), F32), 2)(queries, heads)
    parts, near, heads = lax.optimization_barrier((parts, near, heads))
    gathered = kernel_call(merge_body, shape((8, 32, HEAD), F32), 1)(parts)
    gathered = lax.all_to_all(gathered, (*y_axes, "c"), 0, 0)
    attn = kernel_call(attn_body, shape((64, 512), BF16), 3)(near, heads, gathered)
    attn_other = lax.ppermute(attn, "c", [(0, 1), (1, 0)])
    weights, attn_other = lax.optimization_barrier((weights, attn_other))
    terms = kernel_call(
        proj_body,
        shape((8, 64, 256), BF16),
        2,
        [
            pltpu.VMEM((16, 4, 64, 128), BF16),
            pltpu.VMEM((1024, 512), BF16),
            pltpu.SemaphoreType.DMA(()),
        ],
        core=c[None],
        n_far=1,
        grant=LARGE,
    )(attn, attn_other, weights)
    terms, weights = lax.optimization_barrier((terms, weights))
    swapped = lax.ppermute(weights, "c", [(0, 1), (1, 0)])
    parts = lax.all_to_all(terms, ("c", "x"), 0, 0)
    w1, w2 = kernel_call(
        unmix_body,
        [shape((2048, 768), BF16), shape((2048, 384), BF16)],
        0,
        [pltpu.VMEM((2, 16, 4, 144, 128), BF16), pltpu.SemaphoreType.DMA((2,))],
        core=c[None],
        n_far=2,
        grant=LARGE,
    )(weights, swapped)
    halves = jnp.sum(parts.reshape(2, 4, 64, 256).astype(F32), axis=1)
    at = np.arange(256, dtype=np.int32)
    at = (at // 16) * 32 + at % 16 + 16 * np.arange(2, dtype=np.int32)[:, None]
    order = (at[:, :, None] == jnp.arange(512, dtype=jnp.int32)).astype(F32)
    proj = jnp.einsum("ctk,ckf->tf", halves, order, precision=HI, preferred_element_type=F32)
    resid = (stream.astype(F32) + proj).astype(BF16)
    whole = lax.all_to_all(jnp.broadcast_to(resid[None], (8, 64, 512)), ("yl", "x"), 0, 0)
    terms = kernel_call(
        ffn_body,
        shape((8, 64, 512), BF16),
        2,
        [
            pltpu.VMEM((128, 2048), BF16),
            pltpu.VMEM((2048, 768), BF16),
            pltpu.VMEM((2048, 384), BF16),
            pltpu.SemaphoreType.DMA((2,)),
        ],
        n_far=2,
        grant=LARGE,
    )(whole, gain[None, :], w1, w2)
    parts = lax.all_to_all(terms, ("yl", "x"), 0, 0)
    return (resid.astype(F32) + jnp.sum(parts.astype(F32), axis=0)).astype(BF16)


def solution(mesh):
    fine = Mesh(mesh.devices.reshape(16, 2, 2, 2, 4), ("z", "yh", "yl", "c", "x"))
    seq = ("z", "yh", "yl", "c")
    return jax.shard_map(
        on_device,
        mesh=fine,
        in_specs=(
            P(seq, "x"),
            P(seq, "x"),
            P(seq, "x"),
            P(seq, "x"),
            P(),
            P(),
            P("x", seq),
            P(seq, "x"),
            P(seq, "x"),
            P("x", seq),
        ),
        out_specs=P(seq, "x"),
        check_vma=False,
    )
```

```python
import math

import jax
import jax.numpy as jnp
import numpy as np
from jax import lax
from jax.experimental import pallas as pl
from jax.experimental.pallas import tpu as pltpu
from jax.sharding import Mesh
from jax.sharding import PartitionSpec as P

PINV_ITERS = 6
HEAD = 128
EPS = 1e-05
SCALE = 1.0 / math.sqrt(HEAD)
HI = lax.Precision.HIGHEST
F32 = jnp.float32
BF16 = jnp.bfloat16
SMALL = 24 << 20
LARGE = 60 << 20


def dot(a, b, dims, precision=None):
    return lax.dot_general(
        a, b, (dims, ((), ())), precision=precision, preferred_element_type=F32
    )


def kernel_call(body, out_shape, n_in, scratch=(), cost=None, core=None, grant=SMALL, n_far=0):
    whole = pl.BlockSpec(memory_space=pltpu.VMEM)
    many = isinstance(out_shape, (list, tuple))
    call = pl.pallas_call(
        body,
        out_shape=out_shape,
        in_specs=([] if core is None else [pl.BlockSpec(memory_space=pltpu.SMEM)])
        + [whole] * n_in
        + [pl.BlockSpec(memory_space=pltpu.HBM)] * n_far,
        out_specs=[whole] * len(out_shape) if many else whole,
        scratch_shapes=list(scratch),
        cost_estimate=cost,
        compiler_params=pltpu.CompilerParams(vmem_limit_bytes=grant),
    )
    return call if core is None else lambda *args: call(core, *args)


def shape(dims, dtype):
    return jax.ShapeDtypeStruct(dims, dtype)


def pack_body(q, k, v, wg, wu, wd, wo, out):
    for y in range(4):
        tile = slice(y * 128, y * 128 + 128)
        out[y, 0:64] = q[:, tile]
        out[y, 64:128] = k[:, tile]
        out[y, 128:192] = v[:, tile]
        for t in range(4):
            out[y, 192 + t * 16 : 208 + t * 16] = wo[:, t * 128 : t * 128 + 128]
        for t in range(3):
            low = ((y % 2) * 3 + t) * 128
            for i, w in enumerate((wg, wu, wd)):
                at = 256 + (3 * i + t) * 16
                out[y, at : at + 16] = w[:, low : low + 128]


def marks_body(place, mine, other, lengths, out):
    c = place[0]
    row = lax.broadcasted_iota(jnp.int32, (64, 64), 0)
    lane = lax.broadcasted_iota(jnp.int32, (64, 64), 1)
    sizes = jnp.broadcast_to(lengths[...], (64, 64))
    starts = jnp.sum(jnp.where(lane < row, sizes, 0.0), axis=1, keepdims=True)
    ends = jnp.sum(jnp.where(lane <= row, sizes, 0.0), axis=1, keepdims=True)
    starts, ends = (e.astype(jnp.int32) - place[1] * 512 for e in (starts, ends))
    low = pl.multiple_of(c * 64, 64)
    total = None
    for got, at_core in ((mine, c), (other, 1 - c)):
        at = lax.broadcasted_iota(jnp.int32, (64, 256), 1)
        at = at + (at // 64) * 64 + at_core * 64
        member = ((at >= starts) & (at < ends)).astype(BF16)
        part = dot(member, got[:, pl.ds(low, 64), :].reshape(256, HEAD), ((1,), (0,)))
        total = part if total is None else total + part
    out[...] = total


def far_body(core, mine, other, marks, out):
    query = marks[0, pl.ds(core[0] * 32, 32), :]
    far = [
        dot(query, got[:, 64:128].reshape(256, HEAD).astype(F32), ((1,), (1,)), HI) * SCALE
        for got in (mine, other)
    ]
    peak = jnp.maximum(*(jnp.max(f, axis=-1, keepdims=True) for f in far))
    far = [jnp.exp(f - peak) for f in far]
    mass = sum(jnp.sum(f, axis=-1, keepdims=True) for f in far)
    part = sum(
        dot(f, got[:, 128:192].reshape(256, HEAD).astype(F32), ((1,), (0,)), HI)
        for f, got in zip(far, (mine, other))
    )
    row = lax.broadcasted_iota(jnp.int32, (32, HEAD), 0)
    lane = lax.broadcasted_iota(jnp.int32, (32, HEAD), 1)
    stats = jnp.where(lane == row, peak, 0.0) + jnp.where(lane == row + 32, mass, 0.0)
    stats = jnp.broadcast_to(jnp.sum(stats, axis=0, keepdims=True), (8, HEAD))
    for z in range(16):
        out[z, 0:32] = part
        out[z, 32:40] = stats


def merge_body(parts, out):
    row = lax.broadcasted_iota(jnp.int32, (16, 32, HEAD), 1)
    lane = lax.broadcasted_iota(jnp.int32, (16, 32, HEAD), 2)
    stats = jnp.broadcast_to(parts[:, 32:33, :], (16, 32, HEAD))
    peak = jnp.sum(jnp.where(lane == row, stats, 0.0), axis=-1, keepdims=True)
    mass = jnp.sum(jnp.where(lane == row + 32, stats, 0.0), axis=-1, keepdims=True)
    factor = jnp.exp(peak - jnp.max(peak, axis=0, keepdims=True))
    total = jnp.sum(factor * mass, axis=0)
    rows = jnp.sum(factor * parts[:, 0:32, :], axis=0) / total
    for i in range(8):
        out[i] = rows


def softmax(scores, axis):
    scores = jnp.exp(scores - jnp.max(scores, axis=axis, keepdims=True))
    return scores / jnp.sum(scores, axis=axis, keepdims=True)


def inverse_body(marks, out):
    qm, km = marks[0], marks[1]
    out[0] = km
    land = softmax(dot(qm, km, ((1,), (1,)), HI) * SCALE, 1)
    across = softmax(dot(km, qm, ((1,), (1,)), HI) * SCALE, 0)
    most = jnp.max(jnp.sum(land, axis=0, keepdims=True), axis=1, keepdims=True) * jnp.max(
        jnp.sum(land, axis=1, keepdims=True), axis=0, keepdims=True
    )
    row = lax.broadcasted_iota(jnp.int32, (64, 64), 0)
    eye = (row == lax.broadcasted_iota(jnp.int32, (64, 64), 1)).astype(F32)
    mul = lambda a, b: dot(a, b, ((1,), (0,)), HI)
    approx = across / most
    for _ in range(PINV_ITERS):
        prod = mul(land, approx)
        inner = 7.0 * eye - prod
        inner = 15.0 * eye - mul(prod, inner)
        inner = 13.0 * eye - mul(prod, inner)
        approx = 0.25 * mul(approx, inner)
    out[1] = jnp.concatenate([approx, jnp.zeros_like(approx)], axis=-1)


def near_body(queries, heads, out):
    for h in range(4):
        query = queries[:, h * HEAD : h * HEAD + HEAD].astype(F32)
        near = softmax(dot(query, heads[h, 0], ((1,), (1,)), HI) * SCALE, -1)
        out[h] = jnp.concatenate([near, jnp.zeros_like(near)], axis=-1)


def spread(terms, out):
    for y in range(terms.shape[0] // 64):
        for x in range(4):
            out[y * 4 + x] = terms[y * 64 : y * 64 + 64, x * 512 : x * 512 + 512].astype(BF16)


def unmix(blocks, tile, dest, lanes, c):
    for z in range(16):
        for y in range(4):
            low = pl.multiple_of((z * 8 + y * 2 + c) * 16, 16)
            dest[pl.ds(low, 16), lanes] = blocks[z, y, tile * 16 : tile * 16 + 16, :]


def unmix_body(core, mine, other, w1, w2, raw, sems):
    copies = [
        pltpu.make_async_copy(far.at[:, :, 64:208], raw.at[i], sems.at[i])
        for i, far in enumerate((mine, other))
    ]
    for copy in copies:
        copy.start()
    for i, c in enumerate((core[0], 1 - core[0])):
        copies[i].wait()
        for t in range(6):
            unmix(raw.at[i], t, w1, slice(t * 128, t * 128 + 128), c)
        for t in range(3):
            unmix(raw.at[i], 6 + t, w2, slice(t * 128, t * 128 + 128), c)


def attn_body(near, heads, gathered, out):
    for h in range(4):
        rows = jnp.concatenate([gathered[2 * h], gathered[2 * h + 1]], axis=0)
        mixer = dot(heads[h, 1][:, :64], rows, ((1,), (0,)), HI)
        attn = dot(near[h][:, :64], mixer, ((1,), (0,)), HI)
        out[:, h * HEAD : h * HEAD + HEAD] = attn.astype(BF16)


def proj_body(core, mine, other, weights, out, wo):
    for z in range(16):
        for y in range(4):
            low = (z * 4 + y) * 16
            for t in range(4):
                lanes = slice(t * 128, t * 128 + 128)
                wo[low : low + 16, lanes] = weights[z, y, t * 16 : t * 16 + 16, :]
    attn = jnp.concatenate([mine[...], other[...]], axis=0)
    terms = dot(attn, wo[...], ((1,), (1,)))
    for i, c in enumerate((core[0], 1 - core[0])):
        for x in range(4):
            out[c * 4 + x] = terms[i * 64 : i * 64 + 64, x * 256 : x * 256 + 256].astype(BF16)


def ffn_body(whole, gain, far1, far2, out, normed, w1, w2, sems):
    first_copy = pltpu.make_async_copy(far1, w1, sems.at[0])
    second_copy = pltpu.make_async_copy(far2, w2, sems.at[1])
    first_copy.start()
    second_copy.start()
    for y in range(2):
        blocks = [whole[y * 4 + x].astype(F32) for x in range(4)]
        square = sum(jnp.sum(b * b, axis=-1, keepdims=True) for b in blocks)
        factor = lax.rsqrt(square * (1.0 / 2048.0) + EPS)
        for x in range(4):
            lanes = slice(x * 512, x * 512 + 512)
            normed[y * 64 : y * 64 + 64, lanes] = (
                blocks[x] * factor * gain[:, lanes]
            ).astype(BF16)
    first_copy.wait()
    first = dot(normed[...], w1[...], ((1,), (0,)))
    gate, up = first[:, :384], first[:, 384:]
    hidden = (gate / (1.0 + jnp.exp(-gate)) * up).astype(BF16)
    second_copy.wait()
    spread(dot(hidden, w2[...], ((1,), (1,))), out)


def on_device(queries, keys, values, stream, seg_lengths, gain, w_out, w_gate, w_up, w_down):
    z, c = lax.axis_index("z"), lax.axis_index("c")
    y_axes = ("yh", "yl")
    pack = kernel_call(pack_body, shape((4, 400, 128), BF16), 7, grant=None)(
        queries, keys, values, w_gate, w_up, w_down.T, w_out.T
    )
    got = lax.all_to_all(pack, y_axes, 0, 0)
    weights = lax.all_gather(got[:, 192:400], "z", axis=0)
    other = lax.ppermute(got, "c", [(0, 1), (1, 0)])
    lengths = seg_lengths.astype(F32)
    place = jnp.stack([c, z]).astype(jnp.int32)
    mine = kernel_call(marks_body, shape((64, HEAD), F32), 3, core=place)(
        got, other, lengths[None, :]
    )
    mine = jnp.sum(lax.all_gather(mine, "z", axis=0), axis=0)
    marks = lax.all_gather(mine / lengths[:, None], "c", axis=0)
    send = kernel_call(far_body, shape((16, 40, HEAD), F32), 3, core=c[None])(got, other, marks)
    parts = lax.all_to_all(send, "z", 0, 0)
    heads = kernel_call(
        inverse_body,
        shape((2, 64, HEAD), F32),
        1,
        cost=pl.CostEstimate(flops=10**9, bytes_accessed=2 * 10**7, transcendentals=0),
    )(marks)
    heads = lax.all_gather(heads, y_axes, axis=0)
    near = kernel_call(near_body, shape((4, 64, HEAD), F32), 2)(queries, heads)
    parts, near, heads = lax.optimization_barrier((parts, near, heads))
    gathered = kernel_call(merge_body, shape((8, 32, HEAD), F32), 1)(parts)
    gathered = lax.all_to_all(gathered, (*y_axes, "c"), 0, 0)
    attn = kernel_call(attn_body, shape((64, 512), BF16), 3)(near, heads, gathered)
    attn_other = lax.ppermute(attn, "c", [(0, 1), (1, 0)])
    weights, attn_other = lax.optimization_barrier((weights, attn_other))
    block = pl.BlockSpec(memory_space=pltpu.VMEM)
    terms = pl.pallas_call(
        proj_body,
        grid=(1,),
        out_shape=shape((8, 64, 256), BF16),
        in_specs=[
            pl.BlockSpec(memory_space=pltpu.SMEM),
            block,
            block,
            pl.BlockSpec((16, 4, 64, 128), lambda i: (0, 0, 0, 0)),
        ],
        out_specs=block,
        scratch_shapes=[pltpu.VMEM((1024, 512), BF16)],
        compiler_params=pltpu.CompilerParams(vmem_limit_bytes=SMALL),
    )(c[None], attn, attn_other, weights)
    terms, weights = lax.optimization_barrier((terms, weights))
    swapped = lax.ppermute(weights, "c", [(0, 1), (1, 0)])
    parts = lax.all_to_all(terms, ("c", "x"), 0, 0)
    w1, w2 = kernel_call(
        unmix_body,
        [shape((2048, 768), BF16), shape((2048, 384), BF16)],
        0,
        [pltpu.VMEM((2, 16, 4, 144, 128), BF16), pltpu.SemaphoreType.DMA((2,))],
        core=c[None],
        n_far=2,
        grant=LARGE,
    )(weights, swapped)
    halves = jnp.sum(parts.reshape(2, 4, 64, 256).astype(F32), axis=1)
    at = np.arange(256, dtype=np.int32)
    at = (at // 16) * 32 + at % 16 + 16 * np.arange(2, dtype=np.int32)[:, None]
    order = (at[:, :, None] == jnp.arange(512, dtype=jnp.int32)).astype(F32)
    proj = jnp.einsum("ctk,ckf->tf", halves, order, precision=HI, preferred_element_type=F32)
    resid = (stream.astype(F32) + proj).astype(BF16)
    whole = lax.all_to_all(jnp.broadcast_to(resid[None], (8, 64, 512)), ("yl", "x"), 0, 0)
    terms = kernel_call(
        ffn_body,
        shape((8, 64, 512), BF16),
        2,
        [
            pltpu.VMEM((128, 2048), BF16),
            pltpu.VMEM((2048, 768), BF16),
            pltpu.VMEM((2048, 384), BF16),
            pltpu.SemaphoreType.DMA((2,)),
        ],
        n_far=2,
        grant=LARGE,
    )(whole, gain[None, :], w1, w2)
    parts = lax.all_to_all(terms, ("yl", "x"), 0, 0)
    return (resid.astype(F32) + jnp.sum(parts.astype(F32), axis=0)).astype(BF16)


def solution(mesh):
    fine = Mesh(mesh.devices.reshape(16, 2, 2, 2, 4), ("z", "yh", "yl", "c", "x"))
    seq = ("z", "yh", "yl", "c")
    return jax.shard_map(
        on_device,
        mesh=fine,
        in_specs=(
            P(seq, "x"),
            P(seq, "x"),
            P(seq, "x"),
            P(seq, "x"),
            P(),
            P(),
            P("x", seq),
            P(seq, "x"),
            P(seq, "x"),
            P("x", seq),
        ),
        out_specs=P(seq, "x"),
        check_vma=False,
    )
```

```python
import math

import jax
import jax.numpy as jnp
import numpy as np
from jax import lax
from jax.experimental import pallas as pl
from jax.experimental.pallas import tpu as pltpu
from jax.sharding import Mesh
from jax.sharding import PartitionSpec as P

PINV_ITERS = 6
HEAD = 128
EPS = 1e-05
SCALE = 1.0 / math.sqrt(HEAD)
HI = lax.Precision.HIGHEST
F32 = jnp.float32
BF16 = jnp.bfloat16
SMALL = 24 << 20
LARGE = 60 << 20


def dot(a, b, dims, precision=None):
    return lax.dot_general(
        a, b, (dims, ((), ())), precision=precision, preferred_element_type=F32
    )


def kernel_call(body, out_shape, n_in, scratch=(), cost=None, core=None, grant=SMALL, n_far=0):
    whole = pl.BlockSpec(memory_space=pltpu.VMEM)
    many = isinstance(out_shape, (list, tuple))
    call = pl.pallas_call(
        body,
        out_shape=out_shape,
        in_specs=([] if core is None else [pl.BlockSpec(memory_space=pltpu.SMEM)])
        + [whole] * n_in
        + [pl.BlockSpec(memory_space=pltpu.HBM)] * n_far,
        out_specs=[whole] * len(out_shape) if many else whole,
        scratch_shapes=list(scratch),
        cost_estimate=cost,
        compiler_params=pltpu.CompilerParams(vmem_limit_bytes=grant),
    )
    return call if core is None else lambda *args: call(core, *args)


def shape(dims, dtype):
    return jax.ShapeDtypeStruct(dims, dtype)


def pack_body(q, k, v, wg, wu, wd, wo, out):
    for y in range(4):
        tile = slice(y * 128, y * 128 + 128)
        out[y, 0:64] = q[:, tile]
        out[y, 64:128] = k[:, tile]
        out[y, 128:192] = v[:, tile]
        for t in range(4):
            out[y, 192 + t * 16 : 208 + t * 16] = wo[:, t * 128 : t * 128 + 128]
        for t in range(3):
            low = ((y % 2) * 3 + t) * 128
            for i, w in enumerate((wg, wu, wd)):
                at = 256 + (3 * i + t) * 16
                out[y, at : at + 16] = w[:, low : low + 128]


def marks_body(place, mine, other, lengths, out):
    c = place[0]
    row = lax.broadcasted_iota(jnp.int32, (64, 64), 0)
    lane = lax.broadcasted_iota(jnp.int32, (64, 64), 1)
    sizes = jnp.broadcast_to(lengths[...], (64, 64))
    starts = jnp.sum(jnp.where(lane < row, sizes, 0.0), axis=1, keepdims=True)
    ends = jnp.sum(jnp.where(lane <= row, sizes, 0.0), axis=1, keepdims=True)
    starts, ends = (e.astype(jnp.int32) - place[1] * 512 for e in (starts, ends))
    low = pl.multiple_of(c * 64, 64)
    total = None
    for got, at_core in ((mine, c), (other, 1 - c)):
        at = lax.broadcasted_iota(jnp.int32, (64, 256), 1)
        at = at + (at // 64) * 64 + at_core * 64
        member = ((at >= starts) & (at < ends)).astype(BF16)
        part = dot(member, got[:, pl.ds(low, 64), :].reshape(256, HEAD), ((1,), (0,)))
        total = part if total is None else total + part
    out[...] = total


def far_body(core, mine, other, marks, out):
    query = marks[0, pl.ds(core[0] * 32, 32), :]
    far = [
        dot(query, got[:, 64:128].reshape(256, HEAD).astype(F32), ((1,), (1,)), HI) * SCALE
        for got in (mine, other)
    ]
    peak = jnp.maximum(*(jnp.max(f, axis=-1, keepdims=True) for f in far))
    far = [jnp.exp(f - peak) for f in far]
    mass = sum(jnp.sum(f, axis=-1, keepdims=True) for f in far)
    part = sum(
        dot(f, got[:, 128:192].reshape(256, HEAD).astype(F32), ((1,), (0,)), HI)
        for f, got in zip(far, (mine, other))
    )
    row = lax.broadcasted_iota(jnp.int32, (32, HEAD), 0)
    lane = lax.broadcasted_iota(jnp.int32, (32, HEAD), 1)
    stats = jnp.where(lane == row, peak, 0.0) + jnp.where(lane == row + 32, mass, 0.0)
    stats = jnp.broadcast_to(jnp.sum(stats, axis=0, keepdims=True), (8, HEAD))
    for z in range(16):
        out[z, 0:32] = part
        out[z, 32:40] = stats


def merge_body(parts, out):
    row = lax.broadcasted_iota(jnp.int32, (16, 32, HEAD), 1)
    lane = lax.broadcasted_iota(jnp.int32, (16, 32, HEAD), 2)
    stats = jnp.broadcast_to(parts[:, 32:33, :], (16, 32, HEAD))
    peak = jnp.sum(jnp.where(lane == row, stats, 0.0), axis=-1, keepdims=True)
    mass = jnp.sum(jnp.where(lane == row + 32, stats, 0.0), axis=-1, keepdims=True)
    factor = jnp.exp(peak - jnp.max(peak, axis=0, keepdims=True))
    total = jnp.sum(factor * mass, axis=0)
    rows = jnp.sum(factor * parts[:, 0:32, :], axis=0) / total
    for i in range(8):
        out[i] = rows


def softmax(scores, axis):
    scores = jnp.exp(scores - jnp.max(scores, axis=axis, keepdims=True))
    return scores / jnp.sum(scores, axis=axis, keepdims=True)


def inverse_body(marks, out):
    qm, km = marks[0], marks[1]
    out[0] = km
    land = softmax(dot(qm, km, ((1,), (1,)), HI) * SCALE, 1)
    across = softmax(dot(km, qm, ((1,), (1,)), HI) * SCALE, 0)
    most = jnp.max(jnp.sum(land, axis=0, keepdims=True), axis=1, keepdims=True) * jnp.max(
        jnp.sum(land, axis=1, keepdims=True), axis=0, keepdims=True
    )
    row = lax.broadcasted_iota(jnp.int32, (64, 64), 0)
    eye = (row == lax.broadcasted_iota(jnp.int32, (64, 64), 1)).astype(F32)
    mul = lambda a, b: dot(a, b, ((1,), (0,)), HI)
    approx = across / most
    for _ in range(PINV_ITERS):
        prod = mul(land, approx)
        inner = 7.0 * eye - prod
        inner = 15.0 * eye - mul(prod, inner)
        inner = 13.0 * eye - mul(prod, inner)
        approx = 0.25 * mul(approx, inner)
    out[1] = jnp.concatenate([approx, jnp.zeros_like(approx)], axis=-1)


def near_body(mine, other, heads, out):
    for i, queries in enumerate((mine, other)):
        for h in range(4):
            query = queries[:, h * HEAD : h * HEAD + HEAD].astype(F32)
            near = softmax(dot(query, heads[h, 0], ((1,), (1,)), HI) * SCALE, -1)
            out[h, i * 64 : i * 64 + 64] = jnp.concatenate([near, jnp.zeros_like(near)], axis=-1)


def spread(terms, out):
    for y in range(terms.shape[0] // 64):
        for x in range(4):
            out[y * 4 + x] = terms[y * 64 : y * 64 + 64, x * 512 : x * 512 + 512].astype(BF16)


def unmix(blocks, tile, dest, lanes, c):
    for z in range(16):
        for y in range(4):
            low = pl.multiple_of((z * 8 + y * 2 + c) * 16, 16)
            dest[pl.ds(low, 16), lanes] = blocks[z, y, tile * 16 : tile * 16 + 16, :]


def unmix_body(core, mine, other, w1, w2, raw, sems):
    copies = [
        pltpu.make_async_copy(far.at[:, :, 64:208], raw.at[i], sems.at[i])
        for i, far in enumerate((mine, other))
    ]
    for copy in copies:
        copy.start()
    for i, c in enumerate((core[0], 1 - core[0])):
        copies[i].wait()
        for t in range(6):
            unmix(raw.at[i], t, w1, slice(t * 128, t * 128 + 128), c)
        for t in range(3):
            unmix(raw.at[i], 6 + t, w2, slice(t * 128, t * 128 + 128), c)


def attn_body(near, heads, gathered, out):
    for h in range(4):
        rows = jnp.concatenate([gathered[2 * h], gathered[2 * h + 1]], axis=0)
        mixer = dot(heads[h, 1][:, :64], rows, ((1,), (0,)), HI)
        attn = dot(near[h][:, :64], mixer, ((1,), (0,)), HI)
        out[:, h * HEAD : h * HEAD + HEAD] = attn.astype(BF16)


def proj_body(core, attn, weights, out, wo):
    for z in range(16):
        for y in range(4):
            low = (z * 4 + y) * 16
            for t in range(4):
                lanes = slice(t * 128, t * 128 + 128)
                wo[low : low + 16, lanes] = weights[z, y, t * 16 : t * 16 + 16, :]
    terms = dot(attn[...], wo[...], ((1,), (1,)))
    for i, c in enumerate((core[0], 1 - core[0])):
        for x in range(4):
            out[c * 4 + x] = terms[i * 64 : i * 64 + 64, x * 256 : x * 256 + 256].astype(BF16)


def ffn_body(whole, gain, far1, far2, out, normed, w1, w2, sems):
    first_copy = pltpu.make_async_copy(far1, w1, sems.at[0])
    second_copy = pltpu.make_async_copy(far2, w2, sems.at[1])
    first_copy.start()
    second_copy.start()
    for y in range(2):
        blocks = [whole[y * 4 + x].astype(F32) for x in range(4)]
        square = sum(jnp.sum(b * b, axis=-1, keepdims=True) for b in blocks)
        factor = lax.rsqrt(square * (1.0 / 2048.0) + EPS)
        for x in range(4):
            lanes = slice(x * 512, x * 512 + 512)
            normed[y * 64 : y * 64 + 64, lanes] = (
                blocks[x] * factor * gain[:, lanes]
            ).astype(BF16)
    first_copy.wait()
    first = dot(normed[...], w1[...], ((1,), (0,)))
    gate, up = first[:, :384], first[:, 384:]
    hidden = (gate / (1.0 + jnp.exp(-gate)) * up).astype(BF16)
    second_copy.wait()
    spread(dot(hidden, w2[...], ((1,), (1,))), out)


def on_device(queries, keys, values, stream, seg_lengths, gain, w_out, w_gate, w_up, w_down):
    z, c = lax.axis_index("z"), lax.axis_index("c")
    y_axes = ("yh", "yl")
    pack = kernel_call(pack_body, shape((4, 400, 128), BF16), 7, grant=None)(
        queries, keys, values, w_gate, w_up, w_down.T, w_out.T
    )
    got = lax.all_to_all(pack, y_axes, 0, 0)
    weights = lax.all_gather(got[:, 192:400], "z", axis=0)
    other = lax.ppermute(got, "c", [(0, 1), (1, 0)])
    lengths = seg_lengths.astype(F32)
    place = jnp.stack([c, z]).astype(jnp.int32)
    mine = kernel_call(marks_body, shape((64, HEAD), F32), 3, core=place)(
        got, other, lengths[None, :]
    )
    mine = jnp.sum(lax.all_gather(mine, "z", axis=0), axis=0)
    marks = lax.all_gather(mine / lengths[:, None], "c", axis=0)
    send = kernel_call(far_body, shape((16, 40, HEAD), F32), 3, core=c[None])(got, other, marks)
    parts = lax.all_to_all(send, "z", 0, 0)
    heads = kernel_call(
        inverse_body,
        shape((2, 64, HEAD), F32),
        1,
        cost=pl.CostEstimate(flops=10**9, bytes_accessed=2 * 10**7, transcendentals=0),
    )(marks)
    heads = lax.all_gather(heads, y_axes, axis=0)
    queries_other = lax.ppermute(queries, "c", [(0, 1), (1, 0)])
    near = kernel_call(near_body, shape((4, 128, HEAD), F32), 3)(queries, queries_other, heads)
    parts, near, heads = lax.optimization_barrier((parts, near, heads))
    gathered = kernel_call(merge_body, shape((8, 32, HEAD), F32), 1)(parts)
    gathered = lax.all_to_all(gathered, (*y_axes, "c"), 0, 0)
    attn = kernel_call(attn_body, shape((128, 512), BF16), 3)(near, heads, gathered)
    weights, attn = lax.optimization_barrier((weights, attn))
    block = pl.BlockSpec(memory_space=pltpu.VMEM)
    terms = pl.pallas_call(
        proj_body,
        grid=(1,),
        out_shape=shape((8, 64, 256), BF16),
        in_specs=[
            pl.BlockSpec(memory_space=pltpu.SMEM),
            block,
            pl.BlockSpec((16, 4, 64, 128), lambda i: (0, 0, 0, 0)),
        ],
        out_specs=block,
        scratch_shapes=[pltpu.VMEM((1024, 512), BF16)],
        compiler_params=pltpu.CompilerParams(vmem_limit_bytes=SMALL),
    )(c[None], attn, weights)
    terms, weights = lax.optimization_barrier((terms, weights))
    swapped = lax.ppermute(weights, "c", [(0, 1), (1, 0)])
    parts = lax.all_to_all(terms, ("c", "x"), 0, 0)
    w1, w2 = kernel_call(
        unmix_body,
        [shape((2048, 768), BF16), shape((2048, 384), BF16)],
        0,
        [pltpu.VMEM((2, 16, 4, 144, 128), BF16), pltpu.SemaphoreType.DMA((2,))],
        core=c[None],
        n_far=2,
        grant=LARGE,
    )(weights, swapped)
    halves = jnp.sum(parts.reshape(2, 4, 64, 256).astype(F32), axis=1)
    at = np.arange(256, dtype=np.int32)
    at = (at // 16) * 32 + at % 16 + 16 * np.arange(2, dtype=np.int32)[:, None]
    order = (at[:, :, None] == jnp.arange(512, dtype=jnp.int32)).astype(F32)
    proj = jnp.einsum("ctk,ckf->tf", halves, order, precision=HI, preferred_element_type=F32)
    resid = (stream.astype(F32) + proj).astype(BF16)
    whole = lax.all_to_all(jnp.broadcast_to(resid[None], (8, 64, 512)), ("yl", "x"), 0, 0)
    terms = kernel_call(
        ffn_body,
        shape((8, 64, 512), BF16),
        2,
        [
            pltpu.VMEM((128, 2048), BF16),
            pltpu.VMEM((2048, 768), BF16),
            pltpu.VMEM((2048, 384), BF16),
            pltpu.SemaphoreType.DMA((2,)),
        ],
        n_far=2,
        grant=LARGE,
    )(whole, gain[None, :], w1, w2)
    parts = lax.all_to_all(terms, ("yl", "x"), 0, 0)
    return (resid.astype(F32) + jnp.sum(parts.astype(F32), axis=0)).astype(BF16)


def solution(mesh):
    fine = Mesh(mesh.devices.reshape(16, 2, 2, 2, 4), ("z", "yh", "yl", "c", "x"))
    seq = ("z", "yh", "yl", "c")
    return jax.shard_map(
        on_device,
        mesh=fine,
        in_specs=(
            P(seq, "x"),
            P(seq, "x"),
            P(seq, "x"),
            P(seq, "x"),
            P(),
            P(),
            P("x", seq),
            P(seq, "x"),
            P(seq, "x"),
            P("x", seq),
        ),
        out_specs=P(seq, "x"),
        check_vma=False,
    )
```

```python
import math

import jax
import jax.numpy as jnp
import numpy as np
from jax import lax
from jax.experimental import pallas as pl
from jax.experimental.pallas import tpu as pltpu
from jax.sharding import Mesh
from jax.sharding import PartitionSpec as P

PINV_ITERS = 6
HEAD = 128
EPS = 1e-05
SCALE = 1.0 / math.sqrt(HEAD)
HI = lax.Precision.HIGHEST
F32 = jnp.float32
BF16 = jnp.bfloat16
SMALL = 24 << 20
LARGE = 60 << 20


def dot(a, b, dims, precision=None):
    return lax.dot_general(
        a, b, (dims, ((), ())), precision=precision, preferred_element_type=F32
    )


def kernel_call(body, out_shape, n_in, scratch=(), cost=None, core=None, grant=SMALL, n_far=0):
    whole = pl.BlockSpec(memory_space=pltpu.VMEM)
    many = isinstance(out_shape, (list, tuple))
    call = pl.pallas_call(
        body,
        out_shape=out_shape,
        in_specs=([] if core is None else [pl.BlockSpec(memory_space=pltpu.SMEM)])
        + [whole] * n_in
        + [pl.BlockSpec(memory_space=pltpu.HBM)] * n_far,
        out_specs=[whole] * len(out_shape) if many else whole,
        scratch_shapes=list(scratch),
        cost_estimate=cost,
        compiler_params=pltpu.CompilerParams(vmem_limit_bytes=grant),
    )
    return call if core is None else lambda *args: call(core, *args)


def shape(dims, dtype):
    return jax.ShapeDtypeStruct(dims, dtype)


def pack_body(q, k, v, wg, wu, wd, wo, out):
    for y in range(4):
        tile = slice(y * 128, y * 128 + 128)
        out[y, 0:64] = q[:, tile]
        out[y, 64:128] = k[:, tile]
        out[y, 128:192] = v[:, tile]
        for t in range(4):
            out[y, 192 + t * 16 : 208 + t * 16] = wo[:, t * 128 : t * 128 + 128]
        for t in range(3):
            low = ((y % 2) * 3 + t) * 128
            for i, w in enumerate((wg, wu, wd)):
                at = 256 + (3 * i + t) * 16
                out[y, at : at + 16] = w[:, low : low + 128]


def marks_body(place, mine, other, lengths, out):
    c = place[0]
    row = lax.broadcasted_iota(jnp.int32, (64, 64), 0)
    lane = lax.broadcasted_iota(jnp.int32, (64, 64), 1)
    sizes = jnp.broadcast_to(lengths[...], (64, 64))
    starts = jnp.sum(jnp.where(lane < row, sizes, 0.0), axis=1, keepdims=True)
    ends = jnp.sum(jnp.where(lane <= row, sizes, 0.0), axis=1, keepdims=True)
    starts, ends = (e.astype(jnp.int32) - place[1] * 512 for e in (starts, ends))
    low = pl.multiple_of(c * 64, 64)
    total = None
    for got, at_core in ((mine, c), (other, 1 - c)):
        at = lax.broadcasted_iota(jnp.int32, (64, 256), 1)
        at = at + (at // 64) * 64 + at_core * 64
        member = ((at >= starts) & (at < ends)).astype(BF16)
        part = dot(member, got[:, pl.ds(low, 64), :].reshape(256, HEAD), ((1,), (0,)))
        total = part if total is None else total + part
    out[...] = total


def far_body(core, mine, other, marks, out):
    query = marks[0, pl.ds(core[0] * 32, 32), :]
    far = [
        dot(query, got[:, 64:128].reshape(256, HEAD).astype(F32), ((1,), (1,)), HI) * SCALE
        for got in (mine, other)
    ]
    peak = jnp.maximum(*(jnp.max(f, axis=-1, keepdims=True) for f in far))
    far = [jnp.exp(f - peak) for f in far]
    mass = sum(jnp.sum(f, axis=-1, keepdims=True) for f in far)
    part = sum(
        dot(f, got[:, 128:192].reshape(256, HEAD).astype(F32), ((1,), (0,)), HI)
        for f, got in zip(far, (mine, other))
    )
    row = lax.broadcasted_iota(jnp.int32, (32, HEAD), 0)
    lane = lax.broadcasted_iota(jnp.int32, (32, HEAD), 1)
    stats = jnp.where(lane == row, peak, 0.0) + jnp.where(lane == row + 32, mass, 0.0)
    stats = jnp.broadcast_to(jnp.sum(stats, axis=0, keepdims=True), (8, HEAD))
    for z in range(16):
        out[z, 0:32] = part
        out[z, 32:40] = stats


def merge_body(parts, out):
    row = lax.broadcasted_iota(jnp.int32, (16, 32, HEAD), 1)
    lane = lax.broadcasted_iota(jnp.int32, (16, 32, HEAD), 2)
    stats = jnp.broadcast_to(parts[:, 32:33, :], (16, 32, HEAD))
    peak = jnp.sum(jnp.where(lane == row, stats, 0.0), axis=-1, keepdims=True)
    mass = jnp.sum(jnp.where(lane == row + 32, stats, 0.0), axis=-1, keepdims=True)
    factor = jnp.exp(peak - jnp.max(peak, axis=0, keepdims=True))
    total = jnp.sum(factor * mass, axis=0)
    rows = jnp.sum(factor * parts[:, 0:32, :], axis=0) / total
    for i in range(8):
        out[i] = rows


def softmax(scores, axis):
    scores = jnp.exp(scores - jnp.max(scores, axis=axis, keepdims=True))
    return scores / jnp.sum(scores, axis=axis, keepdims=True)


def inverse_body(marks, out):
    qm, km = marks[0], marks[1]
    out[0] = km
    land = softmax(dot(qm, km, ((1,), (1,)), HI) * SCALE, 1)
    across = softmax(dot(km, qm, ((1,), (1,)), HI) * SCALE, 0)
    most = jnp.max(jnp.sum(land, axis=0, keepdims=True), axis=1, keepdims=True) * jnp.max(
        jnp.sum(land, axis=1, keepdims=True), axis=0, keepdims=True
    )
    row = lax.broadcasted_iota(jnp.int32, (64, 64), 0)
    eye = (row == lax.broadcasted_iota(jnp.int32, (64, 64), 1)).astype(F32)
    mul = lambda a, b: dot(a, b, ((1,), (0,)), HI)
    approx = across / most
    for _ in range(PINV_ITERS):
        prod = mul(land, approx)
        inner = 7.0 * eye - prod
        inner = 15.0 * eye - mul(prod, inner)
        inner = 13.0 * eye - mul(prod, inner)
        approx = 0.25 * mul(approx, inner)
    out[1] = jnp.concatenate([approx, jnp.zeros_like(approx)], axis=-1)


def near_body(mine, other, heads, out):
    for i, queries in enumerate((mine, other)):
        for h in range(4):
            query = queries[:, h * HEAD : h * HEAD + HEAD].astype(F32)
            near = softmax(dot(query, heads[h, 0], ((1,), (1,)), HI) * SCALE, -1)
            out[h, i * 64 : i * 64 + 64] = jnp.concatenate([near, jnp.zeros_like(near)], axis=-1)


def spread(terms, out):
    for y in range(terms.shape[0] // 64):
        for x in range(4):
            out[y * 4 + x] = terms[y * 64 : y * 64 + 64, x * 512 : x * 512 + 512].astype(BF16)


def unmix(blocks, tile, dest, lanes, c):
    for z in range(16):
        for y in range(4):
            low = (z * 8 + y * 2 + c) * 16
            dest[low : low + 16, lanes] = blocks[z, y, tile * 16 : tile * 16 + 16, :]


def unmix_body(cores, w1, w2, raw, sems):
    copies = [
        pltpu.make_async_copy(cores.at[c, :, :, 64:208], raw.at[c], sems.at[c]) for c in range(2)
    ]
    for copy in copies:
        copy.start()
    for c in range(2):
        copies[c].wait()
        for t in range(6):
            unmix(raw.at[c], t, w1, slice(t * 128, t * 128 + 128), c)
        for t in range(3):
            unmix(raw.at[c], 6 + t, w2, slice(t * 128, t * 128 + 128), c)


def attn_body(near, heads, gathered, out):
    for h in range(4):
        rows = jnp.concatenate([gathered[2 * h], gathered[2 * h + 1]], axis=0)
        mixer = dot(heads[h, 1][:, :64], rows, ((1,), (0,)), HI)
        attn = dot(near[h][:, :64], mixer, ((1,), (0,)), HI)
        out[:, h * HEAD : h * HEAD + HEAD] = attn.astype(BF16)


def proj_body(core, attn, weights, out, wo):
    for z in range(16):
        for y in range(4):
            low = (z * 4 + y) * 16
            for t in range(4):
                lanes = slice(t * 128, t * 128 + 128)
                wo[low : low + 16, lanes] = weights[z, y, t * 16 : t * 16 + 16, :]
    terms = dot(attn[...], wo[...], ((1,), (1,)))
    for i, c in enumerate((core[0], 1 - core[0])):
        for x in range(4):
            out[c * 4 + x] = terms[i * 64 : i * 64 + 64, x * 256 : x * 256 + 256].astype(BF16)


def ffn_body(whole, gain, far1, far2, out, normed, w1, w2, sems):
    first_copy = pltpu.make_async_copy(far1, w1, sems.at[0])
    second_copy = pltpu.make_async_copy(far2, w2, sems.at[1])
    first_copy.start()
    second_copy.start()
    for y in range(2):
        blocks = [whole[y * 4 + x].astype(F32) for x in range(4)]
        square = sum(jnp.sum(b * b, axis=-1, keepdims=True) for b in blocks)
        factor = lax.rsqrt(square * (1.0 / 2048.0) + EPS)
        for x in range(4):
            lanes = slice(x * 512, x * 512 + 512)
            normed[y * 64 : y * 64 + 64, lanes] = (
                blocks[x] * factor * gain[:, lanes]
            ).astype(BF16)
    first_copy.wait()
    first = dot(normed[...], w1[...], ((1,), (0,)))
    gate, up = first[:, :384], first[:, 384:]
    hidden = (gate / (1.0 + jnp.exp(-gate)) * up).astype(BF16)
    second_copy.wait()
    spread(dot(hidden, w2[...], ((1,), (1,))), out)


def on_device(queries, keys, values, stream, seg_lengths, gain, w_out, w_gate, w_up, w_down):
    z, c = lax.axis_index("z"), lax.axis_index("c")
    y_axes = ("yh", "yl")
    pack = kernel_call(pack_body, shape((4, 400, 128), BF16), 7, grant=None)(
        queries, keys, values, w_gate, w_up, w_down.T, w_out.T
    )
    got = lax.all_to_all(pack, y_axes, 0, 0)
    weights = lax.all_gather(got[:, 192:400], "z", axis=0)
    other = lax.ppermute(got, "c", [(0, 1), (1, 0)])
    lengths = seg_lengths.astype(F32)
    place = jnp.stack([c, z]).astype(jnp.int32)
    mine = kernel_call(marks_body, shape((64, HEAD), F32), 3, core=place)(
        got, other, lengths[None, :]
    )
    mine = jnp.sum(lax.all_gather(mine, "z", axis=0), axis=0)
    marks = lax.all_gather(mine / lengths[:, None], "c", axis=0)
    send = kernel_call(far_body, shape((16, 40, HEAD), F32), 3, core=c[None])(got, other, marks)
    parts = lax.all_to_all(send, "z", 0, 0)
    heads = kernel_call(
        inverse_body,
        shape((2, 64, HEAD), F32),
        1,
        cost=pl.CostEstimate(flops=10**9, bytes_accessed=2 * 10**7, transcendentals=0),
    )(marks)
    heads = lax.all_gather(heads, y_axes, axis=0)
    queries_other = lax.ppermute(queries, "c", [(0, 1), (1, 0)])
    near = kernel_call(near_body, shape((4, 128, HEAD), F32), 3)(queries, queries_other, heads)
    parts, near, heads = lax.optimization_barrier((parts, near, heads))
    gathered = kernel_call(merge_body, shape((8, 32, HEAD), F32), 1)(parts)
    gathered = lax.all_to_all(gathered, (*y_axes, "c"), 0, 0)
    attn = kernel_call(attn_body, shape((128, 512), BF16), 3)(near, heads, gathered)
    weights, attn = lax.optimization_barrier((weights, attn))
    block = pl.BlockSpec(memory_space=pltpu.VMEM)
    terms = pl.pallas_call(
        proj_body,
        grid=(1,),
        out_shape=shape((8, 64, 256), BF16),
        in_specs=[
            pl.BlockSpec(memory_space=pltpu.SMEM),
            block,
            pl.BlockSpec((16, 4, 64, 128), lambda i: (0, 0, 0, 0)),
        ],
        out_specs=block,
        scratch_shapes=[pltpu.VMEM((1024, 512), BF16)],
        compiler_params=pltpu.CompilerParams(vmem_limit_bytes=LARGE),
    )(c[None], attn, weights)
    cores = lax.all_gather(weights, "c", axis=0)
    parts = lax.all_to_all(terms, ("c", "x"), 0, 0)
    w1, w2 = kernel_call(
        unmix_body,
        [shape((2048, 768), BF16), shape((2048, 384), BF16)],
        0,
        [pltpu.VMEM((2, 16, 4, 144, 128), BF16), pltpu.SemaphoreType.DMA((2,))],
        n_far=1,
        grant=LARGE,
    )(cores)
    halves = jnp.sum(parts.reshape(2, 4, 64, 256).astype(F32), axis=1)
    at = np.arange(256, dtype=np.int32)
    at = (at // 16) * 32 + at % 16 + 16 * np.arange(2, dtype=np.int32)[:, None]
    order = (at[:, :, None] == jnp.arange(512, dtype=jnp.int32)).astype(F32)
    proj = jnp.einsum("ctk,ckf->tf", halves, order, precision=HI, preferred_element_type=F32)
    resid = (stream.astype(F32) + proj).astype(BF16)
    whole = lax.all_to_all(jnp.broadcast_to(resid[None], (8, 64, 512)), ("yl", "x"), 0, 0)
    terms = kernel_call(
        ffn_body,
        shape((8, 64, 512), BF16),
        2,
        [
            pltpu.VMEM((128, 2048), BF16),
            pltpu.VMEM((2048, 768), BF16),
            pltpu.VMEM((2048, 384), BF16),
            pltpu.SemaphoreType.DMA((2,)),
        ],
        n_far=2,
        grant=LARGE,
    )(whole, gain[None, :], w1, w2)
    parts = lax.all_to_all(terms, ("yl", "x"), 0, 0)
    return (resid.astype(F32) + jnp.sum(parts.astype(F32), axis=0)).astype(BF16)


def solution(mesh):
    fine = Mesh(mesh.devices.reshape(16, 2, 2, 2, 4), ("z", "yh", "yl", "c", "x"))
    seq = ("z", "yh", "yl", "c")
    return jax.shard_map(
        on_device,
        mesh=fine,
        in_specs=(
            P(seq, "x"),
            P(seq, "x"),
            P(seq, "x"),
            P(seq, "x"),
            P(),
            P(),
            P("x", seq),
            P(seq, "x"),
            P(seq, "x"),
            P("x", seq),
        ),
        out_specs=P(seq, "x"),
        check_vma=False,
    )
```
